512 devices in a mesh: layer: 8 (over z_hi, y), pos: 64 (over x, z_lo, core).
Axes of the slice: x: 4, y: 4, z: 16 (z_hi: 2, z_lo: 8; z = z_hi * 8 + z_lo), core: 2. Of those that a mesh axis runs over, the one named last changes fastest.
Arguments:
- layer_inputs: bfloat16 [8, 128, 16, 16, 128], P('layer', 'pos'), may hold values from -6 to 6
- output_grads: bfloat16 [8, 128, 16, 16, 128], P('layer', 'pos'), may hold values from -2 to 2
- input_inverse: float32 [8, 1152, 1152], P('layer', 'pos'), may hold values from -0.06 to 2.1
- grad_inverse: float32 [8, 128, 128], P('layer'), may hold values from -4 to 54
Outputs:
- update: float32 [8, 1152, 128], P('layer', 'pos')
- grad_grams: float32 [8, 2, 128, 128], P('layer')
The draws below stay inside these ranges and needn't reach their ends.
All inputs are finite; a program needn't handle non-finite values.
Results may differ from the reference program's by a relative error of at most 0.0023.
Values may be sent and summed in bfloat16 or wider, within the bound.
A program may use at most 64 MiB of HBM per device.

```python
import jax
import jax.numpy as jnp
from jax import lax

CH = 128
KK = 9
SIDE = 16
LAYERS = 8
IMAGES = 128
POSITIONS = 32768


def fresh_noise(key, shape):
    return jnp.clip(jax.random.normal(key, shape, jnp.float32), -4.0, 4.0)


def layer_chain(prev, fresh):
    nxt = 0.6 * prev + 0.8 * fresh
    return (nxt, nxt)


def joint_fields(key):
    base = jax.random.fold_in(key, 7)
    key_input, key_grad = jax.random.split(base)
    shape = (LAYERS, IMAGES, SIDE, SIDE, CH)
    noise_input = fresh_noise(key_input, shape)
    _, rest_input = lax.scan(layer_chain, noise_input[0], noise_input[1:])
    inputs = jnp.concatenate([noise_input[:1], rest_input], axis=0)
    noise_grad = fresh_noise(key_grad, shape)
    _, rest_grad = lax.scan(layer_chain, noise_grad[0], noise_grad[1:])
    hidden_part = jnp.concatenate([noise_grad[:1], rest_grad], axis=0)
    image_scale = 1.0 + 2.0 * jnp.arange(IMAGES, dtype=jnp.float32) / max(IMAGES - 1, 1)
    image_scale = image_scale.reshape(1, IMAGES, 1, 1, 1)
    grads = 0.1 * image_scale * (0.8 * hidden_part + 0.6 * inputs)
    return (jnp.clip(inputs, -6.0, 6.0), jnp.clip(grads, -2.0, 2.0))


def stale_inverse(key, order, level):
    key_diag, key_off = jax.random.split(key)
    diagonal = level * jnp.exp(jax.random.uniform(key_diag, (LAYERS, order), jnp.float32, -0.6931472, 0.6931472))
    off_part = fresh_noise(key_off, (LAYERS, order, order)) * (level * 0.3 / order ** 0.5)
    return off_part + diagonal[:, :, None] * jnp.eye(order, dtype=jnp.float32)[None]


def draw_layer_inputs(key, part):
    return joint_fields(key)[0].astype(jnp.bfloat16)


def draw_output_grads(key, part):
    return joint_fields(key)[1].astype(jnp.bfloat16)


def draw_input_inverse(key, part):
    return stale_inverse(jax.random.fold_in(key, 21), KK * CH, 1.0)


def draw_grad_inverse(key, part):
    return stale_inverse(jax.random.fold_in(key, 22), CH, 25.0)


def setup_inputs(seed: int = 0) -> dict:
    keys = jax.random.split(jax.random.key(seed), 5)
    return {
        "layer_inputs": draw_layer_inputs(jax.random.fold_in(keys[4], 71), 0),
        "output_grads": draw_output_grads(jax.random.fold_in(keys[4], 71), 0),
        "input_inverse": draw_input_inverse(jax.random.fold_in(keys[4], 71), 0),
        "grad_inverse": draw_grad_inverse(jax.random.fold_in(keys[4], 71), 0),
    }


def pad_maps(layer_maps):
    return jnp.pad(layer_maps, ((0, 0), (1, 1), (1, 1), (0, 0)))


def unfold_piece(padded, kernel_tap):
    offset_row = kernel_tap // 3
    offset_col = kernel_tap % 3
    return padded[:, offset_row:offset_row + SIDE, offset_col:offset_col + SIDE, :].reshape(-1, CH)


def reference(layer_inputs, output_grads, input_inverse, grad_inverse):
    scale_all = 1.0 / POSITIONS
    next_inputs = jnp.concatenate([layer_inputs[1:], jnp.zeros_like(layer_inputs[:1])], axis=0)
    next_grads = jnp.concatenate([output_grads[1:], jnp.zeros_like(output_grads[:1])], axis=0)

    def first_pass(inputs):
        layer_maps, grad_maps, grad_after = inputs
        padded = pad_maps(layer_maps)
        grad_rows = grad_maps.reshape(-1, CH)
        blocks = [jnp.dot(unfold_piece(padded, kernel_tap).T, grad_rows, preferred_element_type=jnp.float32) for kernel_tap in range(KK)]
        grad_w = jnp.concatenate(blocks, axis=0) * scale_all
        g_own = jnp.dot(grad_rows.T, grad_rows, preferred_element_type=jnp.float32) * scale_all
        g_cross = jnp.dot(grad_rows.T, grad_after.reshape(-1, CH), preferred_element_type=jnp.float32) * scale_all
        return grad_w, g_own, g_cross

    grad_w, g_own, g_cross = lax.map(first_pass, (layer_inputs, output_grads, next_grads))
    high = lax.Precision.HIGHEST
    precond = jnp.einsum("lij,ljk->lik", input_inverse, grad_w, precision=high)
    precond = jnp.einsum("lik,lkm->lim", precond, grad_inverse, precision=high).astype(jnp.bfloat16)
    precond_next = jnp.concatenate([precond[1:], jnp.zeros_like(precond[:1])], axis=0)

    def second_pass(inputs):
        layer_maps, maps_after, precond_after = inputs
        padded = pad_maps(layer_maps)
        padded_after = pad_maps(maps_after)
        mapped = jnp.zeros((layer_maps.shape[0] * SIDE * SIDE, CH), jnp.float32)
        for kernel_tap in range(KK):
            mapped = mapped + jnp.dot(unfold_piece(padded_after, kernel_tap), precond_after[kernel_tap * CH:(kernel_tap + 1) * CH], preferred_element_type=jnp.float32)
        mapped = mapped.astype(jnp.bfloat16)
        blocks = [jnp.dot(unfold_piece(padded, kernel_tap).T, mapped, preferred_element_type=jnp.float32) for kernel_tap in range(KK)]
        return jnp.concatenate(blocks, axis=0) * scale_all

    cross_term = lax.map(second_pass, (layer_inputs, next_inputs, precond_next))
    corrected = grad_w - jnp.einsum("lij,lkj->lik", cross_term, g_cross, precision=high)
    update = jnp.einsum("lij,ljk->lik", input_inverse, corrected, precision=high)
    update = jnp.einsum("lik,lkm->lim", update, grad_inverse, precision=high)
    grad_grams = jnp.stack([g_own, g_cross], axis=1)
    return update, grad_grams
```

```python
import functools

import jax
import jax.numpy as jnp
from jax import lax
from jax.experimental import pallas as pl
from jax.experimental.pallas import tpu as pltpu
from jax.sharding import PartitionSpec as P

NX, NZ, NC = 4, 8, 2
ROOT = 3
TAPS = 9
MESH = pl.DeviceIdType.MESH
F32 = jnp.float32
BF16 = jnp.bfloat16
HIGH = lax.Precision.HIGHEST


def peers():
    order = sorted(range(NX), key=lambda d: -min(d, NX - d))
    return [(dx, dc) for dx in order for dc in range(NC) if dx or dc]


def rcopy(src, dst, send_sem, recv_sem, to):
    return pltpu.make_async_remote_copy(
        src_ref=src,
        dst_ref=dst,
        send_sem=send_sem,
        recv_sem=recv_sem,
        device_id=to,
        device_id_type=MESH,
    )


def dot(a, b, contract=(1, 0), precision=None):
    return lax.dot_general(
        a,
        b,
        (((contract[0],), (contract[1],)), ((), ())),
        precision=precision,
        preferred_element_type=F32,
    )


def unfold(src, dst, images, side, width):
    area = side * side
    rows = images * area
    value = src[...].astype(F32)
    col = lax.rem(lax.broadcasted_iota(jnp.int32, (rows, width), 0), side)
    before = jnp.where(col == 0, 0.0, pltpu.roll(value, 1, 0))
    after = jnp.where(col == side - 1, 0.0, pltpu.roll(value, rows - 1, 0))
    edge = jnp.zeros((side, width), BF16)
    for s, piece in enumerate((before, value, after)):
        piece = piece.astype(BF16)
        for image in range(images):
            top = image * area
            one = piece[top : top + area]
            lanes = pl.ds(s * width, width)
            dst[pl.ds(top, side), lanes] = edge
            dst[pl.ds(top + side, area - side), lanes] = one[: area - side]
            lanes = pl.ds((3 + s) * width, width)
            dst[pl.ds(top, area), lanes] = one
            lanes = pl.ds((6 + s) * width, width)
            dst[pl.ds(top, area - side), lanes] = one[side:]
            dst[pl.ds(top + area - side, side), lanes] = edge


def kernel(
    layers,
    images,
    side,
    scale,
    x_ref,
    g_ref,
    a_ref,
    ginv_ref,
    upd_ref,
    gram_ref,
    patches,
    patches_next,
    grad_t,
    x_next,
    g_next,
    part,
    part_one,
    in_one,
    out_two,
    in_two,
    plane_sum,
    z_out,
    z_in,
    z_out_wide,
    z_in_wide,
    full,
    full_wide,
    a_in,
    a_all,
    a_two,
    pre,
    rows_full,
    base,
    result,
    result_out,
    result_in,
    gram_part,
    gram_in,
    gram_z_out,
    gram_z_in,
    gram_full,
    ex_send,
    ex_recv,
    z_send,
    z_recv,
    a_send,
    a_recv,
    shift_send,
    shift_recv,
    pre_send,
    pre_recv,
    bc_send,
    bc_recv,
    up_send,
    up_recv,
):
    layer = lax.axis_index("layer")
    pos = lax.axis_index("pos")
    c = lax.rem(pos, NC)
    z = lax.rem(lax.div(pos, NC), NZ)
    x = lax.div(pos, NC * NZ)
    me = x * NC + c
    n = NX * NC
    width = g_ref.shape[1]
    lanes = TAPS * width
    per = NZ // NC
    own_rows = a_ref.shape[0]
    is_root = z == ROOT
    is_rim = z != ROOT
    has_next = layer < layers - 1
    has_prev = layer > 0

    def dev(lay, px, pz, pc):
        return (lay, (px * NZ + pz) * NC + pc)

    def peer(dx, dc):
        return lax.rem(x + dx, NX), lax.rem(c + dc, NC)

    def origin(dx, dc):
        return lax.rem(x + NX - dx, NX) * NC + lax.rem(c + NC - dc, NC)

    barrier = pltpu.get_barrier_semaphore()

    def greet(to):
        pl.semaphore_signal(barrier, inc=1, device_id=to, device_id_type=MESH)

    for dx, dc in peers():
        px, pc = peer(dx, dc)
        greet(dev(layer, px, z, pc))

    @pl.when(is_rim)
    def _():
        for pc in range(NC):
            greet(dev(layer, x, ROOT, pc))

    @pl.when(is_root)
    def _():
        for pz in range(NZ):
            if pz != ROOT:
                for pc in range(NC):
                    greet(dev(layer, x, pz, pc))

    @pl.when(has_prev)
    def _():
        greet(dev(layer - 1, x, z, c))

    @pl.when(has_next)
    def _():
        greet(dev(layer + 1, x, z, c))

    @pl.when(has_prev & is_root)
    def _():
        for pz in range(NZ):
            if pz != ROOT:
                greet(dev(layer - 1, x, pz, c))

    @pl.when(has_next & is_rim)
    def _():
        greet(dev(layer + 1, x, ROOT, c))

    unfold(x_ref, patches, images, side, width)
    grad_t[...] = g_ref[...].T

    root = is_root.astype(jnp.int32)
    nxt = has_next.astype(jnp.int32)
    prv = has_prev.astype(jnp.int32)
    expected = n - 1 + prv + nxt
    expected = expected + root * ((NZ - 1) * NC + prv * (NZ - 1))
    expected = expected + (1 - root) * (NC + nxt)
    pl.semaphore_wait(barrier, expected)

    map_shift = rcopy(x_ref, x_next, shift_send.at[0], shift_recv.at[0], dev(layer - 1, x, z, c))
    grad_shift = rcopy(g_ref, g_next, shift_send.at[1], shift_recv.at[1], dev(layer - 1, x, z, c))

    @pl.when(has_prev)
    def _():
        map_shift.start()

    half = lax.div(z, per)
    slot = lax.rem(z, per) * NC + c
    a_self = is_root & (half == c)
    a_other = jnp.logical_not(a_self)
    a_remote = rcopy(a_ref, a_in.at[slot], a_send.at[0], a_recv.at[slot], dev(layer, x, ROOT, half))
    a_local = pltpu.make_async_copy(a_ref, a_in.at[slot], a_recv.at[slot])

    @pl.when(a_other)
    def _():
        a_remote.start()

    @pl.when(a_self)
    def _():
        a_local.start()

    def scatter(kind, src, dst):
        copies = []
        for dx, dc in peers():
            px, pc = peer(dx, dc)
            s = dx * NC + dc
            copy = rcopy(
                src.at[px * NC + pc],
                dst.at[s],
                ex_send.at[kind, s],
                ex_recv.at[kind, s],
                dev(layer, px, z, pc),
            )
            copy.start()
            copies.append(copy)
        return copies

    def gather(kind, buf):
        copies = []
        for dx, dc in peers():
            px, pc = peer(dx, dc)
            s = dx * NC + dc
            copy = rcopy(
                buf.at[me],
                buf.at[me],
                ex_send.at[kind, s],
                ex_recv.at[kind, s],
                dev(layer, px, z, pc),
            )
            copy.start()
            copies.append(copy)
        return copies

    def gathered(kind, buf):
        for dx, dc in reversed(peers()):
            s = dx * NC + dc
            block = buf.at[origin(dx, dc)]
            rcopy(
                block, block, ex_send.at[kind, s], ex_recv.at[kind, s], dev(layer, x, z, c)
            ).wait_recv()

    def sent(copies):
        for copy in copies:
            copy.wait_send()

    def z_copy(kind, src, dst):
        return rcopy(
            src, dst.at[z], z_send.at[kind], z_recv.at[kind, z], dev(layer, x, ROOT, c)
        )

    def z_arrived(kind, src, dst, pz):
        rcopy(
            src, dst.at[pz], z_send.at[kind], z_recv.at[kind, pz], dev(layer, x, ROOT, c)
        ).wait_recv()

    z_bufs = ((z_out_wide, z_in_wide), (z_out, z_in))

    def reduce_plane(kind, product, part, out, inn):
        part[...] = product.reshape(part.shape)
        if out is not part:
            out[...] = product.astype(BF16).reshape(out.shape)
        return scatter(kind, out, inn)

    def finish_plane(copies, part, inn, z_slot):
        total = part[me]
        for copy, (dx, dc) in reversed(list(zip(copies, peers()))):
            copy.wait_recv()
            total = total + inn[dx * NC + dc].astype(F32)
        plane_sum[...] = total

        src, dst = z_bufs[z_slot]

        @pl.when(is_rim)
        def _():
            src[...] = total.astype(src.dtype)
            z_copy(z_slot, src, dst).start()

    def root_total(z_slot, buf):
        total = plane_sum[...]
        src, dst = z_bufs[z_slot]
        for pz in range(NZ):
            if pz != ROOT:
                z_arrived(z_slot, src, dst, pz)
                total = total + dst[pz].astype(F32)
        buf[me] = (total * scale).astype(buf.dtype)

    def fold(both):
        half_rows = both.shape[0] // 2
        return both[:half_rows] + both[half_rows:]

    def times_inverse(buf):
        value = buf[...].reshape(width, lanes)
        top = value.astype(BF16)
        low = (value - top.astype(F32)).astype(BF16)
        both = dot(a_two[...], jnp.concatenate([top, low], axis=0), (1, 1))
        return fold(both[:, :width] + both[:, width:])

    first = reduce_plane(0, dot(grad_t[...], patches[...]), part_one, part_one, in_one)
    finish_plane(first, part_one, in_one, 0)

    @pl.when(has_prev)
    def _():
        grad_shift.start()

    pre_copies = [
        rcopy(
            rows_full,
            pre.at[me],
            pre_send.at[pz],
            pre_recv.at[0],
            dev(layer - 1, x, pz, c),
        )
        for pz in range(NZ)
    ]

    @pl.when(is_root)
    def _():
        for q in range(NZ):
            pltpu.make_async_copy(a_ref, a_in.at[q], a_recv.at[q]).wait()
            a_all[pl.ds(q * own_rows, own_rows), :] = a_in[q]
        rows = a_all[...]
        top = rows.astype(BF16)
        a_two[pl.ds(0, rows.shape[0]), :] = top
        a_two[pl.ds(rows.shape[0], rows.shape[0]), :] = (rows - top.astype(F32)).astype(BF16)
        root_total(0, full_wide)
        copies = gather(1, full_wide)
        gathered(1, full_wide)
        value = dot(times_inverse(full_wide), ginv_ref[...], precision=HIGH)
        base[...] = value
        rows_full[...] = value.astype(BF16)

        @pl.when(has_prev)
        def _():
            for copy in pre_copies:
                copy.start()

        sent(copies)

    @pl.when(has_next)
    def _():
        map_shift.wait_recv()

    @pl.when(jnp.logical_not(has_next))
    def _():
        x_next[...] = jnp.zeros_like(x_next)
        g_next[...] = jnp.zeros_like(g_next)
        pre[...] = jnp.zeros_like(pre)

    unfold(x_next, patches_next, images, side, width)

    @pl.when(has_next)
    def _():
        grad_shift.wait_recv()

    blocks = gram_part.shape[0] // 2
    gram_part[pl.ds(0, blocks)] = dot(grad_t[...], g_ref[...]).reshape(
        blocks, gram_part.shape[1], width
    )
    gram_part[pl.ds(blocks, blocks)] = dot(grad_t[...], g_next[...]).reshape(
        blocks, gram_part.shape[1], width
    )
    gram_copies = scatter(2, gram_part, gram_in)

    @pl.when(has_next)
    def _():
        rcopy(
            rows_full, pre.at[me], pre_send.at[0], pre_recv.at[0], dev(layer, x, z, c)
        ).wait_recv()
        copies = gather(3, pre)
        gathered(3, pre)
        sent(copies)

    mapped = dot(patches_next[...], pre[...].reshape(lanes, width)).astype(BF16)
    second = reduce_plane(4, dot(mapped.T, patches[...]), part, out_two, in_two)

    gram = gram_part[me]
    for copy, (dx, dc) in reversed(list(zip(gram_copies, peers()))):
        copy.wait_recv()
        gram = gram + gram_in[dx * NC + dc]
    gram_z_out[...] = gram

    @pl.when(is_rim)
    def _():
        z_copy(2, gram_z_out, gram_z_in).start()

    finish_plane(second, part, in_two, 1)

    bc_copies = [
        rcopy(
            gram_full.at[me],
            gram_full.at[me],
            bc_send.at[pz],
            bc_recv.at[0],
            dev(layer, x, pz, c),
        )
        for pz in range(NZ)
    ]

    @pl.when(is_root)
    def _():
        total = gram_z_out[...]
        for pz in range(NZ):
            if pz != ROOT:
                z_arrived(2, gram_z_out, gram_z_in, pz)
                total = total + gram_z_in[pz]
        gram_full[me] = total * scale
        for pz in range(NZ):
            if pz != ROOT:
                bc_copies[pz].start()

    @pl.when(is_rim)
    def _():
        bc_copies[ROOT].wait_recv()

    gram_gather = gather(5, gram_full)

    @pl.when(is_root)
    def _():
        root_total(1, full)
        copies = gather(6, full)
        gathered(5, gram_full)
        cross_gram = gram_full[pl.ds(blocks, blocks)].reshape(width, width)
        mix = dot(cross_gram, ginv_ref[...], (0, 0), HIGH)
        gathered(6, full)
        value = base[...] - dot(times_inverse(full), mix, precision=HIGH)
        result[...] = value
        for q in range(NZ):
            result_out[q] = result[pl.ds(q * own_rows, own_rows), :]
            copy = rcopy(
                result_out.at[q],
                result_in,
                up_send.at[q],
                up_recv.at[0],
                dev(layer, x, c * per + q // NC, q % NC),
            )
            if q // NC == ROOT % per and q % NC == ROOT // per:

                @pl.when(c == ROOT // per)
                def _(q=q):
                    upd_ref[...] = result_out[q]

                @pl.when(c != ROOT // per)
                def _(copy=copy):
                    copy.start()
                    copy.wait_send()
            else:
                copy.start()
        for q in range(NZ):
            if not (q // NC == ROOT % per and q % NC == ROOT // per):
                rcopy(
                    result_out.at[q],
                    result_in,
                    up_send.at[q],
                    up_recv.at[0],
                    dev(layer, x, c * per + q // NC, q % NC),
                ).wait_send()
        sent(copies)

    @pl.when(is_rim)
    def _():
        gathered(5, gram_full)

    gram_ref[...] = gram_full[...].reshape(gram_ref.shape)

    @pl.when(a_other)
    def _():
        rcopy(
            result_out.at[0], result_in, up_send.at[0], up_recv.at[0], dev(layer, x, z, c)
        ).wait_recv()
        upd_ref[...] = result_in[...]

    sent(first)
    sent(second)
    sent(gram_copies)
    sent(gram_gather)

    @pl.when(a_other)
    def _():
        a_remote.wait_send()

    @pl.when(has_prev)
    def _():
        map_shift.wait_send()
        grad_shift.wait_send()

    @pl.when(is_rim)
    def _():
        z_copy(0, z_out_wide, z_in_wide).wait_send()
        z_copy(1, z_out, z_in).wait_send()
        z_copy(2, gram_z_out, gram_z_in).wait_send()

    @pl.when(is_root)
    def _():
        for pz in range(NZ):
            if pz != ROOT:
                bc_copies[pz].wait_send()

    @pl.when(is_root & has_prev)
    def _():
        for copy in pre_copies:
            copy.wait_send()


def per_device(layers, layer_inputs, output_grads, input_inverse, grad_inverse):
    _, images, side, _, width = layer_inputs.shape
    rows = images * side * side
    own_rows = input_inverse.shape[1]
    lanes = TAPS * width
    n = NX * NC
    strip = width // n
    block_rows = lanes // n
    gram_rows = 2 * width // n
    scale = 1.0 / (rows * n * NZ)
    vmem = pltpu.VMEM
    dma = pltpu.SemaphoreType.DMA
    scratch = [
        vmem((rows, lanes), BF16),
        vmem((rows, lanes), BF16),
        vmem((width, rows), BF16),
        vmem((rows, width), BF16),
        vmem((rows, width), BF16),
        vmem((n, strip, lanes), F32),
        vmem((n, strip, lanes), F32),
        vmem((n, strip, lanes), F32),
        vmem((n, strip, lanes), BF16),
        vmem((n, strip, lanes), BF16),
        vmem((strip, lanes), F32),
        vmem((strip, lanes), BF16),
        vmem((NZ, strip, lanes), BF16),
        vmem((strip, lanes), F32),
        vmem((NZ, strip, lanes), F32),
        vmem((n, strip, lanes), F32),
        vmem((n, strip, lanes), F32),
        vmem((NZ, own_rows, lanes), F32),
        vmem((block_rows, lanes), F32),
        vmem((2 * block_rows, lanes), BF16),
        vmem((n, block_rows, width), BF16),
        vmem((block_rows, width), BF16),
        vmem((block_rows, width), F32),
        vmem((block_rows, width), F32),
        vmem((NZ, own_rows, width), F32),
        vmem((own_rows, width), F32),
        vmem((n, gram_rows, width), F32),
        vmem((n, gram_rows, width), F32),
        vmem((gram_rows, width), F32),
        vmem((NZ, gram_rows, width), F32),
        vmem((n, gram_rows, width), F32),
        dma((7, n)),
        dma((7, n)),
        dma((3,)),
        dma((3, NZ)),
        dma((1,)),
        dma((NZ,)),
        dma((2,)),
        dma((2,)),
        dma((NZ,)),
        dma((1,)),
        dma((NZ,)),
        dma((1,)),
        dma((NZ,)),
        dma((1,)),
    ]
    whole = pl.BlockSpec(memory_space=pltpu.VMEM)
    update, grams = pl.pallas_call(
        functools.partial(kernel, layers, images, side, scale),
        out_shape=(
            jax.ShapeDtypeStruct((own_rows, width), F32),
            jax.ShapeDtypeStruct((2, width, width), F32),
        ),
        in_specs=[whole] * 4,
        out_specs=(whole, whole),
        scratch_shapes=scratch,
        compiler_params=pltpu.CompilerParams(
            collective_id=0, has_side_effects=True, vmem_limit_bytes=48 * 1024 * 1024
        ),
        name="kfac_step",
    )(
        layer_inputs.reshape(rows, width),
        output_grads.reshape(rows, width),
        input_inverse.reshape(own_rows, lanes),
        grad_inverse.reshape(width, width),
    )
    return update[None], grams[None]


def solution(mesh):
    assert mesh.shape["pos"] == NX * NZ * NC
    return jax.shard_map(
        functools.partial(per_device, mesh.shape["layer"]),
        mesh=mesh,
        in_specs=(
            P("layer", "pos", None, None, None),
            P("layer", "pos", None, None, None),
            P("layer", "pos", None),
            P("layer", None, None),
        ),
        out_specs=(P("layer", "pos", None), P("layer", None, None, None)),
        check_vma=False,
    )
```

```python
import functools

import jax
import jax.numpy as jnp
from jax import lax
from jax.experimental import pallas as pl
from jax.experimental.pallas import tpu as pltpu
from jax.sharding import PartitionSpec as P

NX, NY, NZ, NC = 4, 4, 8, 2
ROOT = 3
TAPS = 9
MESH = pl.DeviceIdType.MESH
F32 = jnp.float32
BF16 = jnp.bfloat16
HIGH = lax.Precision.HIGHEST


def offsets():
    return sorted(range(1, NX), key=lambda d: -min(d, NX - d))


def rcopy(src, dst, send_sem, recv_sem, to):
    return pltpu.make_async_remote_copy(
        src_ref=src,
        dst_ref=dst,
        send_sem=send_sem,
        recv_sem=recv_sem,
        device_id=to,
        device_id_type=MESH,
    )


def dot(a, b, contract=(1, 0), precision=None):
    return lax.dot_general(
        a,
        b,
        (((contract[0],), (contract[1],)), ((), ())),
        precision=precision,
        preferred_element_type=F32,
    )


def unfold(src, dst, images, side, width):
    area = side * side
    rows = images * area
    value = src[...].astype(F32)
    col = lax.rem(lax.broadcasted_iota(jnp.int32, (rows, width), 0), side)
    before = jnp.where(col == 0, 0.0, pltpu.roll(value, 1, 0))
    after = jnp.where(col == side - 1, 0.0, pltpu.roll(value, rows - 1, 0))
    edge = jnp.zeros((side, width), BF16)
    for s, piece in enumerate((before, value, after)):
        piece = piece.astype(BF16)
        for image in range(images):
            top = image * area
            one = piece[top : top + area]
            lanes = pl.ds(s * width, width)
            dst[pl.ds(top, side), lanes] = edge
            dst[pl.ds(top + side, area - side), lanes] = one[: area - side]
            lanes = pl.ds((3 + s) * width, width)
            dst[pl.ds(top, area), lanes] = one
            lanes = pl.ds((6 + s) * width, width)
            dst[pl.ds(top, area - side), lanes] = one[side:]
            dst[pl.ds(top + area - side, side), lanes] = edge


def kernel(
    layers,
    images,
    side,
    scale,
    x_hbm,
    g_hbm,
    a_ref,
    ginv_hbm,
    upd_ref,
    gram_ref,
    xg_ref,
    ginv_ref,
    patches,
    patches_next,
    grad_t,
    xg_next,
    relay,
    part,
    part_one,
    in_one,
    out_x_one,
    in_x_one,
    out_two,
    in_two,
    out_x_two,
    in_x_two,
    plane_sum,
    z_out,
    z_in,
    z_out_wide,
    z_in_wide,
    full,
    full_wide,
    a_in,
    a_all,
    a_two,
    pre,
    rows_full,
    base,
    result,
    result_out,
    result_in,
    gram_part,
    gram_in,
    gram_out_x,
    gram_in_x,
    gram_z_out,
    gram_z_in,
    gram_full,
    ex_send,
    ex_recv,
    z_send,
    z_recv,
    a_send,
    a_recv,
    shift_send,
    shift_recv,
    relay_send,
    relay_recv,
    far_send,
    far_recv,
    pre_send,
    pre_recv,
    bc_send,
    bc_recv,
    up_send,
    up_recv,
    load_sem,
):
    layer = lax.axis_index("layer")
    pos = lax.axis_index("pos")
    c = lax.rem(pos, NC)
    z = lax.rem(lax.div(pos, NC), NZ)
    x = lax.div(pos, NC * NZ)
    block = x * NC + c
    strip = c * NX + x
    n = NX * NC
    _, rows, width = xg_ref.shape
    quarter = rows // NY
    y = lax.rem(layer, NY)
    lanes = TAPS * width
    per = NZ // NC
    own_rows = result_in.shape[0]
    is_root = z == ROOT
    is_rim = z != ROOT
    has_next = layer < layers - 1
    has_prev = layer > 0
    sends_far = has_prev & (y == 0)
    sends_near = has_prev & (y != 0)
    relays = (layer >= NY) & (y != 0)
    late = has_next & (y == NY - 1)

    def dev(lay, px, pz, pc):
        return (lay, (px * NZ + pz) * NC + pc)

    def ahead(dx):
        return lax.rem(x + dx, NX)

    def behind(dx):
        return lax.rem(x + NX - dx, NX)

    other = NC - 1 - c

    loads = [
        pltpu.make_async_copy(src, dst, load_sem.at[i])
        for i, (src, dst) in enumerate(((x_hbm, xg_ref.at[0]), (g_hbm, xg_ref.at[1]), (ginv_hbm, ginv_ref)))
    ]
    for load in loads:
        load.start()

    barrier = pltpu.get_barrier_semaphore()

    def greet(to):
        pl.semaphore_signal(barrier, inc=1, device_id=to, device_id_type=MESH)

    greet(dev(layer, x, z, other))
    for dx in offsets():
        greet(dev(layer, ahead(dx), z, c))

    @pl.when(is_rim)
    def _():
        for pc in range(NC):
            greet(dev(layer, x, ROOT, pc))

    @pl.when(is_root)
    def _():
        for pz in range(NZ):
            if pz != ROOT:
                for pc in range(NC):
                    greet(dev(layer, x, pz, pc))

    @pl.when(has_next)
    def _():
        greet(dev(layer + 1, x, z, c))

    @pl.when(has_next & is_rim)
    def _():
        greet(dev(layer + 1, x, ROOT, c))

    @pl.when(relays)
    def _():
        greet(dev(layer - y, x, z, c))

    @pl.when(late)
    def _():
        for q in range(1, NY):
            greet(dev(layer + 1 + q, x, z, c))

    for load in loads:
        load.wait()
    unfold(xg_ref.at[0], patches, images, side, width)
    grad_t[...] = xg_ref[1].T

    root = is_root.astype(jnp.int32)
    prv = has_prev.astype(jnp.int32)
    expected = NX + prv + sends_far.astype(jnp.int32) * (NY - 1) + relays.astype(jnp.int32)
    expected = expected + root * ((NZ - 1) * NC + prv * (NZ - 1)) + (1 - root) * NC
    pl.semaphore_wait(barrier, expected)

    shift = rcopy(xg_ref, xg_next, shift_send.at[0], shift_recv.at[0], dev(layer - 1, x, z, c))

    def piece(ref, q):
        return ref.at[:, pl.ds(pl.multiple_of(q * quarter, quarter), quarter)]

    to_relay = [
        rcopy(
            piece(xg_ref, q),
            relay,
            relay_send.at[q],
            relay_recv.at[0],
            dev(layer + q, x, z, c),
        )
        for q in range(1, NY)
    ]
    far_own = rcopy(
        piece(xg_ref, 0), piece(xg_next, 0), far_send.at[0], far_recv.at[0], dev(layer - 1, x, z, c)
    )
    far_relay = rcopy(
        relay, piece(xg_next, y), far_send.at[0], far_recv.at[y], dev(layer - y - 1, x, z, c)
    )

    def arrived():
        @pl.when(has_next & jnp.logical_not(late))
        def _():
            shift.wait_recv()

        @pl.when(late)
        def _():
            for q in range(NY):
                rcopy(
                    relay, piece(xg_next, q), far_send.at[0], far_recv.at[q], dev(layer, x, z, other)
                ).wait_recv()

    half = lax.div(z, per)
    slot = lax.rem(z, per) * NC + c
    a_self = is_root & (half == c)
    a_other = jnp.logical_not(a_self)
    a_remote = rcopy(a_ref, a_in.at[slot], a_send.at[0], a_recv.at[slot], dev(layer, x, ROOT, half))
    a_local = pltpu.make_async_copy(a_ref, a_in.at[slot], a_recv.at[slot])

    @pl.when(a_other)
    def _():
        a_remote.start()

    @pl.when(a_self)
    def _():
        a_local.start()

    @pl.when(sends_near)
    def _():
        shift.start()

    @pl.when(sends_far)
    def _():
        for copy in to_relay:
            copy.start()

    def sent(copies):
        for copy in copies:
            copy.wait_send()

    def plane_start(kind, out, in_core):
        copies = []
        for dx in offsets() + [0]:
            copy = rcopy(
                out.at[other * NX + ahead(dx)],
                in_core.at[dx],
                ex_send.at[kind, dx],
                ex_recv.at[kind, dx],
                dev(layer, x, z, other),
            )
            copy.start()
            copies.append(copy)
        return copies

    def plane_finish(kind, core_copies, part, in_core, out_x, in_x):
        copies = []
        for dx, arrival in zip(offsets(), core_copies):
            arrival.wait_recv()
            out_x[dx] = (part[c * NX + ahead(dx)] + in_core[dx].astype(F32)).astype(out_x.dtype)
            copy = rcopy(
                out_x.at[dx],
                in_x.at[dx],
                ex_send.at[kind, NX + dx],
                ex_recv.at[kind, NX + dx],
                dev(layer, ahead(dx), z, c),
            )
            copy.start()
            copies.append(copy)
        core_copies[-1].wait_recv()
        total = part[strip] + in_core[0].astype(F32)
        for dx, copy in reversed(list(zip(offsets(), copies))):
            copy.wait_recv()
            total = total + in_x[dx].astype(F32)
        return total, copies

    def gather(kind, buf, own):
        copies = []
        for dx in offsets():
            copies.append(
                rcopy(
                    buf.at[own],
                    buf.at[own],
                    ex_send.at[kind, dx],
                    ex_recv.at[kind, dx],
                    dev(layer, ahead(dx), z, c),
                )
            )
        copies.append(
            rcopy(
                buf.at[own],
                buf.at[own],
                ex_send.at[kind, 0],
                ex_recv.at[kind, 0],
                dev(layer, x, z, other),
            )
        )
        return copies

    def gathered(kind, buf, place):
        copies = []
        for dx in reversed(offsets()):
            got = buf.at[place(behind(dx), c)]
            rcopy(
                got, got, ex_send.at[kind, dx], ex_recv.at[kind, dx], dev(layer, x, z, other)
            ).wait_recv()
            copy = rcopy(
                got,
                got,
                ex_send.at[kind, NX + dx],
                ex_recv.at[kind, NX + dx],
                dev(layer, x, z, other),
            )
            copy.start()
            copies.append(copy)
        for slot_of, dx in [(0, 0)] + [(NX + dx, dx) for dx in reversed(offsets())]:
            got = buf.at[place(behind(dx), other)]
            rcopy(
                got,
                got,
                ex_send.at[kind, slot_of],
                ex_recv.at[kind, slot_of],
                dev(layer, x, z, other),
            ).wait_recv()
        return copies

    def by_strip(px, pc):
        return pc * NX + px

    def by_block(px, pc):
        return px * NC + pc

    def z_copy(kind, src, dst):
        return rcopy(
            src, dst.at[z], z_send.at[kind], z_recv.at[kind, z], dev(layer, x, ROOT, c)
        )

    def z_arrived(kind, src, dst, pz):
        rcopy(
            src, dst.at[pz], z_send.at[kind], z_recv.at[kind, pz], dev(layer, x, ROOT, c)
        ).wait_recv()

    z_bufs = ((z_out_wide, z_in_wide), (z_out, z_in))

    def z_start(z_slot, total):
        plane_sum[...] = total
        src, dst = z_bufs[z_slot]

        @pl.when(is_rim)
        def _():
            src[...] = total.astype(src.dtype)
            z_copy(z_slot, src, dst).start()

    def root_total(z_slot, buf):
        total = plane_sum[...]
        src, dst = z_bufs[z_slot]
        for pz in range(NZ):
            if pz != ROOT:
                z_arrived(z_slot, src, dst, pz)
                total = total + dst[pz].astype(F32)
        buf[strip] = total * scale

    def fold(both):
        half_rows = both.shape[0] // 2
        return both[:half_rows] + both[half_rows:]

    def times_inverse(buf):
        value = buf[...].reshape(width, lanes)
        top = value.astype(BF16)
        low = (value - top.astype(F32)).astype(BF16)
        both = dot(a_two[...], jnp.concatenate([top, low], axis=0), (1, 1))
        return fold(both[:, :width] + both[:, width:])

    part_one[...] = dot(grad_t[...], patches[...]).reshape(part_one.shape)
    first = plane_start(0, part_one, in_one)
    total, first_x = plane_finish(0, first, part_one, in_one, out_x_one, in_x_one)
    z_start(0, total)

    @pl.when(jnp.logical_not(has_next))
    def _():
        xg_next[...] = jnp.zeros_like(xg_next)
        pre[...] = jnp.zeros_like(pre)

    half_blocks = gram_part.shape[0] // 2

    def grams():
        arrived()
        shape = (half_blocks, gram_part.shape[1], width)
        gram_part[pl.ds(0, half_blocks)] = dot(grad_t[...], xg_ref[1]).reshape(shape)
        gram_part[pl.ds(half_blocks, half_blocks)] = dot(grad_t[...], xg_next[1]).reshape(shape)
        copies = plane_start(2, gram_part, gram_in)
        gram, copies_x = plane_finish(2, copies, gram_part, gram_in, gram_out_x, gram_in_x)
        gram_z_out[...] = gram

        @pl.when(is_rim)
        def _():
            z_copy(2, gram_z_out, gram_z_in).start()

        sent(copies)
        sent(copies_x)

    @pl.when(jnp.logical_not(late))
    def _():
        grams()

    @pl.when(sends_far)
    def _():
        far_own.start()

    @pl.when(relays)
    def _():
        to_relay[0].wait_recv()
        far_relay.start()

    pre_copies = [
        rcopy(
            rows_full,
            pre.at[block],
            pre_send.at[pz],
            pre_recv.at[0],
            dev(layer - 1, x, pz, c),
        )
        for pz in range(NZ)
    ]

    @pl.when(is_root)
    def _():
        for q in range(NZ):
            pltpu.make_async_copy(a_ref, a_in.at[q], a_recv.at[q]).wait()
            a_all[pl.ds(q * own_rows, own_rows), :] = a_in[q, :, 0, :]
        rows = a_all[...]
        top = rows.astype(BF16)
        a_two[pl.ds(0, rows.shape[0]), :] = top
        a_two[pl.ds(rows.shape[0], rows.shape[0]), :] = (rows - top.astype(F32)).astype(BF16)
        root_total(0, full_wide)
        copies = gather(1, full_wide, strip)
        for copy in copies:
            copy.start()
        passed = gathered(1, full_wide, by_strip)
        value = dot(times_inverse(full_wide), ginv_ref[...], precision=HIGH)
        base[...] = value
        rows_full[...] = value.astype(BF16)

        @pl.when(has_prev)
        def _():
            for copy in pre_copies:
                copy.start()

        sent(copies)
        sent(passed)

    @pl.when(late)
    def _():
        grams()

    unfold(xg_next.at[0], patches_next, images, side, width)

    @pl.when(has_next)
    def _():
        rcopy(
            rows_full, pre.at[block], pre_send.at[0], pre_recv.at[0], dev(layer, x, z, other)
        ).wait_recv()
        copies = gather(3, pre, block)
        for copy in copies:
            copy.start()
        passed = gathered(3, pre, by_block)
        sent(copies)
        sent(passed)

    mapped = dot(patches_next[...], pre[...].reshape(lanes, width)).astype(BF16)
    product = dot(mapped.T, patches[...])
    part[...] = product.reshape(part.shape)
    out_two[...] = product.astype(BF16).reshape(out_two.shape)
    second = plane_start(4, out_two, in_two)
    total, second_x = plane_finish(4, second, part, in_two, out_x_two, in_x_two)
    z_start(1, total)

    bc_copies = [
        rcopy(
            gram_full.at[strip],
            gram_full.at[strip],
            bc_send.at[pz],
            bc_recv.at[0],
            dev(layer, x, pz, c),
        )
        for pz in range(NZ)
    ]

    gram_gather = gather(5, gram_full, strip)

    @pl.when(is_rim)
    def _():
        bc_copies[ROOT].wait_recv()
        for copy in gram_gather:
            copy.start()

    @pl.when(is_root)
    def _():
        root_total(1, full)
        copies = gather(6, full, strip)
        for copy in copies:
            copy.start()
        total = gram_z_out[...]
        for pz in range(NZ):
            if pz != ROOT:
                z_arrived(2, gram_z_out, gram_z_in, pz)
                total = total + gram_z_in[pz]
        gram_full[strip] = total * scale
        for pz in range(NZ):
            if pz != ROOT:
                bc_copies[pz].start()
        for copy in gram_gather:
            copy.start()
        passed = gathered(6, full, by_strip)
        gram_passed = gathered(5, gram_full, by_strip)
        cross_gram = gram_full[pl.ds(half_blocks, half_blocks)].reshape(width, width)
        mix = dot(cross_gram, ginv_ref[...], (0, 0), HIGH)
        value = base[...] - dot(times_inverse(full), mix, precision=HIGH)
        result[...] = value
        for q in range(NZ):
            result_out[q] = result[pl.ds(q * own_rows, own_rows), :]
            copy = rcopy(
                result_out.at[q],
                result_in,
                up_send.at[q],
                up_recv.at[0],
                dev(layer, x, c * per + q // NC, q % NC),
            )
            if q // NC == ROOT % per and q % NC == ROOT // per:

                @pl.when(c == ROOT // per)
                def _(q=q):
                    upd_ref[...] = result_out[q]

                @pl.when(c != ROOT // per)
                def _(copy=copy):
                    copy.start()
                    copy.wait_send()
            else:
                copy.start()
        for q in range(NZ):
            if not (q // NC == ROOT % per and q % NC == ROOT // per):
                rcopy(
                    result_out.at[q],
                    result_in,
                    up_send.at[q],
                    up_recv.at[0],
                    dev(layer, x, c * per + q // NC, q % NC),
                ).wait_send()
        sent(copies)
        sent(passed)
        sent(gram_passed)

    @pl.when(is_rim)
    def _():
        sent(gathered(5, gram_full, by_strip))

    gram_ref[...] = gram_full[...].reshape(gram_ref.shape)

    @pl.when(a_other)
    def _():
        rcopy(
            result_out.at[0], result_in, up_send.at[0], up_recv.at[0], dev(layer, x, z, other)
        ).wait_recv()
        upd_ref[...] = result_in[...]

    sent(first)
    sent(first_x)
    sent(second)
    sent(second_x)
    sent(gram_gather)

    @pl.when(a_other)
    def _():
        a_remote.wait_send()

    @pl.when(sends_near)
    def _():
        shift.wait_send()

    @pl.when(sends_far)
    def _():
        for copy in to_relay:
            copy.wait_send()
        far_own.wait_send()

    @pl.when(relays)
    def _():
        far_relay.wait_send()

    @pl.when(is_rim)
    def _():
        z_copy(0, z_out_wide, z_in_wide).wait_send()
        z_copy(1, z_out, z_in).wait_send()
        z_copy(2, gram_z_out, gram_z_in).wait_send()

    @pl.when(is_root)
    def _():
        for pz in range(NZ):
            if pz != ROOT:
                bc_copies[pz].wait_send()

    @pl.when(is_root & has_prev)
    def _():
        for copy in pre_copies:
            copy.wait_send()


def per_device(layers, layer_inputs, output_grads, input_inverse, grad_inverse):
    _, images, side, _, width = layer_inputs.shape
    rows = images * side * side
    own_rows = input_inverse.shape[1]
    lanes = TAPS * width
    n = NX * NC
    strip = width // n
    block_rows = lanes // n
    gram_rows = 2 * width // n
    scale = 1.0 / (rows * n * NZ)
    vmem = pltpu.VMEM
    dma = pltpu.SemaphoreType.DMA
    scratch = [
        vmem((2, rows, width), BF16),
        vmem((width, width), F32),
        vmem((rows, lanes), BF16),
        vmem((rows, lanes), BF16),
        vmem((width, rows), BF16),
        vmem((2, rows, width), BF16),
        vmem((2, rows // NY, width), BF16),
        vmem((n, strip, lanes), F32),
        vmem((n, strip, lanes), F32),
        vmem((NX, strip, lanes), F32),
        vmem((NX, strip, lanes), F32),
        vmem((NX, strip, lanes), F32),
        vmem((n, strip, lanes), BF16),
        vmem((NX, strip, lanes), BF16),
        vmem((NX, strip, lanes), BF16),
        vmem((NX, strip, lanes), BF16),
        vmem((strip, lanes), F32),
        vmem((strip, lanes), BF16),
        vmem((NZ, strip, lanes), BF16),
        vmem((strip, lanes), F32),
        vmem((NZ, strip, lanes), F32),
        vmem((n, strip, lanes), F32),
        vmem((n, strip, lanes), F32),
        vmem((NZ, own_rows, 1, lanes), F32),
        vmem((block_rows, lanes), F32),
        vmem((2 * block_rows, lanes), BF16),
        vmem((n, block_rows, width), BF16),
        vmem((block_rows, width), BF16),
        vmem((block_rows, width), F32),
        vmem((block_rows, width), F32),
        vmem((NZ, own_rows, width), F32),
        vmem((own_rows, width), F32),
        vmem((n, gram_rows, width), F32),
        vmem((NX, gram_rows, width), F32),
        vmem((NX, gram_rows, width), F32),
        vmem((NX, gram_rows, width), F32),
        vmem((gram_rows, width), F32),
        vmem((NZ, gram_rows, width), F32),
        vmem((n, gram_rows, width), F32),
        dma((7, n)),
        dma((7, n)),
        dma((3,)),
        dma((3, NZ)),
        dma((1,)),
        dma((NZ,)),
        dma((1,)),
        dma((1,)),
        dma((NY,)),
        dma((1,)),
        dma((NY,)),
        dma((NY,)),
        dma((NZ,)),
        dma((1,)),
        dma((NZ,)),
        dma((1,)),
        dma((NZ,)),
        dma((1,)),
        dma((3,)),
    ]
    whole = pl.BlockSpec(memory_space=pltpu.VMEM)
    update, grams = pl.pallas_call(
        functools.partial(kernel, layers, images, side, scale),
        out_shape=(
            jax.ShapeDtypeStruct((own_rows, width), F32),
            jax.ShapeDtypeStruct((2, width, width), F32),
        ),
        in_specs=[pl.BlockSpec(memory_space=pltpu.HBM)] * 4,
        out_specs=(whole, whole),
        scratch_shapes=scratch,
        compiler_params=pltpu.CompilerParams(
            collective_id=0, has_side_effects=True, vmem_limit_bytes=63 * 1024 * 1024
        ),
        name="kfac_step",
    )(
        layer_inputs.reshape(rows, width),
        output_grads.reshape(rows, width),
        input_inverse.transpose(1, 0, 2),
        grad_inverse.reshape(width, width),
    )
    return update[None], grams[None]


def solution(mesh):
    assert mesh.shape["pos"] == NX * NZ * NC and mesh.shape["layer"] % NY == 0
    return jax.shard_map(
        functools.partial(per_device, mesh.shape["layer"]),
        mesh=mesh,
        in_specs=(
            P("layer", "pos", None, None, None),
            P("layer", "pos", None, None, None),
            P("layer", "pos", None),
            P("layer", None, None),
        ),
        out_specs=(P("layer", "pos", None), P("layer", None, None, None)),
        check_vma=False,
    )
```

```python
import functools

import jax
import jax.numpy as jnp
from jax import lax
from jax.experimental import pallas as pl
from jax.experimental.pallas import tpu as pltpu
from jax.sharding import PartitionSpec as P

NX, NY, NZ, NC = 4, 4, 8, 2
ROOT = 3
TAPS = 9
MESH = pl.DeviceIdType.MESH
F32 = jnp.float32
BF16 = jnp.bfloat16
HIGH = lax.Precision.HIGHEST


def offsets():
    return sorted(range(1, NX), key=lambda d: -min(d, NX - d))


def rcopy(src, dst, send_sem, recv_sem, to):
    return pltpu.make_async_remote_copy(
        src_ref=src,
        dst_ref=dst,
        send_sem=send_sem,
        recv_sem=recv_sem,
        device_id=to,
        device_id_type=MESH,
    )


def dot(a, b, contract=(1, 0), precision=None):
    return lax.dot_general(
        a,
        b,
        (((contract[0],), (contract[1],)), ((), ())),
        precision=precision,
        preferred_element_type=F32,
    )


def unfold(src, dst, images, side, width):
    area = side * side
    rows = images * area
    value = src[...].astype(F32)
    col = lax.rem(lax.broadcasted_iota(jnp.int32, (rows, width), 0), side)
    before = jnp.where(col == 0, 0.0, pltpu.roll(value, 1, 0))
    after = jnp.where(col == side - 1, 0.0, pltpu.roll(value, rows - 1, 0))
    edge = jnp.zeros((side, width), BF16)
    for s, piece in enumerate((before, value, after)):
        piece = piece.astype(BF16)
        for image in range(images):
            top = image * area
            one = piece[top : top + area]
            lanes = pl.ds(s * width, width)
            dst[pl.ds(top, side), lanes] = edge
            dst[pl.ds(top + side, area - side), lanes] = one[: area - side]
            lanes = pl.ds((3 + s) * width, width)
            dst[pl.ds(top, area), lanes] = one
            lanes = pl.ds((6 + s) * width, width)
            dst[pl.ds(top, area - side), lanes] = one[side:]
            dst[pl.ds(top + area - side, side), lanes] = edge


def kernel(
    layers,
    images,
    side,
    scale,
    x_hbm,
    g_hbm,
    a_ref,
    ginv_hbm,
    upd_ref,
    gram_ref,
    xg_ref,
    ginv_ref,
    patches,
    patches_next,
    grad_t,
    xg_next,
    relay,
    part,
    part_one,
    in_one,
    out_x_one,
    in_x_one,
    out_two,
    in_two,
    out_x_two,
    in_x_two,
    plane_sum,
    z_out,
    z_in,
    z_out_wide,
    z_in_wide,
    full,
    full_wide,
    a_in,
    a_all,
    a_two,
    pre,
    rows_full,
    base,
    result,
    result_out,
    result_in,
    gram_part,
    gram_in,
    gram_out_x,
    gram_in_x,
    gram_z_out,
    gram_z_in,
    gram_full,
    ex_send,
    ex_recv,
    z_send,
    z_recv,
    a_send,
    a_recv,
    shift_send,
    shift_recv,
    relay_send,
    relay_recv,
    far_send,
    far_recv,
    pre_send,
    pre_recv,
    bc_send,
    bc_recv,
    up_send,
    up_recv,
    load_sem,
    go_sem,
):
    layer = lax.axis_index("layer")
    pos = lax.axis_index("pos")
    c = lax.rem(pos, NC)
    z = lax.rem(lax.div(pos, NC), NZ)
    x = lax.div(pos, NC * NZ)
    block = x * NC + c
    strip = c * NX + x
    n = NX * NC
    _, rows, width = xg_ref.shape
    quarter = rows // NY
    y = lax.rem(layer, NY)
    lanes = TAPS * width
    per = NZ // NC
    own_rows = result_in.shape[0]
    is_root = z == ROOT
    is_rim = z != ROOT
    has_next = layer < layers - 1
    has_prev = layer > 0
    sends_far = has_prev & (y == 0)
    sends_near = has_prev & (y != 0)
    relays = (layer >= NY) & (y != 0)
    late = has_next & (y == NY - 1)

    def dev(lay, px, pz, pc):
        return (lay, (px * NZ + pz) * NC + pc)

    def ahead(dx):
        return lax.rem(x + dx, NX)

    def behind(dx):
        return lax.rem(x + NX - dx, NX)

    other = NC - 1 - c
    far_first = sorted(range(NZ), key=lambda pz: -abs(pz - ROOT))
    others = far_first[:-1]

    loads = [
        pltpu.make_async_copy(src, dst, load_sem.at[i])
        for i, (src, dst) in enumerate(((x_hbm, xg_ref.at[0]), (g_hbm, xg_ref.at[1]), (ginv_hbm, ginv_ref)))
    ]
    for load in loads:
        load.start()

    barrier = pltpu.get_barrier_semaphore()

    def greet(to):
        pl.semaphore_signal(barrier, inc=1, device_id=to, device_id_type=MESH)

    greet(dev(layer, x, z, other))
    for dx in offsets():
        greet(dev(layer, ahead(dx), z, c))

    @pl.when(is_rim)
    def _():
        for pc in range(NC):
            greet(dev(layer, x, ROOT, pc))

    @pl.when(is_root)
    def _():
        for pz in range(NZ):
            if pz != ROOT:
                for pc in range(NC):
                    greet(dev(layer, x, pz, pc))

    @pl.when(has_next)
    def _():
        greet(dev(layer + 1, x, z, c))

    @pl.when(has_next & is_rim)
    def _():
        greet(dev(layer + 1, x, ROOT, c))

    @pl.when(relays)
    def _():
        greet(dev(layer - y, x, z, c))

    @pl.when(late)
    def _():
        for q in range(1, NY):
            greet(dev(layer + 1 + q, x, z, c))

    for load in loads:
        load.wait()
    unfold(xg_ref.at[0], patches, images, side, width)
    grad_t[...] = xg_ref[1].T

    root = is_root.astype(jnp.int32)
    prv = has_prev.astype(jnp.int32)
    expected = NX + prv + sends_far.astype(jnp.int32) * (NY - 1) + relays.astype(jnp.int32)
    expected = expected + root * ((NZ - 1) * NC + prv * (NZ - 1)) + (1 - root) * NC
    pl.semaphore_wait(barrier, expected)

    shift = rcopy(xg_ref, xg_next, shift_send.at[0], shift_recv.at[0], dev(layer - 1, x, z, c))

    def piece(ref, q):
        return ref.at[:, pl.ds(pl.multiple_of(q * quarter, quarter), quarter)]

    to_relay = [
        rcopy(
            piece(xg_ref, q),
            relay,
            relay_send.at[q],
            relay_recv.at[0],
            dev(layer + q, x, z, c),
        )
        for q in range(1, NY)
    ]
    far_own = rcopy(
        piece(xg_ref, 0), piece(xg_next, 0), far_send.at[0], far_recv.at[0], dev(layer - 1, x, z, c)
    )
    far_relay = rcopy(
        relay, piece(xg_next, y), far_send.at[0], far_recv.at[y], dev(layer - y - 1, x, z, c)
    )

    def arrived():
        @pl.when(has_next & jnp.logical_not(late))
        def _():
            shift.wait_recv()

        @pl.when(late)
        def _():
            for q in range(NY):
                rcopy(
                    relay, piece(xg_next, q), far_send.at[0], far_recv.at[q], dev(layer, x, z, other)
                ).wait_recv()

    half = lax.div(z, per)
    slot = lax.rem(z, per) * NC + c
    a_self = is_root & (half == c)
    a_other = jnp.logical_not(a_self)
    a_remote = rcopy(a_ref, a_in.at[slot], a_send.at[0], a_recv.at[slot], dev(layer, x, ROOT, half))
    a_local = pltpu.make_async_copy(a_ref, a_in.at[slot], a_recv.at[slot])

    @pl.when(a_other)
    def _():
        a_remote.start()

    @pl.when(a_self)
    def _():
        a_local.start()

    @pl.when(sends_near)
    def _():
        shift.start()

    @pl.when(sends_far)
    def _():
        for copy in to_relay:
            copy.start()

    def sent(copies):
        for copy in copies:
            copy.wait_send()

    def begin(copies):
        for copy in copies:
            copy.start()

    def core_copies(kind, out, in_core):
        return [
            rcopy(
                out.at[other * NX + ahead(dx)],
                in_core.at[dx],
                ex_send.at[kind, dx],
                ex_recv.at[kind, dx],
                dev(layer, x, z, other),
            )
            for dx in offsets() + [0]
        ]

    def x_copies(kind, out_x, in_x):
        return [
            rcopy(
                out_x.at[dx],
                in_x.at[dx],
                ex_send.at[kind, NX + dx],
                ex_recv.at[kind, NX + dx],
                dev(layer, ahead(dx), z, c),
            )
            for dx in offsets()
        ]

    def pass_on(core, along, part, in_core, out_x):
        for dx, arrival, copy in zip(offsets(), core, along):
            arrival.wait_recv()
            out_x[dx] = (part[c * NX + ahead(dx)] + in_core[dx].astype(F32)).astype(out_x.dtype)
            copy.start()

    def plane_total(core, along, part, in_core, in_x):
        core[-1].wait_recv()
        total = part[strip] + in_core[0].astype(F32)
        for dx, copy in reversed(list(zip(offsets(), along))):
            copy.wait_recv()
            total = total + in_x[dx].astype(F32)
        return total

    def gather(kind, buf, own):
        targets = [(dx, dev(layer, ahead(dx), z, c)) for dx in offsets()]
        return [
            rcopy(buf.at[own], buf.at[own], ex_send.at[kind, dx], ex_recv.at[kind, dx], to)
            for dx, to in targets + [(0, dev(layer, x, z, other))]
        ]

    def passes(kind, buf, place):
        copies = []
        for dx in reversed(offsets()):
            got = buf.at[place(behind(dx), c)]
            s = NX + dx
            copies.append(
                rcopy(got, got, ex_send.at[kind, s], ex_recv.at[kind, s], dev(layer, x, z, other))
            )
        return copies

    def arrival(kind, s, got):
        rcopy(
            got, got, ex_send.at[kind, s], ex_recv.at[kind, s], dev(layer, x, z, other)
        ).wait_recv()

    def gathered(kind, buf, place):
        for dx, copy in zip(reversed(offsets()), passes(kind, buf, place)):
            arrival(kind, dx, buf.at[place(behind(dx), c)])
            copy.start()
        arrival(kind, 0, buf.at[place(x, other)])
        for dx in reversed(offsets()):
            arrival(kind, NX + dx, buf.at[place(behind(dx), other)])

    def by_strip(px, pc):
        return pc * NX + px

    def by_block(px, pc):
        return px * NC + pc

    def z_copy(kind, src, dst):
        return rcopy(
            src, dst.at[z], z_send.at[kind], z_recv.at[kind, z], dev(layer, x, ROOT, c)
        )

    def z_arrived(kind, src, dst, pz):
        rcopy(
            src, dst.at[pz], z_send.at[kind], z_recv.at[kind, pz], dev(layer, x, ROOT, c)
        ).wait_recv()

    z_bufs = ((z_out_wide, z_in_wide), (z_out, z_in))

    def z_start(z_slot, total):
        plane_sum[...] = total
        src, dst = z_bufs[z_slot]

        @pl.when(is_rim)
        def _():
            src[...] = total.astype(src.dtype)
            z_copy(z_slot, src, dst).start()

    def root_total(z_slot, buf):
        total = plane_sum[...]
        src, dst = z_bufs[z_slot]
        for pz in others:
            z_arrived(z_slot, src, dst, pz)
            total = total + dst[pz].astype(F32)
        buf[strip] = total * scale

    def fold(both):
        half_rows = both.shape[0] // 2
        return both[:half_rows] + both[half_rows:]

    def times_inverse(buf):
        value = buf[...].reshape(width, lanes)
        top = value.astype(BF16)
        low = (value - top.astype(F32)).astype(BF16)
        both = dot(a_two[...], jnp.concatenate([top, low], axis=0), (1, 1))
        return fold(both[:, :width] + both[:, width:])

    part_one[...] = dot(grad_t[...], patches[...]).reshape(part_one.shape)
    first = core_copies(0, part_one, in_one)
    first_x = x_copies(0, out_x_one, in_x_one)
    begin(first)
    pass_on(first, first_x, part_one, in_one, out_x_one)
    total = plane_total(first, first_x, part_one, in_one, in_x_one)
    z_start(0, total)

    @pl.when(jnp.logical_not(has_next))
    def _():
        xg_next[...] = jnp.zeros_like(xg_next)
        pre[...] = jnp.zeros_like(pre)

    half_blocks = gram_part.shape[0] // 2
    gram_core = core_copies(2, gram_part, gram_in)
    gram_x = x_copies(2, gram_out_x, gram_in_x)
    gram_gather = gather(5, gram_full, strip)
    bc_copies = [
        rcopy(
            gram_full.at[strip],
            gram_full.at[strip],
            bc_send.at[pz],
            bc_recv.at[0],
            dev(layer, x, pz, c),
        )
        for pz in others
    ]

    def gram_begin():
        arrived()
        shape = (half_blocks, gram_part.shape[1], width)
        gram_part[pl.ds(0, half_blocks)] = dot(grad_t[...], xg_ref[1]).reshape(shape)
        gram_part[pl.ds(half_blocks, half_blocks)] = dot(grad_t[...], xg_next[1]).reshape(shape)
        begin(gram_core)

    def gram_pass():
        pass_on(gram_core, gram_x, gram_part, gram_in, gram_out_x)

    def gram_end():
        gram_z_out[...] = plane_total(gram_core, gram_x, gram_part, gram_in, gram_in_x)

    def gram_root():
        total = gram_z_out[...]
        for pz in others:
            z_arrived(2, gram_z_out, gram_z_in, pz)
            total = total + gram_z_in[pz]
        gram_full[strip] = total * scale
        begin(bc_copies)

    def gram_send():
        z_copy(2, gram_z_out, gram_z_in).start()

    def far_start():
        @pl.when(sends_far)
        def _():
            far_own.start()

        @pl.when(relays)
        def _():
            to_relay[0].wait_recv()
            far_relay.start()

    early = jnp.logical_not(late)

    @pl.when(early)
    def _():
        gram_begin()
        gram_pass()

    @pl.when(early & is_rim)
    def _():
        gram_end()

    @pl.when(is_rim & (layer >= NY))
    def _():
        pl.semaphore_wait(go_sem, 1)
        far_start()

    pre_copies = [
        rcopy(
            rows_full,
            pre.at[block],
            pre_send.at[pz],
            pre_recv.at[0],
            dev(layer - 1, x, pz, c),
        )
        for pz in far_first
    ]

    @pl.when(is_root)
    def _():
        root_total(0, full_wide)
        copies = gather(1, full_wide, strip)
        begin(copies)

        @pl.when(layer >= NY)
        def _():
            for pz in others:
                pl.semaphore_signal(
                    go_sem, inc=1, device_id=dev(layer, x, pz, c), device_id_type=MESH
                )
            far_start()

        for q in range(NZ):
            pltpu.make_async_copy(a_ref, a_in.at[q], a_recv.at[q]).wait()
            a_all[pl.ds(q * own_rows, own_rows), :] = a_in[q, :, 0, :]
        rows = a_all[...]
        top = rows.astype(BF16)
        a_two[pl.ds(0, rows.shape[0]), :] = top
        a_two[pl.ds(rows.shape[0], rows.shape[0]), :] = (rows - top.astype(F32)).astype(BF16)
        gathered(1, full_wide, by_strip)
        value = dot(times_inverse(full_wide), ginv_ref[...], precision=HIGH)
        base[...] = value
        rows_full[...] = value.astype(BF16)

        @pl.when(sends_near)
        def _():
            for copy in pre_copies:
                copy.start()

        @pl.when(sends_far)
        def _():
            for copy in reversed(pre_copies):
                copy.start()

        @pl.when(early)
        def _():
            gram_end()

        sent(copies)
        sent(passes(1, full_wide, by_strip))

    @pl.when(late)
    def _():
        gram_begin()

    unfold(xg_next.at[0], patches_next, images, side, width)

    @pl.when(has_next)
    def _():
        rcopy(
            rows_full, pre.at[block], pre_send.at[0], pre_recv.at[0], dev(layer, x, z, other)
        ).wait_recv()
        copies = gather(3, pre, block)
        begin(copies)
        gathered(3, pre, by_block)
        sent(copies)
        sent(passes(3, pre, by_block))

    @pl.when(early & is_rim)
    def _():
        gram_send()

    mapped = dot(patches_next[...], pre[...].reshape(lanes, width)).astype(BF16)
    product = dot(mapped.T, patches[...])
    part[...] = product.reshape(part.shape)
    out_two[...] = product.astype(BF16).reshape(out_two.shape)
    second = core_copies(4, out_two, in_two)
    second_x = x_copies(4, out_x_two, in_x_two)
    begin(second)

    @pl.when(late)
    def _():
        gram_pass()

    pass_on(second, second_x, part, in_two, out_x_two)
    total = plane_total(second, second_x, part, in_two, in_x_two)
    z_start(1, total)

    def gram_back():
        @pl.when(is_root)
        def _():
            gram_root()

        @pl.when(is_rim)
        def _():
            bc_copies[0].wait_recv()

        begin(gram_gather)

    @pl.when(late)
    def _():
        gram_end()

    @pl.when(late & is_rim)
    def _():
        gram_send()

    @pl.when(early)
    def _():
        gram_back()
        gathered(5, gram_full, by_strip)

    @pl.when(late & is_rim)
    def _():
        gram_back()
        gathered(5, gram_full, by_strip)

    @pl.when(is_root)
    def _():
        root_total(1, full)
        copies = gather(6, full, strip)
        begin(copies)

        @pl.when(late)
        def _():
            gram_back()

        gathered(6, full, by_strip)

        @pl.when(late)
        def _():
            gathered(5, gram_full, by_strip)

        cross_gram = gram_full[pl.ds(half_blocks, half_blocks)].reshape(width, width)
        mix = dot(cross_gram, ginv_ref[...], (0, 0), HIGH)
        value = base[...] - dot(times_inverse(full), mix, precision=HIGH)
        result[...] = value
        up_copies = [
            rcopy(
                result_out.at[q],
                result_in,
                up_send.at[q],
                up_recv.at[0],
                dev(layer, x, c * per + q // NC, q % NC),
            )
            for q in range(NZ)
        ]
        own_q = (ROOT - c * per) * NC + c
        for q in sorted(range(NZ), key=lambda q: -abs(q // NC - ROOT % per)):
            result_out[q] = result[pl.ds(q * own_rows, own_rows), :]

            @pl.when(own_q != q)
            def _(copy=up_copies[q]):
                copy.start()

        @pl.when(a_self)
        def _():
            upd_ref[...] = result_out[ROOT % per * NC + ROOT // per]

        for q, copy in enumerate(up_copies):

            @pl.when(own_q != q)
            def _(copy=copy):
                copy.wait_send()

        sent(copies)
        sent(passes(6, full, by_strip))

    gram_ref[...] = gram_full[...].reshape(gram_ref.shape)

    @pl.when(a_other)
    def _():
        rcopy(
            result_out.at[0], result_in, up_send.at[0], up_recv.at[0], dev(layer, x, z, other)
        ).wait_recv()
        upd_ref[...] = result_in[...]

    sent(first)
    sent(first_x)
    sent(second)
    sent(second_x)
    sent(gram_core)
    sent(gram_x)
    sent(gram_gather)
    sent(passes(5, gram_full, by_strip))

    @pl.when(a_other)
    def _():
        a_remote.wait_send()

    @pl.when(sends_near)
    def _():
        shift.wait_send()

    @pl.when(sends_far)
    def _():
        for copy in to_relay:
            copy.wait_send()
        far_own.wait_send()

    @pl.when(relays)
    def _():
        far_relay.wait_send()

    @pl.when(is_rim)
    def _():
        z_copy(0, z_out_wide, z_in_wide).wait_send()
        z_copy(1, z_out, z_in).wait_send()
        z_copy(2, gram_z_out, gram_z_in).wait_send()

    @pl.when(is_root)
    def _():
        for copy in bc_copies:
            copy.wait_send()

    @pl.when(is_root & has_prev)
    def _():
        for copy in pre_copies:
            copy.wait_send()


def per_device(layers, layer_inputs, output_grads, input_inverse, grad_inverse):
    _, images, side, _, width = layer_inputs.shape
    rows = images * side * side
    own_rows = input_inverse.shape[1]
    lanes = TAPS * width
    n = NX * NC
    strip = width // n
    block_rows = lanes // n
    gram_rows = 2 * width // n
    scale = 1.0 / (rows * n * NZ)
    vmem = pltpu.VMEM
    dma = pltpu.SemaphoreType.DMA
    scratch = [
        vmem((2, rows, width), BF16),
        vmem((width, width), F32),
        vmem((rows, lanes), BF16),
        vmem((rows, lanes), BF16),
        vmem((width, rows), BF16),
        vmem((2, rows, width), BF16),
        vmem((2, rows // NY, width), BF16),
        vmem((n, strip, lanes), F32),
        vmem((n, strip, lanes), F32),
        vmem((NX, strip, lanes), F32),
        vmem((NX, strip, lanes), F32),
        vmem((NX, strip, lanes), F32),
        vmem((n, strip, lanes), BF16),
        vmem((NX, strip, lanes), BF16),
        vmem((NX, strip, lanes), BF16),
        vmem((NX, strip, lanes), BF16),
        vmem((strip, lanes), F32),
        vmem((strip, lanes), BF16),
        vmem((NZ, strip, lanes), BF16),
        vmem((strip, lanes), F32),
        vmem((NZ, strip, lanes), F32),
        vmem((n, strip, lanes), F32),
        vmem((n, strip, lanes), F32),
        vmem((NZ, own_rows, 1, lanes), F32),
        vmem((block_rows, lanes), F32),
        vmem((2 * block_rows, lanes), BF16),
        vmem((n, block_rows, width), BF16),
        vmem((block_rows, width), BF16),
        vmem((block_rows, width), F32),
        vmem((block_rows, width), F32),
        vmem((NZ, own_rows, width), F32),
        vmem((own_rows, width), F32),
        vmem((n, gram_rows, width), F32),
        vmem((NX, gram_rows, width), F32),
        vmem((NX, gram_rows, width), F32),
        vmem((NX, gram_rows, width), F32),
        vmem((gram_rows, width), F32),
        vmem((NZ, gram_rows, width), F32),
        vmem((n, gram_rows, width), F32),
        dma((7, n)),
        dma((7, n)),
        dma((3,)),
        dma((3, NZ)),
        dma((1,)),
        dma((NZ,)),
        dma((1,)),
        dma((1,)),
        dma((NY,)),
        dma((1,)),
        dma((NY,)),
        dma((NY,)),
        dma((NZ,)),
        dma((1,)),
        dma((NZ,)),
        dma((1,)),
        dma((NZ,)),
        dma((1,)),
        dma((3,)),
        pltpu.SemaphoreType.REGULAR,
    ]
    whole = pl.BlockSpec(memory_space=pltpu.VMEM)
    update, grams = pl.pallas_call(
        functools.partial(kernel, layers, images, side, scale),
        out_shape=(
            jax.ShapeDtypeStruct((own_rows, width), F32),
            jax.ShapeDtypeStruct((2, width, width), F32),
        ),
        in_specs=[pl.BlockSpec(memory_space=pltpu.HBM)] * 4,
        out_specs=(whole, whole),
        scratch_shapes=scratch,
        compiler_params=pltpu.CompilerParams(
            collective_id=0, has_side_effects=True, vmem_limit_bytes=48 * 1024 * 1024
        ),
        name="kfac_step",
    )(
        *(
            pltpu.with_memory_space_constraint(value, pltpu.HBM)
            for value in (
                layer_inputs.reshape(rows, width),
                output_grads.reshape(rows, width),
                input_inverse.transpose(1, 0, 2),
                grad_inverse.reshape(width, width),
            )
        )
    )
    return update[None], grams[None]


def solution(mesh):
    assert mesh.shape["pos"] == NX * NZ * NC and mesh.shape["layer"] % NY == 0
    return jax.shard_map(
        functools.partial(per_device, mesh.shape["layer"]),
        mesh=mesh,
        in_specs=(
            P("layer", "pos", None, None, None),
            P("layer", "pos", None, None, None),
            P("layer", "pos", None),
            P("layer", None, None),
        ),
        out_specs=(P("layer", "pos", None), P("layer", None, None, None)),
        check_vma=False,
    )
```

```python
import functools

import jax
import jax.numpy as jnp
from jax import lax
from jax.experimental import pallas as pl
from jax.experimental.pallas import tpu as pltpu
from jax.sharding import PartitionSpec as P

NX, NY, NZ, NC = 4, 4, 8, 2
ROOT = 3
TAPS = 9
MESH = pl.DeviceIdType.MESH
F32 = jnp.float32
BF16 = jnp.bfloat16
HIGH = lax.Precision.HIGHEST


def offsets():
    return sorted(range(1, NX), key=lambda d: -min(d, NX - d))


def rcopy(src, dst, send_sem, recv_sem, to):
    return pltpu.make_async_remote_copy(
        src_ref=src,
        dst_ref=dst,
        send_sem=send_sem,
        recv_sem=recv_sem,
        device_id=to,
        device_id_type=MESH,
    )


def dot(a, b, contract=(1, 0), precision=None):
    return lax.dot_general(
        a,
        b,
        (((contract[0],), (contract[1],)), ((), ())),
        precision=precision,
        preferred_element_type=F32,
    )


def unfold(src, dst, images, side, width):
    area = side * side
    rows = images * area
    value = src[...].astype(F32)
    col = lax.rem(lax.broadcasted_iota(jnp.int32, (rows, width), 0), side)
    before = jnp.where(col == 0, 0.0, pltpu.roll(value, 1, 0))
    after = jnp.where(col == side - 1, 0.0, pltpu.roll(value, rows - 1, 0))
    edge = jnp.zeros((side, width), BF16)
    for s, piece in enumerate((before, value, after)):
        piece = piece.astype(BF16)
        for image in range(images):
            top = image * area
            one = piece[top : top + area]
            lanes = pl.ds(s * width, width)
            dst[pl.ds(top, side), lanes] = edge
            dst[pl.ds(top + side, area - side), lanes] = one[: area - side]
            lanes = pl.ds((3 + s) * width, width)
            dst[pl.ds(top, area), lanes] = one
            lanes = pl.ds((6 + s) * width, width)
            dst[pl.ds(top, area - side), lanes] = one[side:]
            dst[pl.ds(top + area - side, side), lanes] = edge


def kernel(
    layers,
    images,
    side,
    scale,
    x_hbm,
    g_hbm,
    a_ref,
    ginv_hbm,
    upd_ref,
    gram_ref,
    xg_ref,
    ginv_ref,
    patches,
    patches_next,
    grad_t,
    xg_next,
    relay,
    part,
    part_one,
    in_one,
    out_x_one,
    in_x_one,
    out_two,
    in_two,
    out_x_two,
    in_x_two,
    plane_sum,
    z_out,
    z_in,
    z_out_wide,
    z_in_wide,
    full,
    full_wide,
    a_in,
    a_all,
    a_two,
    pre,
    rows_full,
    base,
    result,
    result_out,
    result_in,
    gram_part,
    gram_in,
    gram_out_x,
    gram_in_x,
    gram_z_out,
    gram_z_in,
    gram_full,
    ex_send,
    ex_recv,
    z_send,
    z_recv,
    a_send,
    a_recv,
    shift_send,
    shift_recv,
    relay_send,
    relay_recv,
    far_send,
    far_recv,
    pre_send,
    pre_recv,
    bc_send,
    bc_recv,
    up_send,
    up_recv,
    load_sem,
    go_sem,
    ready_sem,
):
    layer = lax.axis_index("layer")
    pos = lax.axis_index("pos")
    c = lax.rem(pos, NC)
    z = lax.rem(lax.div(pos, NC), NZ)
    x = lax.div(pos, NC * NZ)
    block = x * NC + c
    strip = c * NX + x
    n = NX * NC
    _, rows, width = xg_ref.shape
    quarter = rows // NY
    y = lax.rem(layer, NY)
    lanes = TAPS * width
    per = NZ // NC
    own_rows = result_in.shape[0]
    is_root = z == ROOT
    is_rim = z != ROOT
    has_next = layer < layers - 1
    has_prev = layer > 0
    sends_far = has_prev & (y == 0)
    sends_near = has_prev & (y != 0)
    relays = (layer >= NY) & (y != 0)
    late = has_next & (y == NY - 1)

    def dev(lay, px, pz, pc):
        return (lay, (px * NZ + pz) * NC + pc)

    def ahead(dx):
        return lax.rem(x + dx, NX)

    def behind(dx):
        return lax.rem(x + NX - dx, NX)

    other = NC - 1 - c
    far_first = sorted(range(NZ), key=lambda pz: -abs(pz - ROOT))
    others = far_first[:-1]

    loads = [
        pltpu.make_async_copy(src, dst, load_sem.at[i])
        for i, (src, dst) in enumerate(((x_hbm, xg_ref.at[0]), (g_hbm, xg_ref.at[1]), (ginv_hbm, ginv_ref)))
    ]
    for load in loads:
        load.start()

    barrier = pltpu.get_barrier_semaphore()

    def greet(to):
        pl.semaphore_signal(barrier, inc=1, device_id=to, device_id_type=MESH)

    @pl.when(c != 0)
    def _():
        greet(dev(layer, x, z, 0))

    for dx in offsets():
        greet(dev(layer, ahead(dx), z, 0))

    @pl.when(is_rim)
    def _():
        greet(dev(layer, x, ROOT, 0))

    @pl.when(is_root)
    def _():
        for pz in others:
            greet(dev(layer, x, pz, 0))

    @pl.when(has_next)
    def _():
        greet(dev(layer + 1, x, z, 1))

    @pl.when(has_next & is_rim)
    def _():
        greet(dev(layer + 1, x, ROOT, 1))

    @pl.when(relays)
    def _():
        greet(dev(layer - y, x, z, 1))

    @pl.when(late)
    def _():
        for q in range(1, NY):
            greet(dev(layer + 1 + q, x, z, 1))

    for load in loads:
        load.wait()
    unfold(xg_ref.at[0], patches, images, side, width)
    grad_t[...] = xg_ref[1].T

    root = is_root.astype(jnp.int32)
    chips = 1 + root * (NZ - 2)
    near_greets = 1 + NC * (NX - 1 + chips)
    chips = 1 + root * (NZ - 1) + sends_far.astype(jnp.int32) * (NY - 1) + relays.astype(jnp.int32)
    far_greets = NC * chips

    @pl.when(c == 0)
    def _():
        pl.semaphore_wait(barrier, near_greets)
        pl.semaphore_signal(
            ready_sem, inc=1, device_id=dev(layer, x, z, other), device_id_type=MESH
        )

    @pl.when(c != 0)
    def _():
        pl.semaphore_wait(ready_sem, 1)

    shift = rcopy(xg_ref, xg_next, shift_send.at[0], shift_recv.at[0], dev(layer - 1, x, z, c))

    def piece(ref, q):
        return ref.at[:, pl.ds(pl.multiple_of(q * quarter, quarter), quarter)]

    to_relay = [
        rcopy(
            piece(xg_ref, q),
            relay,
            relay_send.at[q],
            relay_recv.at[0],
            dev(layer + q, x, z, c),
        )
        for q in range(1, NY)
    ]
    far_own = rcopy(
        piece(xg_ref, 0), piece(xg_next, 0), far_send.at[0], far_recv.at[0], dev(layer - 1, x, z, c)
    )
    far_relay = rcopy(
        relay, piece(xg_next, y), far_send.at[0], far_recv.at[y], dev(layer - y - 1, x, z, c)
    )

    def arrived():
        @pl.when(has_next & jnp.logical_not(late))
        def _():
            shift.wait_recv()

        @pl.when(late)
        def _():
            for q in range(NY):
                rcopy(
                    relay, piece(xg_next, q), far_send.at[0], far_recv.at[q], dev(layer, x, z, other)
                ).wait_recv()

    half = lax.div(z, per)
    slot = lax.rem(z, per) * NC + c
    a_self = is_root & (half == c)
    a_other = jnp.logical_not(a_self)
    a_remote = rcopy(a_ref, a_in.at[slot], a_send.at[0], a_recv.at[slot], dev(layer, x, ROOT, half))
    a_local = pltpu.make_async_copy(a_ref, a_in.at[slot], a_recv.at[slot])

    @pl.when(a_other)
    def _():
        a_remote.start()

    @pl.when(a_self)
    def _():
        a_local.start()

    def sent(copies):
        for copy in copies:
            copy.wait_send()

    def begin(copies):
        for copy in copies:
            copy.start()

    def core_copies(kind, out, in_core):
        return [
            rcopy(
                out.at[other * NX + ahead(dx)],
                in_core.at[dx],
                ex_send.at[kind, dx],
                ex_recv.at[kind, dx],
                dev(layer, x, z, other),
            )
            for dx in offsets() + [0]
        ]

    def x_copies(kind, out_x, in_x):
        return [
            rcopy(
                out_x.at[dx],
                in_x.at[dx],
                ex_send.at[kind, NX + dx],
                ex_recv.at[kind, NX + dx],
                dev(layer, ahead(dx), z, c),
            )
            for dx in offsets()
        ]

    def pass_on(core, along, part, in_core, out_x):
        for dx, arrival, copy in zip(offsets(), core, along):
            arrival.wait_recv()
            out_x[dx] = (part[c * NX + ahead(dx)] + in_core[dx].astype(F32)).astype(out_x.dtype)
            copy.start()

    def plane_total(core, along, part, in_core, in_x):
        core[-1].wait_recv()
        total = part[strip] + in_core[0].astype(F32)
        for dx, copy in reversed(list(zip(offsets(), along))):
            copy.wait_recv()
            total = total + in_x[dx].astype(F32)
        return total

    def gather(kind, buf, own):
        targets = [(dx, dev(layer, ahead(dx), z, c)) for dx in offsets()]
        return [
            rcopy(buf.at[own], buf.at[own], ex_send.at[kind, dx], ex_recv.at[kind, dx], to)
            for dx, to in targets + [(0, dev(layer, x, z, other))]
        ]

    def passes(kind, buf, place):
        copies = []
        for dx in reversed(offsets()):
            got = buf.at[place(behind(dx), c)]
            s = NX + dx
            copies.append(
                rcopy(got, got, ex_send.at[kind, s], ex_recv.at[kind, s], dev(layer, x, z, other))
            )
        return copies

    def arrival(kind, s, got):
        rcopy(
            got, got, ex_send.at[kind, s], ex_recv.at[kind, s], dev(layer, x, z, other)
        ).wait_recv()

    def gathered(kind, buf, place):
        for dx, copy in zip(reversed(offsets()), passes(kind, buf, place)):
            arrival(kind, dx, buf.at[place(behind(dx), c)])
            copy.start()
        arrival(kind, 0, buf.at[place(x, other)])
        for dx in reversed(offsets()):
            arrival(kind, NX + dx, buf.at[place(behind(dx), other)])

    def by_strip(px, pc):
        return pc * NX + px

    def by_block(px, pc):
        return px * NC + pc

    def z_copy(kind, src, dst):
        return rcopy(
            src, dst.at[z], z_send.at[kind], z_recv.at[kind, z], dev(layer, x, ROOT, c)
        )

    def z_arrived(kind, src, dst, pz):
        rcopy(
            src, dst.at[pz], z_send.at[kind], z_recv.at[kind, pz], dev(layer, x, ROOT, c)
        ).wait_recv()

    z_bufs = ((z_out_wide, z_in_wide), (z_out, z_in))

    def z_start(z_slot, total):
        plane_sum[...] = total
        src, dst = z_bufs[z_slot]

        @pl.when(is_rim)
        def _():
            src[...] = total.astype(src.dtype)
            z_copy(z_slot, src, dst).start()

    def root_total(z_slot, buf):
        total = plane_sum[...]
        src, dst = z_bufs[z_slot]
        for pz in others:
            z_arrived(z_slot, src, dst, pz)
            total = total + dst[pz].astype(F32)
        buf[strip] = total * scale

    def fold(both):
        half_rows = both.shape[0] // 2
        return both[:half_rows] + both[half_rows:]

    def times_inverse(buf):
        value = buf[...].reshape(width, lanes)
        top = value.astype(BF16)
        low = (value - top.astype(F32)).astype(BF16)
        both = dot(a_two[...], jnp.concatenate([top, low], axis=0), (1, 1))
        return fold(both[:, :width] + both[:, width:])

    part_one[...] = dot(grad_t[...], patches[...]).reshape(part_one.shape)
    first = core_copies(0, part_one, in_one)
    first_x = x_copies(0, out_x_one, in_x_one)
    begin(first)
    pass_on(first, first_x, part_one, in_one, out_x_one)

    @pl.when(has_prev & (c != 0))
    def _():
        pl.semaphore_wait(barrier, far_greets)
        pl.semaphore_signal(
            ready_sem, inc=1, device_id=dev(layer, x, z, other), device_id_type=MESH
        )

    @pl.when(has_prev & (c == 0))
    def _():
        pl.semaphore_wait(ready_sem, 1)

    @pl.when(sends_near)
    def _():
        shift.start()

    @pl.when(sends_far)
    def _():
        for copy in to_relay:
            copy.start()

    total = plane_total(first, first_x, part_one, in_one, in_x_one)
    z_start(0, total)

    @pl.when(jnp.logical_not(has_next))
    def _():
        xg_next[...] = jnp.zeros_like(xg_next)
        pre[...] = jnp.zeros_like(pre)

    half_blocks = gram_part.shape[0] // 2
    gram_core = core_copies(2, gram_part, gram_in)
    gram_x = x_copies(2, gram_out_x, gram_in_x)
    gram_gather = gather(5, gram_full, strip)
    bc_copies = [
        rcopy(
            gram_full.at[strip],
            gram_full.at[strip],
            bc_send.at[pz],
            bc_recv.at[0],
            dev(layer, x, pz, c),
        )
        for pz in others
    ]

    def gram_begin():
        arrived()
        shape = (half_blocks, gram_part.shape[1], width)
        gram_part[pl.ds(0, half_blocks)] = dot(grad_t[...], xg_ref[1]).reshape(shape)
        gram_part[pl.ds(half_blocks, half_blocks)] = dot(grad_t[...], xg_next[1]).reshape(shape)
        begin(gram_core)

    def gram_pass():
        pass_on(gram_core, gram_x, gram_part, gram_in, gram_out_x)

    def gram_end():
        gram_z_out[...] = plane_total(gram_core, gram_x, gram_part, gram_in, gram_in_x)

    def gram_root():
        total = gram_z_out[...]
        for pz in others:
            z_arrived(2, gram_z_out, gram_z_in, pz)
            total = total + gram_z_in[pz]
        gram_full[strip] = total * scale
        begin(bc_copies)

    def gram_send():
        z_copy(2, gram_z_out, gram_z_in).start()

    def far_start():
        @pl.when(sends_far)
        def _():
            far_own.start()

        @pl.when(relays)
        def _():
            to_relay[0].wait_recv()
            far_relay.start()

    early = jnp.logical_not(late)

    @pl.when(early)
    def _():
        gram_begin()
        gram_pass()

    @pl.when(early & is_rim)
    def _():
        gram_end()

    @pl.when(is_rim & (layer >= NY))
    def _():
        pl.semaphore_wait(go_sem, 1)
        far_start()

    pre_copies = [
        rcopy(
            rows_full,
            pre.at[block],
            pre_send.at[pz],
            pre_recv.at[0],
            dev(layer - 1, x, pz, c),
        )
        for pz in far_first
    ]

    @pl.when(is_root)
    def _():
        root_total(0, full_wide)
        begin(gather(1, full_wide, strip))

        @pl.when(layer >= NY)
        def _():
            for pz in others:
                pl.semaphore_signal(
                    go_sem, inc=1, device_id=dev(layer, x, pz, c), device_id_type=MESH
                )
            far_start()

        for q in range(NZ):
            pltpu.make_async_copy(a_ref, a_in.at[q], a_recv.at[q]).wait()
            a_all[pl.ds(q * own_rows, own_rows), :] = a_in[q, :, 0, :]
        rows = a_all[...]
        top = rows.astype(BF16)
        a_two[pl.ds(0, rows.shape[0]), :] = top
        a_two[pl.ds(rows.shape[0], rows.shape[0]), :] = (rows - top.astype(F32)).astype(BF16)
        gathered(1, full_wide, by_strip)
        value = dot(times_inverse(full_wide), ginv_ref[...], precision=HIGH)
        base[...] = value
        rows_full[...] = value.astype(BF16)

        @pl.when(sends_near)
        def _():
            for copy in pre_copies:
                copy.start()

        @pl.when(sends_far)
        def _():
            for copy in reversed(pre_copies):
                copy.start()

        @pl.when(early)
        def _():
            gram_end()


    @pl.when(late)
    def _():
        gram_begin()

    unfold(xg_next.at[0], patches_next, images, side, width)

    @pl.when(has_next)
    def _():
        rcopy(
            rows_full, pre.at[block], pre_send.at[0], pre_recv.at[0], dev(layer, x, z, other)
        ).wait_recv()
        begin(gather(3, pre, block))
        gathered(3, pre, by_block)

    @pl.when(early & is_rim)
    def _():
        gram_send()

    mapped = dot(patches_next[...], pre[...].reshape(lanes, width)).astype(BF16)
    product = dot(mapped.T, patches[...])
    part[...] = product.reshape(part.shape)
    out_two[...] = product.astype(BF16).reshape(out_two.shape)
    second = core_copies(4, out_two, in_two)
    second_x = x_copies(4, out_x_two, in_x_two)
    begin(second)

    @pl.when(late)
    def _():
        gram_pass()

    pass_on(second, second_x, part, in_two, out_x_two)
    total = plane_total(second, second_x, part, in_two, in_x_two)
    z_start(1, total)

    def gram_back():
        @pl.when(is_root)
        def _():
            gram_root()

        @pl.when(is_rim)
        def _():
            bc_copies[0].wait_recv()

        begin(gram_gather)

    @pl.when(late)
    def _():
        gram_end()

    @pl.when(late & is_rim)
    def _():
        gram_send()

    @pl.when(early)
    def _():
        gram_back()
        gathered(5, gram_full, by_strip)

    @pl.when(late & is_rim)
    def _():
        gram_back()
        gathered(5, gram_full, by_strip)

    up_copies = [
        rcopy(
            result_out.at[q],
            result_in,
            up_send.at[q],
            up_recv.at[0],
            dev(layer, x, c * per + q // NC, q % NC),
        )
        for q in range(NZ)
    ]
    own_q = (ROOT - c * per) * NC + c

    @pl.when(is_root)
    def _():
        root_total(1, full)
        begin(gather(6, full, strip))

        @pl.when(late)
        def _():
            gram_back()

        gathered(6, full, by_strip)

        @pl.when(late)
        def _():
            gathered(5, gram_full, by_strip)

        cross_gram = gram_full[pl.ds(half_blocks, half_blocks)].reshape(width, width)
        mix = dot(cross_gram, ginv_ref[...], (0, 0), HIGH)
        value = base[...] - dot(times_inverse(full), mix, precision=HIGH)
        result[...] = value
        for q in sorted(range(NZ), key=lambda q: -abs(q // NC - ROOT % per)):
            result_out[q] = result[pl.ds(q * own_rows, own_rows), :]

            @pl.when(own_q != q)
            def _(copy=up_copies[q]):
                copy.start()

        @pl.when(a_self)
        def _():
            upd_ref[...] = result_out[ROOT % per * NC + ROOT // per]

    gram_ref[...] = gram_full[...].reshape(gram_ref.shape)

    @pl.when(a_other)
    def _():
        rcopy(
            result_out.at[0], result_in, up_send.at[0], up_recv.at[0], dev(layer, x, z, other)
        ).wait_recv()
        upd_ref[...] = result_in[...]

    sent(first)
    sent(first_x)
    sent(second)
    sent(second_x)
    sent(gram_core)
    sent(gram_x)
    sent(gram_gather)
    sent(passes(5, gram_full, by_strip))

    @pl.when(a_other)
    def _():
        a_remote.wait_send()

    @pl.when(sends_near)
    def _():
        shift.wait_send()

    @pl.when(sends_far)
    def _():
        for copy in to_relay:
            copy.wait_send()
        far_own.wait_send()

    @pl.when(relays)
    def _():
        far_relay.wait_send()

    @pl.when(is_rim)
    def _():
        z_copy(0, z_out_wide, z_in_wide).wait_send()
        z_copy(1, z_out, z_in).wait_send()
        z_copy(2, gram_z_out, gram_z_in).wait_send()

    @pl.when(is_root)
    def _():
        sent(bc_copies)
        for kind, buf in ((1, full_wide), (6, full)):
            sent(gather(kind, buf, strip))
            sent(passes(kind, buf, by_strip))
        for q, copy in enumerate(up_copies):

            @pl.when(own_q != q)
            def _(copy=copy):
                copy.wait_send()

    @pl.when(has_next)
    def _():
        sent(gather(3, pre, block))
        sent(passes(3, pre, by_block))

    @pl.when(is_root & has_prev)
    def _():
        for copy in pre_copies:
            copy.wait_send()


def per_device(layers, layer_inputs, output_grads, input_inverse, grad_inverse):
    _, images, side, _, width = layer_inputs.shape
    rows = images * side * side
    own_rows = input_inverse.shape[1]
    lanes = TAPS * width
    n = NX * NC
    strip = width // n
    block_rows = lanes // n
    gram_rows = 2 * width // n
    scale = 1.0 / (rows * n * NZ)
    vmem = pltpu.VMEM
    dma = pltpu.SemaphoreType.DMA
    scratch = [
        vmem((2, rows, width), BF16),
        vmem((width, width), F32),
        vmem((rows, lanes), BF16),
        vmem((rows, lanes), BF16),
        vmem((width, rows), BF16),
        vmem((2, rows, width), BF16),
        vmem((2, rows // NY, width), BF16),
        vmem((n, strip, lanes), F32),
        vmem((n, strip, lanes), F32),
        vmem((NX, strip, lanes), F32),
        vmem((NX, strip, lanes), F32),
        vmem((NX, strip, lanes), F32),
        vmem((n, strip, lanes), BF16),
        vmem((NX, strip, lanes), BF16),
        vmem((NX, strip, lanes), BF16),
        vmem((NX, strip, lanes), BF16),
        vmem((strip, lanes), F32),
        vmem((strip, lanes), BF16),
        vmem((NZ, strip, lanes), BF16),
        vmem((strip, lanes), F32),
        vmem((NZ, strip, lanes), F32),
        vmem((n, strip, lanes), F32),
        vmem((n, strip, lanes), F32),
        vmem((NZ, own_rows, 1, lanes), F32),
        vmem((block_rows, lanes), F32),
        vmem((2 * block_rows, lanes), BF16),
        vmem((n, block_rows, width), BF16),
        vmem((block_rows, width), BF16),
        vmem((block_rows, width), F32),
        vmem((block_rows, width), F32),
        vmem((NZ, own_rows, width), F32),
        vmem((own_rows, width), F32),
        vmem((n, gram_rows, width), F32),
        vmem((NX, gram_rows, width), F32),
        vmem((NX, gram_rows, width), F32),
        vmem((NX, gram_rows, width), F32),
        vmem((gram_rows, width), F32),
        vmem((NZ, gram_rows, width), F32),
        vmem((n, gram_rows, width), F32),
        dma((7, n)),
        dma((7, n)),
        dma((3,)),
        dma((3, NZ)),
        dma((1,)),
        dma((NZ,)),
        dma((1,)),
        dma((1,)),
        dma((NY,)),
        dma((1,)),
        dma((NY,)),
        dma((NY,)),
        dma((NZ,)),
        dma((1,)),
        dma((NZ,)),
        dma((1,)),
        dma((NZ,)),
        dma((1,)),
        dma((3,)),
        pltpu.SemaphoreType.REGULAR,
        pltpu.SemaphoreType.REGULAR,
    ]
    whole = pl.BlockSpec(memory_space=pltpu.VMEM)
    update, grams = pl.pallas_call(
        functools.partial(kernel, layers, images, side, scale),
        out_shape=(
            jax.ShapeDtypeStruct((own_rows, width), F32),
            jax.ShapeDtypeStruct((2, width, width), F32),
        ),
        in_specs=[pl.BlockSpec(memory_space=pltpu.HBM)] * 4,
        out_specs=(whole, whole),
        scratch_shapes=scratch,
        compiler_params=pltpu.CompilerParams(
            collective_id=0, has_side_effects=True, vmem_limit_bytes=48 * 1024 * 1024
        ),
        name="kfac_step",
    )(
        *(
            pltpu.with_memory_space_constraint(value, pltpu.HBM)
            for value in (
                layer_inputs.reshape(rows, width),
                output_grads.reshape(rows, width),
                input_inverse.transpose(1, 0, 2),
                grad_inverse.reshape(width, width),
            )
        )
    )
    return update[None], grams[None]


def solution(mesh):
    assert mesh.shape["pos"] == NX * NZ * NC and mesh.shape["layer"] % NY == 0
    return jax.shard_map(
        functools.partial(per_device, mesh.shape["layer"]),
        mesh=mesh,
        in_specs=(
            P("layer", "pos", None, None, None),
            P("layer", "pos", None, None, None),
            P("layer", "pos", None),
            P("layer", None, None),
        ),
        out_specs=(P("layer", "pos", None), P("layer", None, None, None)),
        check_vma=False,
    )
```

```python
import functools

import jax
import jax.numpy as jnp
from jax import lax
from jax.experimental import pallas as pl
from jax.experimental.pallas import tpu as pltpu
from jax.sharding import PartitionSpec as P

NX, NY, NZ, NC = 4, 4, 8, 2
ROOT = 3
TAPS = 9
MESH = pl.DeviceIdType.MESH
F32 = jnp.float32
BF16 = jnp.bfloat16
HIGH = lax.Precision.HIGHEST


def offsets():
    return sorted(range(1, NX), key=lambda d: -min(d, NX - d))


def rcopy(src, dst, send_sem, recv_sem, to):
    return pltpu.make_async_remote_copy(
        src_ref=src,
        dst_ref=dst,
        send_sem=send_sem,
        recv_sem=recv_sem,
        device_id=to,
        device_id_type=MESH,
    )


def part_of(rows, q):
    size = -(-rows // (NY - 1) // 16) * 16
    start = (q - 1) * size
    return start, min(size, rows - start)


def dot(a, b, contract=(1, 0), precision=None):
    return lax.dot_general(
        a,
        b,
        (((contract[0],), (contract[1],)), ((), ())),
        precision=precision,
        preferred_element_type=F32,
    )


def unfold(src, dst, images, side, width):
    area = side * side
    rows = images * area
    value = src[...].astype(F32)
    col = lax.rem(lax.broadcasted_iota(jnp.int32, (rows, width), 0), side)
    before = jnp.where(col == 0, 0.0, pltpu.roll(value, 1, 0))
    after = jnp.where(col == side - 1, 0.0, pltpu.roll(value, rows - 1, 0))
    edge = jnp.zeros((side, width), BF16)
    for s, piece in enumerate((before, value, after)):
        piece = piece.astype(BF16)
        for image in range(images):
            top = image * area
            one = piece[top : top + area]
            lanes = pl.ds(s * width, width)
            dst[pl.ds(top, side), lanes] = edge
            dst[pl.ds(top + side, area - side), lanes] = one[: area - side]
            lanes = pl.ds((3 + s) * width, width)
            dst[pl.ds(top, area), lanes] = one
            lanes = pl.ds((6 + s) * width, width)
            dst[pl.ds(top, area - side), lanes] = one[side:]
            dst[pl.ds(top + area - side, side), lanes] = edge


def kernel(
    layers,
    images,
    side,
    scale,
    x_hbm,
    g_hbm,
    a_ref,
    ginv_hbm,
    upd_ref,
    gram_ref,
    xg_ref,
    ginv_ref,
    patches,
    patches_next,
    grad_t,
    xg_next,
    relay,
    part,
    part_one,
    in_one,
    out_x_one,
    in_x_one,
    out_two,
    in_two,
    out_x_two,
    in_x_two,
    plane_sum,
    z_out,
    z_in,
    z_out_wide,
    z_in_wide,
    full,
    full_wide,
    a_in,
    a_all,
    a_two,
    pre,
    rows_full,
    base,
    result,
    result_out,
    result_in,
    gram_part,
    gram_in,
    gram_out_x,
    gram_in_x,
    gram_z_out,
    gram_z_in,
    gram_full,
    ex_send,
    ex_recv,
    z_send,
    z_recv,
    a_send,
    a_recv,
    shift_send,
    shift_recv,
    relay_send,
    relay_recv,
    far_send,
    far_recv,
    pre_send,
    pre_recv,
    bc_send,
    bc_recv,
    up_send,
    up_recv,
    load_sem,
    ready_sem,
):
    layer = lax.axis_index("layer")
    pos = lax.axis_index("pos")
    c = lax.rem(pos, NC)
    z = lax.rem(lax.div(pos, NC), NZ)
    x = lax.div(pos, NC * NZ)
    block = x * NC + c
    strip = c * NX + x
    n = NX * NC
    _, rows, width = xg_ref.shape
    y = lax.rem(layer, NY)
    lanes = TAPS * width
    per = NZ // NC
    own_rows = result_in.shape[0]
    is_root = z == ROOT
    is_rim = z != ROOT
    has_next = layer < layers - 1
    has_prev = layer > 0
    sends_far = has_prev & (y == 0)
    sends_near = has_prev & (y != 0)
    relays = (layer >= NY) & (y != 0)
    late = has_next & (y == NY - 1)

    def dev(lay, px, pz, pc):
        return (lay, (px * NZ + pz) * NC + pc)

    def ahead(dx):
        return lax.rem(x + dx, NX)

    def behind(dx):
        return lax.rem(x + NX - dx, NX)

    other = NC - 1 - c
    far_first = sorted(range(NZ), key=lambda pz: -abs(pz - ROOT))
    others = far_first[:-1]

    loads = [
        pltpu.make_async_copy(src, dst, load_sem.at[i])
        for i, (src, dst) in enumerate(((x_hbm, xg_ref.at[0]), (g_hbm, xg_ref.at[1]), (ginv_hbm, ginv_ref)))
    ]
    for load in loads:
        load.start()

    barrier = pltpu.get_barrier_semaphore()

    def greet(to):
        pl.semaphore_signal(barrier, inc=1, device_id=to, device_id_type=MESH)

    @pl.when(c != 0)
    def _():
        greet(dev(layer, x, z, 0))

    for dx in offsets():
        greet(dev(layer, ahead(dx), z, 0))

    @pl.when(is_rim)
    def _():
        greet(dev(layer, x, ROOT, 0))

    @pl.when(is_root)
    def _():
        for pz in others:
            greet(dev(layer, x, pz, 0))

    @pl.when(has_next)
    def _():
        greet(dev(layer + 1, x, z, 1))

    @pl.when(has_next & is_rim)
    def _():
        greet(dev(layer + 1, x, ROOT, 1))

    @pl.when(relays)
    def _():
        greet(dev(layer - y, x, z, 1))

    @pl.when(late)
    def _():
        for q in range(1, NY):
            greet(dev(layer + 1 + q, x, z, 1))

    for load in loads:
        load.wait()
    unfold(xg_ref.at[0], patches, images, side, width)
    grad_t[...] = xg_ref[1].T

    root = is_root.astype(jnp.int32)
    chips = 1 + root * (NZ - 2)
    near_greets = 1 + NC * (NX - 1 + chips)
    chips = 1 + root * (NZ - 1) + sends_far.astype(jnp.int32) * (NY - 1) + relays.astype(jnp.int32)
    far_greets = NC * chips

    @pl.when(c == 0)
    def _():
        pl.semaphore_wait(barrier, near_greets)
        pl.semaphore_signal(
            ready_sem, inc=1, device_id=dev(layer, x, z, other), device_id_type=MESH
        )

    @pl.when(c != 0)
    def _():
        pl.semaphore_wait(ready_sem, 1)

    shift = rcopy(xg_ref, xg_next, shift_send.at[0], shift_recv.at[0], dev(layer - 1, x, z, c))
    hops = range(1, NY)

    def piece(ref, q):
        start, size = part_of(rows, q)
        return ref.at[:, pl.ds(start, size)]

    def held(q):
        return relay.at[:, pl.ds(0, part_of(rows, q)[1])]

    to_relay = [
        rcopy(
            piece(xg_ref, q), held(q), relay_send.at[q], relay_recv.at[0], dev(layer + q, x, z, c)
        )
        for q in hops
    ]
    far_relay = [
        rcopy(
            held(q), piece(xg_next, q), far_send.at[0], far_recv.at[q], dev(layer - q - 1, x, z, c)
        )
        for q in hops
    ]

    def arrived():
        @pl.when(has_next & jnp.logical_not(late))
        def _():
            shift.wait_recv()

        @pl.when(late)
        def _():
            for copy in far_relay:
                copy.wait_recv()

    half = lax.div(z, per)
    slot = lax.rem(z, per) * NC + c
    a_self = is_root & (half == c)
    a_other = jnp.logical_not(a_self)
    a_remote = rcopy(a_ref, a_in.at[slot], a_send.at[0], a_recv.at[slot], dev(layer, x, ROOT, half))
    a_local = pltpu.make_async_copy(a_ref, a_in.at[slot], a_recv.at[slot])

    @pl.when(a_other)
    def _():
        a_remote.start()

    @pl.when(a_self)
    def _():
        a_local.start()

    def sent(copies):
        for copy in copies:
            copy.wait_send()

    def begin(copies):
        for copy in copies:
            copy.start()

    def core_copies(kind, out, in_core):
        return [
            rcopy(
                out.at[other * NX + ahead(dx)],
                in_core.at[dx],
                ex_send.at[kind, dx],
                ex_recv.at[kind, dx],
                dev(layer, x, z, other),
            )
            for dx in offsets() + [0]
        ]

    def x_copies(kind, out_x, in_x):
        return [
            rcopy(
                out_x.at[dx],
                in_x.at[dx],
                ex_send.at[kind, NX + dx],
                ex_recv.at[kind, NX + dx],
                dev(layer, ahead(dx), z, c),
            )
            for dx in offsets()
        ]

    def pass_on(core, along, part, in_core, out_x):
        for dx, arrival, copy in zip(offsets(), core, along):
            arrival.wait_recv()
            out_x[dx] = (part[c * NX + ahead(dx)] + in_core[dx].astype(F32)).astype(out_x.dtype)
            copy.start()

    def plane_total(core, along, part, in_core, in_x):
        core[-1].wait_recv()
        total = part[strip] + in_core[0].astype(F32)
        for dx, copy in reversed(list(zip(offsets(), along))):
            copy.wait_recv()
            total = total + in_x[dx].astype(F32)
        return total

    def gather(kind, buf, own):
        targets = [(dx, dev(layer, ahead(dx), z, c)) for dx in offsets()]
        return [
            rcopy(buf.at[own], buf.at[own], ex_send.at[kind, dx], ex_recv.at[kind, dx], to)
            for dx, to in targets + [(0, dev(layer, x, z, other))]
        ]

    def passes(kind, buf, place):
        copies = []
        for dx in reversed(offsets()):
            got = buf.at[place(behind(dx), c)]
            s = NX + dx
            copies.append(
                rcopy(got, got, ex_send.at[kind, s], ex_recv.at[kind, s], dev(layer, x, z, other))
            )
        return copies

    def arrival(kind, s, got):
        rcopy(
            got, got, ex_send.at[kind, s], ex_recv.at[kind, s], dev(layer, x, z, other)
        ).wait_recv()

    def gathered(kind, buf, place):
        for dx, copy in zip(reversed(offsets()), passes(kind, buf, place)):
            arrival(kind, dx, buf.at[place(behind(dx), c)])
            copy.start()
        arrival(kind, 0, buf.at[place(x, other)])
        for dx in reversed(offsets()):
            arrival(kind, NX + dx, buf.at[place(behind(dx), other)])

    def by_strip(px, pc):
        return pc * NX + px

    def by_block(px, pc):
        return px * NC + pc

    def z_copy(kind, src, dst):
        return rcopy(
            src, dst.at[z], z_send.at[kind], z_recv.at[kind, z], dev(layer, x, ROOT, c)
        )

    def z_arrived(kind, src, dst, pz):
        rcopy(
            src, dst.at[pz], z_send.at[kind], z_recv.at[kind, pz], dev(layer, x, ROOT, c)
        ).wait_recv()

    z_bufs = ((z_out_wide, z_in_wide), (z_out, z_in))

    def z_start(z_slot, total):
        plane_sum[...] = total
        src, dst = z_bufs[z_slot]

        @pl.when(is_rim)
        def _():
            src[...] = total.astype(src.dtype)
            z_copy(z_slot, src, dst).start()

    def root_total(z_slot, buf):
        total = plane_sum[...]
        src, dst = z_bufs[z_slot]
        for pz in others:
            z_arrived(z_slot, src, dst, pz)
            total = total + dst[pz].astype(F32)
        buf[strip] = total * scale

    def fold(both):
        half_rows = both.shape[0] // 2
        return both[:half_rows] + both[half_rows:]

    def times_inverse(buf):
        value = buf[...].reshape(width, lanes)
        top = value.astype(BF16)
        low = (value - top.astype(F32)).astype(BF16)
        both = dot(a_two[...], jnp.concatenate([top, low], axis=0), (1, 1))
        return fold(both[:, :width] + both[:, width:])

    part_one[...] = dot(grad_t[...], patches[...]).reshape(part_one.shape)
    first = core_copies(0, part_one, in_one)
    first_x = x_copies(0, out_x_one, in_x_one)
    begin(first)
    pass_on(first, first_x, part_one, in_one, out_x_one)

    @pl.when(has_prev & (c != 0))
    def _():
        pl.semaphore_wait(barrier, far_greets)
        pl.semaphore_signal(
            ready_sem, inc=1, device_id=dev(layer, x, z, other), device_id_type=MESH
        )

    @pl.when(has_prev & (c == 0))
    def _():
        pl.semaphore_wait(ready_sem, 1)

    @pl.when(sends_near)
    def _():
        shift.start()

    @pl.when(sends_far)
    def _():
        for copy in to_relay:
            copy.start()

    total = plane_total(first, first_x, part_one, in_one, in_x_one)
    z_start(0, total)

    for q in hops:

        @pl.when(relays & (y == q))
        def _(q=q):
            to_relay[q - 1].wait_recv()
            far_relay[q - 1].start()


    @pl.when(jnp.logical_not(has_next))
    def _():
        xg_next[...] = jnp.zeros_like(xg_next)
        pre[...] = jnp.zeros_like(pre)

    half_blocks = gram_part.shape[0] // 2
    gram_core = core_copies(2, gram_part, gram_in)
    gram_x = x_copies(2, gram_out_x, gram_in_x)
    gram_gather = gather(5, gram_full, strip)
    bc_copies = [
        rcopy(
            gram_full.at[strip],
            gram_full.at[strip],
            bc_send.at[pz],
            bc_recv.at[0],
            dev(layer, x, pz, c),
        )
        for pz in others
    ]

    def gram_begin():
        arrived()
        shape = (half_blocks, gram_part.shape[1], width)
        gram_part[pl.ds(0, half_blocks)] = dot(grad_t[...], xg_ref[1]).reshape(shape)
        gram_part[pl.ds(half_blocks, half_blocks)] = dot(grad_t[...], xg_next[1]).reshape(shape)
        begin(gram_core)

    def gram_pass():
        pass_on(gram_core, gram_x, gram_part, gram_in, gram_out_x)

    def gram_end():
        gram_z_out[...] = plane_total(gram_core, gram_x, gram_part, gram_in, gram_in_x)

    def gram_root():
        total = gram_z_out[...]
        for pz in others:
            z_arrived(2, gram_z_out, gram_z_in, pz)
            total = total + gram_z_in[pz]
        gram_full[strip] = total * scale
        begin(bc_copies)

    def gram_send():
        z_copy(2, gram_z_out, gram_z_in).start()

    early = jnp.logical_not(late)

    @pl.when(early)
    def _():
        gram_begin()
        gram_pass()

    @pl.when(early & is_rim)
    def _():
        gram_end()

    pre_copies = [
        rcopy(
            rows_full,
            pre.at[block],
            pre_send.at[pz],
            pre_recv.at[0],
            dev(layer - 1, x, pz, c),
        )
        for pz in far_first
    ]

    @pl.when(is_root)
    def _():
        root_total(0, full_wide)
        begin(gather(1, full_wide, strip))

        for q in range(NZ):
            pltpu.make_async_copy(a_ref, a_in.at[q], a_recv.at[q]).wait()
            a_all[pl.ds(q * own_rows, own_rows), :] = a_in[q, :, 0, :]
        rows = a_all[...]
        top = rows.astype(BF16)
        a_two[pl.ds(0, rows.shape[0]), :] = top
        a_two[pl.ds(rows.shape[0], rows.shape[0]), :] = (rows - top.astype(F32)).astype(BF16)
        gathered(1, full_wide, by_strip)
        value = dot(times_inverse(full_wide), ginv_ref[...], precision=HIGH)
        base[...] = value
        rows_full[...] = value.astype(BF16)

        @pl.when(sends_near)
        def _():
            for copy in pre_copies:
                copy.start()

        @pl.when(sends_far)
        def _():
            for copy in reversed(pre_copies):
                copy.start()

        @pl.when(early)
        def _():
            gram_end()


    @pl.when(late)
    def _():
        gram_begin()

    unfold(xg_next.at[0], patches_next, images, side, width)

    @pl.when(has_next)
    def _():
        rcopy(
            rows_full, pre.at[block], pre_send.at[0], pre_recv.at[0], dev(layer, x, z, other)
        ).wait_recv()
        begin(gather(3, pre, block))
        gathered(3, pre, by_block)

    @pl.when(early & is_rim)
    def _():
        gram_send()

    mapped = dot(patches_next[...], pre[...].reshape(lanes, width)).astype(BF16)
    product = dot(mapped.T, patches[...])
    part[...] = product.reshape(part.shape)
    out_two[...] = product.astype(BF16).reshape(out_two.shape)
    second = core_copies(4, out_two, in_two)
    second_x = x_copies(4, out_x_two, in_x_two)
    begin(second)

    @pl.when(late)
    def _():
        gram_pass()

    pass_on(second, second_x, part, in_two, out_x_two)
    total = plane_total(second, second_x, part, in_two, in_x_two)
    z_start(1, total)

    def gram_back():
        @pl.when(is_root)
        def _():
            gram_root()

        @pl.when(is_rim)
        def _():
            bc_copies[0].wait_recv()

        begin(gram_gather)

    @pl.when(late)
    def _():
        gram_end()

    @pl.when(late & is_rim)
    def _():
        gram_send()

    @pl.when(early)
    def _():
        gram_back()
        gathered(5, gram_full, by_strip)

    @pl.when(late & is_rim)
    def _():
        gram_back()
        gathered(5, gram_full, by_strip)

    up_copies = [
        rcopy(
            result_out.at[q],
            result_in,
            up_send.at[q],
            up_recv.at[0],
            dev(layer, x, c * per + q // NC, q % NC),
        )
        for q in range(NZ)
    ]
    own_q = (ROOT - c * per) * NC + c

    @pl.when(is_root)
    def _():
        root_total(1, full)
        begin(gather(6, full, strip))

        @pl.when(late)
        def _():
            gram_back()

        gathered(6, full, by_strip)

        @pl.when(late)
        def _():
            gathered(5, gram_full, by_strip)

        cross_gram = gram_full[pl.ds(half_blocks, half_blocks)].reshape(width, width)
        mix = dot(cross_gram, ginv_ref[...], (0, 0), HIGH)
        value = base[...] - dot(times_inverse(full), mix, precision=HIGH)
        result[...] = value
        for q in sorted(range(NZ), key=lambda q: -abs(q // NC - ROOT % per)):
            result_out[q] = result[pl.ds(q * own_rows, own_rows), :]

            @pl.when(own_q != q)
            def _(copy=up_copies[q]):
                copy.start()

        @pl.when(a_self)
        def _():
            upd_ref[...] = result_out[ROOT % per * NC + ROOT // per]

    gram_ref[...] = gram_full[...].reshape(gram_ref.shape)

    @pl.when(a_other)
    def _():
        rcopy(
            result_out.at[0], result_in, up_send.at[0], up_recv.at[0], dev(layer, x, z, other)
        ).wait_recv()
        upd_ref[...] = result_in[...]

    sent(first)
    sent(first_x)
    sent(second)
    sent(second_x)
    sent(gram_core)
    sent(gram_x)
    sent(gram_gather)
    sent(passes(5, gram_full, by_strip))

    @pl.when(a_other)
    def _():
        a_remote.wait_send()

    @pl.when(sends_near)
    def _():
        shift.wait_send()

    @pl.when(sends_far)
    def _():
        for copy in to_relay:
            copy.wait_send()

    for q in hops:

        @pl.when(relays & (y == q))
        def _(q=q):
            far_relay[q - 1].wait_send()

    @pl.when(is_rim)
    def _():
        z_copy(0, z_out_wide, z_in_wide).wait_send()
        z_copy(1, z_out, z_in).wait_send()
        z_copy(2, gram_z_out, gram_z_in).wait_send()

    @pl.when(is_root)
    def _():
        sent(bc_copies)
        for kind, buf in ((1, full_wide), (6, full)):
            sent(gather(kind, buf, strip))
            sent(passes(kind, buf, by_strip))
        for q, copy in enumerate(up_copies):

            @pl.when(own_q != q)
            def _(copy=copy):
                copy.wait_send()

    @pl.when(has_next)
    def _():
        sent(gather(3, pre, block))
        sent(passes(3, pre, by_block))

    @pl.when(is_root & has_prev)
    def _():
        for copy in pre_copies:
            copy.wait_send()


def per_device(layers, layer_inputs, output_grads, input_inverse, grad_inverse):
    _, images, side, _, width = layer_inputs.shape
    rows = images * side * side
    own_rows = input_inverse.shape[1]
    lanes = TAPS * width
    n = NX * NC
    strip = width // n
    block_rows = lanes // n
    gram_rows = 2 * width // n
    scale = 1.0 / (rows * n * NZ)
    vmem = pltpu.VMEM
    dma = pltpu.SemaphoreType.DMA
    scratch = [
        vmem((2, rows, width), BF16),
        vmem((width, width), F32),
        vmem((rows, lanes), BF16),
        vmem((rows, lanes), BF16),
        vmem((width, rows), BF16),
        vmem((2, rows, width), BF16),
        vmem((2, part_of(rows, 1)[1], width), BF16),
        vmem((n, strip, lanes), F32),
        vmem((n, strip, lanes), F32),
        vmem((NX, strip, lanes), F32),
        vmem((NX, strip, lanes), F32),
        vmem((NX, strip, lanes), F32),
        vmem((n, strip, lanes), BF16),
        vmem((NX, strip, lanes), BF16),
        vmem((NX, strip, lanes), BF16),
        vmem((NX, strip, lanes), BF16),
        vmem((strip, lanes), F32),
        vmem((strip, lanes), BF16),
        vmem((NZ, strip, lanes), BF16),
        vmem((strip, lanes), F32),
        vmem((NZ, strip, lanes), F32),
        vmem((n, strip, lanes), F32),
        vmem((n, strip, lanes), F32),
        vmem((NZ, own_rows, 1, lanes), F32),
        vmem((block_rows, lanes), F32),
        vmem((2 * block_rows, lanes), BF16),
        vmem((n, block_rows, width), BF16),
        vmem((block_rows, width), BF16),
        vmem((block_rows, width), F32),
        vmem((block_rows, width), F32),
        vmem((NZ, own_rows, width), F32),
        vmem((own_rows, width), F32),
        vmem((n, gram_rows, width), F32),
        vmem((NX, gram_rows, width), F32),
        vmem((NX, gram_rows, width), F32),
        vmem((NX, gram_rows, width), F32),
        vmem((gram_rows, width), F32),
        vmem((NZ, gram_rows, width), F32),
        vmem((n, gram_rows, width), F32),
        dma((7, n)),
        dma((7, n)),
        dma((3,)),
        dma((3, NZ)),
        dma((1,)),
        dma((NZ,)),
        dma((1,)),
        dma((1,)),
        dma((NY,)),
        dma((1,)),
        dma((NY,)),
        dma((NY,)),
        dma((NZ,)),
        dma((1,)),
        dma((NZ,)),
        dma((1,)),
        dma((NZ,)),
        dma((1,)),
        dma((3,)),
        pltpu.SemaphoreType.REGULAR,
    ]
    whole = pl.BlockSpec(memory_space=pltpu.VMEM)
    update, grams = pl.pallas_call(
        functools.partial(kernel, layers, images, side, scale),
        out_shape=(
            jax.ShapeDtypeStruct((own_rows, width), F32),
            jax.ShapeDtypeStruct((2, width, width), F32),
        ),
        in_specs=[pl.BlockSpec(memory_space=pltpu.HBM)] * 4,
        out_specs=(whole, whole),
        scratch_shapes=scratch,
        compiler_params=pltpu.CompilerParams(
            collective_id=0, has_side_effects=True, vmem_limit_bytes=48 * 1024 * 1024
        ),
        name="kfac_step",
    )(
        *(
            pltpu.with_memory_space_constraint(value, pltpu.HBM)
            for value in (
                layer_inputs.reshape(rows, width),
                output_grads.reshape(rows, width),
                input_inverse.transpose(1, 0, 2),
                grad_inverse.reshape(width, width),
            )
        )
    )
    return update[None], grams[None]


def solution(mesh):
    assert mesh.shape["pos"] == NX * NZ * NC and mesh.shape["layer"] % NY == 0
    return jax.shard_map(
        functools.partial(per_device, mesh.shape["layer"]),
        mesh=mesh,
        in_specs=(
            P("layer", "pos", None, None, None),
            P("layer", "pos", None, None, None),
            P("layer", "pos", None),
            P("layer", None, None),
        ),
        out_specs=(P("layer", "pos", None), P("layer", None, None, None)),
        check_vma=False,
    )
```

```python
import functools

import jax
import jax.numpy as jnp
from jax import lax
from jax.experimental import pallas as pl
from jax.experimental.pallas import tpu as pltpu
from jax.sharding import PartitionSpec as P

NX, NY, NZ, NC = 4, 4, 8, 2
ROOT = 3
TAPS = 9
MESH = pl.DeviceIdType.MESH
F32 = jnp.float32
BF16 = jnp.bfloat16
HIGH = lax.Precision.HIGHEST


def offsets():
    return sorted(range(1, NX), key=lambda d: -min(d, NX - d))


def rcopy(src, dst, send_sem, recv_sem, to):
    return pltpu.make_async_remote_copy(
        src_ref=src,
        dst_ref=dst,
        send_sem=send_sem,
        recv_sem=recv_sem,
        device_id=to,
        device_id_type=MESH,
    )


def part_of(rows, q):
    size = -(-rows // (NY - 1) // 16) * 16
    start = (q - 1) * size
    return start, min(size, rows - start)


def dot(a, b, contract=(1, 0), precision=None):
    return lax.dot_general(
        a,
        b,
        (((contract[0],), (contract[1],)), ((), ())),
        precision=precision,
        preferred_element_type=F32,
    )


def unfold(src, dst, images, side, width):
    area = side * side
    rows = images * area
    value = src[...].astype(F32)
    col = lax.rem(lax.broadcasted_iota(jnp.int32, (rows, width), 0), side)
    before = jnp.where(col == 0, 0.0, pltpu.roll(value, 1, 0))
    after = jnp.where(col == side - 1, 0.0, pltpu.roll(value, rows - 1, 0))
    edge = jnp.zeros((side, width), BF16)
    for s, piece in enumerate((before, value, after)):
        piece = piece.astype(BF16)
        for image in range(images):
            top = image * area
            one = piece[top : top + area]
            lanes = pl.ds(s * width, width)
            dst[pl.ds(top, side), lanes] = edge
            dst[pl.ds(top + side, area - side), lanes] = one[: area - side]
            lanes = pl.ds((3 + s) * width, width)
            dst[pl.ds(top, area), lanes] = one
            lanes = pl.ds((6 + s) * width, width)
            dst[pl.ds(top, area - side), lanes] = one[side:]
            dst[pl.ds(top + area - side, side), lanes] = edge


def kernel(
    layers,
    images,
    side,
    scale,
    x_hbm,
    g_hbm,
    a_ref,
    ginv_hbm,
    upd_ref,
    gram_ref,
    xg_ref,
    ginv_ref,
    patches,
    patches_next,
    grad_t,
    xg_next,
    relay,
    part,
    part_one,
    in_one,
    out_x_one,
    in_x_one,
    out_two,
    in_two,
    out_x_two,
    in_x_two,
    plane_sum,
    z_out,
    z_in,
    z_out_wide,
    z_in_wide,
    full,
    full_wide,
    a_in,
    a_all,
    a_two,
    pre,
    rows_full,
    base,
    result,
    result_out,
    result_in,
    gram_part,
    gram_in,
    gram_out_x,
    gram_in_x,
    gram_z_out,
    gram_z_in,
    gram_full,
    ex_send,
    ex_recv,
    z_send,
    z_recv,
    a_send,
    a_recv,
    shift_send,
    shift_recv,
    relay_send,
    relay_recv,
    far_send,
    far_recv,
    pre_send,
    pre_recv,
    bc_send,
    bc_recv,
    up_send,
    up_recv,
    load_sem,
    ready_sem,
    go_sem,
):
    layer = lax.axis_index("layer")
    pos = lax.axis_index("pos")
    c = lax.rem(pos, NC)
    z = lax.rem(lax.div(pos, NC), NZ)
    x = lax.div(pos, NC * NZ)
    block = x * NC + c
    strip = c * NX + x
    n = NX * NC
    _, rows, width = xg_ref.shape
    y = lax.rem(layer, NY)
    lanes = TAPS * width
    per = NZ // NC
    own_rows = result_in.shape[0]
    front = (TAPS + 1) // 2 * width
    spans = ((0, front, 0), (front, lanes - front, 1))
    narrow = (0, width, 0)
    is_root = z == ROOT
    is_rim = z != ROOT
    has_next = layer < layers - 1
    has_prev = layer > 0
    sends_far = has_prev & (y == 0)
    sends_near = has_prev & (y != 0)
    relays = (layer >= NY) & (y != 0)
    late = has_next & (y == NY - 1)

    def dev(lay, px, pz, pc):
        return (lay, (px * NZ + pz) * NC + pc)

    def ahead(dx):
        return lax.rem(x + dx, NX)

    def behind(dx):
        return lax.rem(x + NX - dx, NX)

    other = NC - 1 - c
    far_first = sorted(range(NZ), key=lambda pz: -abs(pz - ROOT))
    others = far_first[:-1]

    loads = [
        pltpu.make_async_copy(src, dst, load_sem.at[i])
        for i, (src, dst) in enumerate(((x_hbm, xg_ref.at[0]), (g_hbm, xg_ref.at[1]), (ginv_hbm, ginv_ref)))
    ]
    for load in loads:
        load.start()

    barrier = pltpu.get_barrier_semaphore()

    def greet(to):
        pl.semaphore_signal(barrier, inc=1, device_id=to, device_id_type=MESH)

    @pl.when(c != 0)
    def _():
        greet(dev(layer, x, z, 0))

    for dx in offsets():
        greet(dev(layer, ahead(dx), z, 0))

    @pl.when(is_rim)
    def _():
        greet(dev(layer, x, ROOT, 0))

    @pl.when(is_root)
    def _():
        for pz in others:
            greet(dev(layer, x, pz, 0))

    @pl.when(has_next)
    def _():
        greet(dev(layer + 1, x, z, 1))

    @pl.when(has_next & is_rim)
    def _():
        greet(dev(layer + 1, x, ROOT, 1))

    @pl.when(relays)
    def _():
        greet(dev(layer - y, x, z, 1))

    @pl.when(late)
    def _():
        for q in range(1, NY):
            greet(dev(layer + 1 + q, x, z, 1))

    for load in loads:
        load.wait()
    unfold(xg_ref.at[0], patches, images, side, width)
    grad_t[...] = xg_ref[1].T

    root = is_root.astype(jnp.int32)
    chips = 1 + root * (NZ - 2)
    near_greets = 1 + NC * (NX - 1 + chips)
    chips = 1 + root * (NZ - 1) + sends_far.astype(jnp.int32) * (NY - 1) + relays.astype(jnp.int32)
    far_greets = NC * chips

    @pl.when(c == 0)
    def _():
        pl.semaphore_wait(barrier, near_greets)
        pl.semaphore_signal(
            ready_sem, inc=1, device_id=dev(layer, x, z, other), device_id_type=MESH
        )

    @pl.when(c != 0)
    def _():
        pl.semaphore_wait(ready_sem, 1)

    shift = rcopy(xg_ref, xg_next, shift_send.at[0], shift_recv.at[0], dev(layer - 1, x, z, c))
    hops = range(1, NY)

    def piece(ref, q):
        start, size = part_of(rows, q)
        return ref.at[:, pl.ds(start, size)]

    def held(q):
        return relay.at[:, pl.ds(0, part_of(rows, q)[1])]

    to_relay = [
        rcopy(
            piece(xg_ref, q), held(q), relay_send.at[0], relay_recv.at[0], dev(layer + q, x, z, c)
        )
        for q in hops
    ]
    far_relay = [
        rcopy(
            held(q), piece(xg_next, q), far_send.at[0], far_recv.at[q], dev(layer - q - 1, x, z, c)
        )
        for q in hops
    ]

    def arrived():
        @pl.when(has_next & jnp.logical_not(late))
        def _():
            shift.wait_recv()

        @pl.when(late)
        def _():
            for copy in far_relay:
                copy.wait_recv()

    half = lax.div(z, per)
    slot = lax.rem(z, per) * NC + c
    a_self = is_root & (half == c)
    a_other = jnp.logical_not(a_self)
    held_back = (z > ROOT) & (z <= ROOT + 2)
    group = lax.div(slot, NZ // 2)
    a_remote = rcopy(a_ref, a_in.at[slot], a_send.at[0], a_recv.at[group], dev(layer, x, ROOT, half))
    a_local = pltpu.make_async_copy(a_ref, a_in.at[slot], a_recv.at[group])

    @pl.when(a_other & jnp.logical_not(held_back))
    def _():
        a_remote.start()

    @pl.when(a_self)
    def _():
        a_local.start()

    def cols(view, span):
        return view.at[:, pl.ds(span[0], span[1])]

    def begin(copies):
        for copy in copies:
            copy.start()

    def core_copies(kind, out, in_core):
        return [
            rcopy(
                out.at[other * NX + ahead(dx)],
                in_core.at[dx],
                ex_send.at[kind, 0],
                ex_recv.at[kind, dx],
                dev(layer, x, z, other),
            )
            for dx in offsets() + [0]
        ]

    def x_copies(kind, out_x, in_x, span):
        return [
            rcopy(
                cols(out_x.at[dx], span),
                cols(in_x.at[dx], span),
                ex_send.at[kind, 1],
                ex_recv.at[kind, NX + span[2]],
                dev(layer, ahead(dx), z, c),
            )
            for dx in offsets()
        ]

    def pass_on(core, along, part, in_core, out_x, span):
        at = pl.ds(span[0], span[1])
        for dx, arrival, copy in zip(offsets(), core, along):
            if span[2] == 0:
                arrival.wait_recv()
            mine = part[c * NX + ahead(dx), :, at]
            out_x[dx, :, at] = (mine + in_core[dx, :, at].astype(F32)).astype(out_x.dtype)
            copy.start()

    def plane_total(kind, core, part, in_core, in_x, span):
        at = pl.ds(span[0], span[1])
        if span[2] == 0:
            core[-1].wait_recv()
        total = part[strip, :, at] + in_core[0, :, at].astype(F32)
        got = in_x.at[pl.ds(1, NX - 1), :, at]
        rcopy(
            got, got, ex_send.at[kind, 1], ex_recv.at[kind, NX + span[2]], dev(layer, x, z, other)
        ).wait_recv()
        for dx in range(1, NX):
            total = total + in_x[dx, :, at].astype(F32)
        return total

    def all_sent(sem, view):
        rcopy(view, view, sem, ex_recv.at[0, 0], dev(layer, x, z, other)).wait_send()

    def plane_sent(kind, in_core, in_x):
        all_sent(ex_send.at[kind, 0], in_core)
        all_sent(ex_send.at[kind, 1], in_x.at[pl.ds(1, NX - 1)])

    def gather_sent(kind, buf):
        all_sent(ex_send.at[kind, 0], buf.at[pl.ds(0, NX)])
        all_sent(ex_send.at[kind, 1], buf.at[pl.ds(0, NX - 1)])

    def crossing(kind, out, s, got, to):
        return rcopy(got, got, ex_send.at[kind, out], ex_recv.at[kind, s], to)

    def gather(kind, buf, own, span):
        targets = [(dx, dev(layer, ahead(dx), z, c)) for dx in offsets()]
        got = cols(buf.at[own], span)
        return [
            crossing(kind, 0, NX * span[2] + dx, got, to)
            for dx, to in targets + [(0, dev(layer, x, z, other))]
        ]

    def gathered(kind, buf, place, span):
        partner = dev(layer, x, z, other)
        for dx in reversed(offsets()):
            got = cols(buf.at[place(behind(dx), c)], span)
            crossing(kind, 0, NX * span[2] + dx, got, partner).wait_recv()
            crossing(kind, 1, NX * span[2], got, partner).start()
        got = buf.at[pl.ds(0, NX), :, pl.ds(span[0], span[1])]
        crossing(kind, 0, NX * span[2], got, partner).wait_recv()

    def by_strip(px, pc):
        return pc * NX + px

    def by_block(px, pc):
        return px * NC + pc

    def z_copy(kind, src, dst, span):
        return rcopy(
            cols(src, span),
            cols(dst.at[z], span),
            z_send.at[kind],
            z_recv.at[kind, span[2]],
            dev(layer, x, ROOT, c),
        )

    def z_arrived(kind, dst, span):
        got = dst.at[pl.ds(0, NZ - 1), :, pl.ds(span[0], span[1])]
        rcopy(got, got, z_send.at[kind], z_recv.at[kind, span[2]], dev(layer, x, z, other)).wait_recv()

    z_bufs = ((z_out_wide, z_in_wide), (z_out, z_in))

    def z_start(z_slot, total, span):
        at = pl.ds(span[0], span[1])
        plane_sum[:, at] = total
        src, dst = z_bufs[z_slot]

        @pl.when(is_rim)
        def _():
            src[:, at] = total.astype(src.dtype)
            z_copy(z_slot, src, dst, span).start()

    def root_total(z_slot, buf, span):
        at = pl.ds(span[0], span[1])
        total = plane_sum[:, at]
        _, dst = z_bufs[z_slot]
        z_arrived(z_slot, dst, span)
        for pz in others:
            total = total + dst[pz, :, at].astype(F32)
        buf[strip, :, at] = total * scale

    def fold(both):
        half_rows = both.shape[0] // 2
        return both[:half_rows] + both[half_rows:]

    def times_inverse(buf):
        value = buf[...].reshape(width, lanes)
        top = value.astype(BF16)
        low = (value - top.astype(F32)).astype(BF16)
        both = dot(a_two[...], jnp.concatenate([top, low], axis=0), (1, 1))
        return fold(both[:, :width] + both[:, width:])

    part_one[...] = dot(grad_t[...], patches[...]).reshape(part_one.shape)
    first = core_copies(0, part_one, in_one)
    first_x = [x_copies(0, out_x_one, in_x_one, span) for span in spans]
    begin(first)
    for span, along in zip(spans, first_x):
        pass_on(first, along, part_one, in_one, out_x_one, span)

    @pl.when(has_prev & (c != 0))
    def _():
        pl.semaphore_wait(barrier, far_greets)
        pl.semaphore_signal(
            ready_sem, inc=1, device_id=dev(layer, x, z, other), device_id_type=MESH
        )

    @pl.when(has_prev & (c == 0))
    def _():
        pl.semaphore_wait(ready_sem, 1)

    @pl.when(sends_near)
    def _():
        shift.start()

    @pl.when(sends_far)
    def _():
        for copy in to_relay:
            copy.start()

    for span in spans:
        z_start(0, plane_total(0, first, part_one, in_one, in_x_one, span), span)

    for q in hops:

        @pl.when(relays & (y == q))
        def _(q=q):
            to_relay[q - 1].wait_recv()
            far_relay[q - 1].start()


    @pl.when(jnp.logical_not(has_next))
    def _():
        xg_next[...] = jnp.zeros_like(xg_next)
        pre[...] = jnp.zeros_like(pre)

    half_blocks = gram_part.shape[0] // 2
    gram_core = core_copies(2, gram_part, gram_in)
    gram_x = x_copies(2, gram_out_x, gram_in_x, narrow)
    gram_gather = gather(5, gram_full, strip, narrow)
    bc_copies = [
        rcopy(
            gram_full.at[strip],
            gram_full.at[strip],
            bc_send.at[0],
            bc_recv.at[0],
            dev(layer, x, pz, c),
        )
        for pz in others
    ]

    def gram_begin():
        arrived()
        shape = (half_blocks, gram_part.shape[1], width)
        gram_part[pl.ds(0, half_blocks)] = dot(grad_t[...], xg_ref[1]).reshape(shape)
        gram_part[pl.ds(half_blocks, half_blocks)] = dot(grad_t[...], xg_next[1]).reshape(shape)
        begin(gram_core)

    def gram_pass():
        pass_on(gram_core, gram_x, gram_part, gram_in, gram_out_x, narrow)

    def gram_end():
        gram_z_out[...] = plane_total(2, gram_core, gram_part, gram_in, gram_in_x, narrow)

    def gram_root():
        total = gram_z_out[...]
        z_arrived(2, gram_z_in, narrow)
        for pz in others:
            total = total + gram_z_in[pz]
        gram_full[strip] = total * scale
        begin(bc_copies)

    def gram_send():
        z_copy(2, gram_z_out, gram_z_in, narrow).start()

    early = jnp.logical_not(late)

    @pl.when(early)
    def _():
        gram_begin()
        gram_pass()

    @pl.when(early & is_rim)
    def _():
        gram_end()

    @pl.when(held_back)
    def _():
        pl.semaphore_wait(go_sem, 1)
        a_remote.start()

    pre_copies = [
        rcopy(
            rows_full,
            pre.at[block],
            pre_send.at[0],
            pre_recv.at[0],
            dev(layer - 1, x, pz, c),
        )
        for pz in far_first
    ]

    def assemble(g):
        taken = a_in.at[pl.ds(g * (NZ // 2), NZ // 2)]
        pltpu.make_async_copy(taken, taken, a_recv.at[g]).wait()
        for q in range(g * (NZ // 2), (g + 1) * (NZ // 2)):
            a_all[pl.ds(q * own_rows, own_rows), :] = a_in[q, :, 0, :]

    @pl.when(is_root)
    def _():
        root_total(0, full_wide, spans[0])
        begin(gather(1, full_wide, strip, spans[0]))
        for d in range(2):
            pl.semaphore_signal(
                go_sem, inc=1, device_id=dev(layer, x, ROOT + 1 + d, c), device_id_type=MESH
            )
        root_total(0, full_wide, spans[1])
        begin(gather(1, full_wide, strip, spans[1]))

        assemble(1)
        for span in spans:
            gathered(1, full_wide, by_strip, span)
        assemble(0)
        rows = a_all[...]
        top = rows.astype(BF16)
        a_two[pl.ds(0, rows.shape[0]), :] = top
        a_two[pl.ds(rows.shape[0], rows.shape[0]), :] = (rows - top.astype(F32)).astype(BF16)
        value = dot(times_inverse(full_wide), ginv_ref[...], precision=HIGH)
        base[...] = value
        rows_full[...] = value.astype(BF16)

        @pl.when(sends_near)
        def _():
            for copy in pre_copies:
                copy.start()

        @pl.when(sends_far)
        def _():
            for copy in reversed(pre_copies):
                copy.start()

        @pl.when(early)
        def _():
            gram_end()


    @pl.when(late)
    def _():
        gram_begin()

    unfold(xg_next.at[0], patches_next, images, side, width)

    @pl.when(has_next)
    def _():
        rcopy(
            rows_full, pre.at[block], pre_send.at[0], pre_recv.at[0], dev(layer, x, z, other)
        ).wait_recv()
        begin(gather(3, pre, block, narrow))
        gathered(3, pre, by_block, narrow)

    @pl.when(early & is_rim)
    def _():
        gram_send()

    mapped = dot(patches_next[...], pre[...].reshape(lanes, width)).astype(BF16)
    product = dot(mapped.T, patches[...])
    part[...] = product.reshape(part.shape)
    out_two[...] = product.astype(BF16).reshape(out_two.shape)
    second = core_copies(4, out_two, in_two)
    second_x = [x_copies(4, out_x_two, in_x_two, span) for span in spans]
    begin(second)

    @pl.when(late)
    def _():
        gram_pass()

    for span, along in zip(spans, second_x):
        pass_on(second, along, part, in_two, out_x_two, span)
    for span in spans:
        z_start(1, plane_total(4, second, part, in_two, in_x_two, span), span)
    def gram_back():
        @pl.when(is_root)
        def _():
            gram_root()

        @pl.when(is_rim)
        def _():
            bc_copies[0].wait_recv()

        begin(gram_gather)

    @pl.when(late)
    def _():
        gram_end()

    @pl.when(late & is_rim)
    def _():
        gram_send()

    @pl.when(early)
    def _():
        gram_back()
        gathered(5, gram_full, by_strip, narrow)

    @pl.when(late & is_rim)
    def _():
        gram_back()
        gathered(5, gram_full, by_strip, narrow)

    @pl.when(is_rim | early)
    def _():
        gram_ref[...] = gram_full[...].reshape(gram_ref.shape)

    plane_sent(0, in_one, in_x_one)
    plane_sent(2, gram_in, gram_in_x)
    plane_sent(4, in_two, in_x_two)

    @pl.when(a_other)
    def _():
        a_remote.wait_send()

    @pl.when(sends_near)
    def _():
        shift.wait_send()

    @pl.when(sends_far)
    def _():
        all_sent(relay_send.at[0], xg_next)

    for q in hops:

        @pl.when(relays & (y == q))
        def _(q=q):
            far_relay[q - 1].wait_send()

    @pl.when(has_next)
    def _():
        gather_sent(3, pre)

    @pl.when(is_root & has_prev)
    def _():
        all_sent(pre_send.at[0], pre)

    @pl.when(is_root)
    def _():
        gather_sent(1, full_wide)

    @pl.when(is_rim)
    def _():
        all_sent(z_send.at[0], z_out_wide)
        all_sent(z_send.at[1], z_out)
        all_sent(z_send.at[2], gram_z_out)
        gather_sent(5, gram_full)

    up_copies = [
        rcopy(
            result_out.at[q],
            result_in,
            up_send.at[0],
            up_recv.at[0],
            dev(layer, x, c * per + q // NC, q % NC),
        )
        for q in range(NZ)
    ]
    own_q = (ROOT - c * per) * NC + c

    @pl.when(is_root)
    def _():
        for span in spans:
            root_total(1, full, span)
            begin(gather(6, full, strip, span))

        @pl.when(late)
        def _():
            gram_back()

        for span in spans:
            gathered(6, full, by_strip, span)

        @pl.when(late)
        def _():
            gathered(5, gram_full, by_strip, narrow)


        @pl.when(late)
        def _():
            gram_ref[...] = gram_full[...].reshape(gram_ref.shape)

        cross_gram = gram_full[pl.ds(half_blocks, half_blocks)].reshape(width, width)
        mix = dot(cross_gram, ginv_ref[...], (0, 0), HIGH)
        value = base[...] - dot(times_inverse(full), mix, precision=HIGH)
        result[...] = value
        for q in sorted(range(NZ), key=lambda q: -abs(q // NC - ROOT % per)):
            result_out[q] = result[pl.ds(q * own_rows, own_rows), :]

            @pl.when(own_q != q)
            def _(copy=up_copies[q]):
                copy.start()

        @pl.when(a_self)
        def _():
            upd_ref[...] = result_out[ROOT % per * NC + ROOT // per]

    @pl.when(a_other)
    def _():
        rcopy(
            result_out.at[0], result_in, up_send.at[0], up_recv.at[0], dev(layer, x, z, other)
        ).wait_recv()
        upd_ref[...] = result_in[...]

    @pl.when(is_root)
    def _():
        all_sent(bc_send.at[0], gram_full.at[pl.ds(0, NZ - 1)])
        gather_sent(5, gram_full)
        gather_sent(6, full)

    @pl.when(a_self)
    def _():
        all_sent(up_send.at[0], result_out.at[pl.ds(0, NZ - 1)])

    @pl.when(is_root & a_other)
    def _():
        all_sent(up_send.at[0], result_out)


def per_device(layers, layer_inputs, output_grads, input_inverse, grad_inverse):
    _, images, side, _, width = layer_inputs.shape
    rows = images * side * side
    own_rows = input_inverse.shape[1]
    lanes = TAPS * width
    n = NX * NC
    strip = width // n
    block_rows = lanes // n
    gram_rows = 2 * width // n
    scale = 1.0 / (rows * n * NZ)
    vmem = pltpu.VMEM
    dma = pltpu.SemaphoreType.DMA
    scratch = [
        vmem((2, rows, width), BF16),
        vmem((width, width), F32),
        vmem((rows, lanes), BF16),
        vmem((rows, lanes), BF16),
        vmem((width, rows), BF16),
        vmem((2, rows, width), BF16),
        vmem((2, part_of(rows, 1)[1], width), BF16),
        vmem((n, strip, lanes), F32),
        vmem((n, strip, lanes), F32),
        vmem((NX, strip, lanes), F32),
        vmem((NX, strip, lanes), F32),
        vmem((NX, strip, lanes), F32),
        vmem((n, strip, lanes), BF16),
        vmem((NX, strip, lanes), BF16),
        vmem((NX, strip, lanes), BF16),
        vmem((NX, strip, lanes), BF16),
        vmem((strip, lanes), F32),
        vmem((strip, lanes), BF16),
        vmem((NZ, strip, lanes), BF16),
        vmem((strip, lanes), F32),
        vmem((NZ, strip, lanes), F32),
        vmem((n, strip, lanes), F32),
        vmem((n, strip, lanes), F32),
        vmem((NZ, own_rows, 1, lanes), F32),
        vmem((block_rows, lanes), F32),
        vmem((2 * block_rows, lanes), BF16),
        vmem((n, block_rows, width), BF16),
        vmem((block_rows, width), BF16),
        vmem((block_rows, width), F32),
        vmem((block_rows, width), F32),
        vmem((NZ, own_rows, width), F32),
        vmem((own_rows, width), F32),
        vmem((n, gram_rows, width), F32),
        vmem((NX, gram_rows, width), F32),
        vmem((NX, gram_rows, width), F32),
        vmem((NX, gram_rows, width), F32),
        vmem((gram_rows, width), F32),
        vmem((NZ, gram_rows, width), F32),
        vmem((n, gram_rows, width), F32),
        dma((7, 2)),
        dma((7, 2 * NX)),
        dma((3,)),
        dma((3, 2)),
        dma((1,)),
        dma((2,)),
        dma((1,)),
        dma((1,)),
        dma((1,)),
        dma((1,)),
        dma((1,)),
        dma((NY,)),
        dma((1,)),
        dma((1,)),
        dma((1,)),
        dma((1,)),
        dma((1,)),
        dma((1,)),
        dma((3,)),
        pltpu.SemaphoreType.REGULAR,
        pltpu.SemaphoreType.REGULAR,
    ]
    whole = pl.BlockSpec(memory_space=pltpu.VMEM)
    update, grams = pl.pallas_call(
        functools.partial(kernel, layers, images, side, scale),
        out_shape=(
            jax.ShapeDtypeStruct((own_rows, width), F32),
            jax.ShapeDtypeStruct((2, width, width), F32),
        ),
        in_specs=[pl.BlockSpec(memory_space=pltpu.HBM)] * 4,
        out_specs=(whole, whole),
        scratch_shapes=scratch,
        compiler_params=pltpu.CompilerParams(
            collective_id=0, has_side_effects=True, vmem_limit_bytes=48 * 1024 * 1024
        ),
        name="kfac_step",
    )(
        *(
            pltpu.with_memory_space_constraint(value, pltpu.HBM)
            for value in (
                layer_inputs.reshape(rows, width),
                output_grads.reshape(rows, width),
                input_inverse.transpose(1, 0, 2),
                grad_inverse.reshape(width, width),
            )
        )
    )
    return update[None], grams[None]


def solution(mesh):
    assert mesh.shape["pos"] == NX * NZ * NC and mesh.shape["layer"] % NY == 0
    return jax.shard_map(
        functools.partial(per_device, mesh.shape["layer"]),
        mesh=mesh,
        in_specs=(
            P("layer", "pos", None, None, None),
            P("layer", "pos", None, None, None),
            P("layer", "pos", None),
            P("layer", None, None),
        ),
        out_specs=(P("layer", "pos", None), P("layer", None, None, None)),
        check_vma=False,
    )
```

```python
import functools

import jax
import jax.numpy as jnp
from jax import lax
from jax.experimental import pallas as pl
from jax.experimental.pallas import tpu as pltpu
from jax.sharding import PartitionSpec as P

NX, NY, NZ, NC = 4, 4, 8, 2
ROOT = 3
TAPS = 9
MESH = pl.DeviceIdType.MESH
F32 = jnp.float32
BF16 = jnp.bfloat16
HIGH = lax.Precision.HIGHEST


def offsets():
    return sorted(range(1, NX), key=lambda d: -min(d, NX - d))


def rcopy(src, dst, send_sem, recv_sem, to):
    return pltpu.make_async_remote_copy(
        src_ref=src,
        dst_ref=dst,
        send_sem=send_sem,
        recv_sem=recv_sem,
        device_id=to,
        device_id_type=MESH,
    )


def part_of(rows, q):
    size = -(-rows // (NY - 1) // 16) * 16
    start = (q - 1) * size
    return start, min(size, rows - start)


def dot(a, b, contract=(1, 0), precision=None):
    return lax.dot_general(
        a,
        b,
        (((contract[0],), (contract[1],)), ((), ())),
        precision=precision,
        preferred_element_type=F32,
    )


def unfold(src, dst, images, side, width):
    area = side * side
    rows = images * area
    value = src[...].astype(F32)
    col = lax.rem(lax.broadcasted_iota(jnp.int32, (rows, width), 0), side)
    before = jnp.where(col == 0, 0.0, pltpu.roll(value, 1, 0))
    after = jnp.where(col == side - 1, 0.0, pltpu.roll(value, rows - 1, 0))
    edge = jnp.zeros((side, width), BF16)
    for s, piece in enumerate((before, value, after)):
        piece = piece.astype(BF16)
        for image in range(images):
            top = image * area
            one = piece[top : top + area]
            lanes = pl.ds(s * width, width)
            dst[pl.ds(top, side), lanes] = edge
            dst[pl.ds(top + side, area - side), lanes] = one[: area - side]
            lanes = pl.ds((3 + s) * width, width)
            dst[pl.ds(top, area), lanes] = one
            lanes = pl.ds((6 + s) * width, width)
            dst[pl.ds(top, area - side), lanes] = one[side:]
            dst[pl.ds(top + area - side, side), lanes] = edge


def kernel(
    layers,
    images,
    side,
    scale,
    x_hbm,
    g_hbm,
    a_ref,
    ginv_hbm,
    upd_ref,
    gram_ref,
    xg_ref,
    ginv_ref,
    patches,
    patches_next,
    grad_t,
    xg_next,
    relay,
    part,
    part_one,
    in_one,
    out_x_one,
    in_x_one,
    out_two,
    in_two,
    out_x_two,
    in_x_two,
    plane_sum,
    z_out,
    z_in,
    z_out_wide,
    z_in_wide,
    full,
    full_wide,
    a_in,
    a_all,
    a_two,
    pre,
    rows_full,
    base,
    result,
    result_out,
    result_in,
    gram_part,
    gram_in,
    gram_out_x,
    gram_in_x,
    gram_z_out,
    gram_z_in,
    gram_full,
    ex_send,
    ex_recv,
    z_send,
    z_recv,
    a_send,
    a_recv,
    shift_send,
    shift_recv,
    relay_send,
    relay_recv,
    far_send,
    far_recv,
    pre_send,
    pre_recv,
    bc_send,
    bc_recv,
    up_send,
    up_recv,
    load_sem,
    ready_sem,
    go_sem,
):
    layer = lax.axis_index("layer")
    pos = lax.axis_index("pos")
    c = lax.rem(pos, NC)
    z = lax.rem(lax.div(pos, NC), NZ)
    x = lax.div(pos, NC * NZ)
    block = x * NC + c
    strip = c * NX + x
    n = NX * NC
    _, rows, width = xg_ref.shape
    y = lax.rem(layer, NY)
    lanes = TAPS * width
    per = NZ // NC
    own_rows = result_in.shape[0]
    front = TAPS // 2 * width
    spans = ((0, front, 0), (front, lanes - front, 1))
    narrow = (0, width, 0)
    is_root = z == ROOT
    is_rim = z != ROOT
    has_next = layer < layers - 1
    has_prev = layer > 0
    sends_far = has_prev & (y == 0)
    sends_near = has_prev & (y != 0)
    relays = (layer >= NY) & (y != 0)
    late = has_next & (y == NY - 1)

    def dev(lay, px, pz, pc):
        return (lay, (px * NZ + pz) * NC + pc)

    def ahead(dx):
        return lax.rem(x + dx, NX)

    def behind(dx):
        return lax.rem(x + NX - dx, NX)

    other = NC - 1 - c
    far_first = sorted(range(NZ), key=lambda pz: -abs(pz - ROOT))
    others = far_first[:-1]

    loads = [
        pltpu.make_async_copy(src, dst, load_sem.at[i])
        for i, (src, dst) in enumerate(((x_hbm, xg_ref.at[0]), (g_hbm, xg_ref.at[1]), (ginv_hbm, ginv_ref)))
    ]
    for load in loads:
        load.start()

    barrier = pltpu.get_barrier_semaphore()

    def greet(to):
        pl.semaphore_signal(barrier, inc=1, device_id=to, device_id_type=MESH)

    @pl.when(c != 0)
    def _():
        greet(dev(layer, x, z, 0))

    for dx in offsets():
        greet(dev(layer, ahead(dx), z, 0))

    @pl.when(is_rim)
    def _():
        greet(dev(layer, x, ROOT, 0))

    @pl.when(is_root)
    def _():
        for pz in others:
            greet(dev(layer, x, pz, 0))

    @pl.when(has_next)
    def _():
        greet(dev(layer + 1, x, z, 1))

    @pl.when(has_next & is_rim)
    def _():
        greet(dev(layer + 1, x, ROOT, 1))

    @pl.when(relays)
    def _():
        greet(dev(layer - y, x, z, 1))

    @pl.when(late)
    def _():
        for q in range(1, NY):
            greet(dev(layer + 1 + q, x, z, 1))

    for load in loads:
        load.wait()
    unfold(xg_ref.at[0], patches, images, side, width)
    grad_t[...] = xg_ref[1].T

    root = is_root.astype(jnp.int32)
    chips = 1 + root * (NZ - 2)
    near_greets = 1 + NC * (NX - 1 + chips)
    chips = 1 + root * (NZ - 1) + sends_far.astype(jnp.int32) * (NY - 1) + relays.astype(jnp.int32)
    far_greets = NC * chips

    @pl.when(c == 0)
    def _():
        pl.semaphore_wait(barrier, near_greets)
        pl.semaphore_signal(
            ready_sem, inc=1, device_id=dev(layer, x, z, other), device_id_type=MESH
        )

    @pl.when(c != 0)
    def _():
        pl.semaphore_wait(ready_sem, 1)

    shift = rcopy(xg_ref, xg_next, shift_send.at[0], shift_recv.at[0], dev(layer - 1, x, z, c))
    hops = range(1, NY)

    def piece(ref, q):
        start, size = part_of(rows, q)
        return ref.at[:, pl.ds(start, size)]

    def held(q):
        return relay.at[:, pl.ds(0, part_of(rows, q)[1])]

    to_relay = [
        rcopy(
            piece(xg_ref, q), held(q), relay_send.at[0], relay_recv.at[0], dev(layer + q, x, z, c)
        )
        for q in hops
    ]
    far_relay = [
        rcopy(
            held(q), piece(xg_next, q), far_send.at[0], far_recv.at[q], dev(layer - q - 1, x, z, c)
        )
        for q in hops
    ]

    def arrived():
        @pl.when(has_next & jnp.logical_not(late))
        def _():
            shift.wait_recv()

        @pl.when(late)
        def _():
            for copy in far_relay:
                copy.wait_recv()

    half = lax.div(z, per)
    slot = lax.rem(z, per) * NC + c
    a_self = is_root & (half == c)
    a_other = jnp.logical_not(a_self)
    held_back = (z > ROOT) & (z <= ROOT + 2)
    group = lax.div(slot, NZ // 2)
    a_remote = rcopy(a_ref, a_in.at[slot], a_send.at[0], a_recv.at[group], dev(layer, x, ROOT, half))
    a_local = pltpu.make_async_copy(a_ref, a_in.at[slot], a_recv.at[group])

    @pl.when(a_other & jnp.logical_not(held_back))
    def _():
        a_remote.start()

    @pl.when(a_self)
    def _():
        a_local.start()

    sizes = (NX + 2, 2 * NX, NX + 1, NX, NX + 2, NX, 2 * NX)
    first_recv = [sum(sizes[:kind]) for kind in range(len(sizes))]

    def cols(view, span):
        return view.at[:, pl.ds(span[0], span[1])]

    def begin(copies):
        for copy in copies:
            copy.start()

    def core_copies(kind, out, in_core):
        return [
            rcopy(
                out.at[other * NX + ahead(dx)],
                in_core.at[dx],
                ex_send.at[kind, 0],
                ex_recv.at[first_recv[kind] + dx],
                dev(layer, x, z, other),
            )
            for dx in offsets() + [0]
        ]

    def x_copies(kind, out_x, in_x, span):
        return [
            rcopy(
                cols(out_x.at[dx], span),
                cols(in_x.at[dx], span),
                ex_send.at[kind, 1],
                ex_recv.at[first_recv[kind] + NX + span[2]],
                dev(layer, ahead(dx), z, c),
            )
            for dx in offsets()
        ]

    def pass_on(core, along, part, in_core, out_x, span):
        at = pl.ds(span[0], span[1])
        for dx, arrival, copy in zip(offsets(), core, along):
            if span[2] == 0:
                arrival.wait_recv()
            mine = part[c * NX + ahead(dx), :, at]
            out_x[dx, :, at] = (mine + in_core[dx, :, at].astype(F32)).astype(out_x.dtype)
            copy.start()

    def plane_total(kind, core, part, in_core, in_x, span):
        at = pl.ds(span[0], span[1])
        if span[2] == 0:
            core[-1].wait_recv()
        total = part[strip, :, at] + in_core[0, :, at].astype(F32)
        got = in_x.at[pl.ds(1, NX - 1), :, at]
        rcopy(
            got, got, ex_send.at[kind, 1], ex_recv.at[first_recv[kind] + NX + span[2]], dev(layer, x, z, other)
        ).wait_recv()
        for dx in range(1, NX):
            total = total + in_x[dx, :, at].astype(F32)
        return total

    def all_sent(sem, view):
        rcopy(view, view, sem, ex_recv.at[0], dev(layer, x, z, other)).wait_send()

    def plane_sent(kind, in_core, in_x):
        all_sent(ex_send.at[kind, 0], in_core)
        all_sent(ex_send.at[kind, 1], in_x.at[pl.ds(1, NX - 1)])

    def gather_sent(kind, buf):
        all_sent(ex_send.at[kind, 0], buf.at[pl.ds(0, NX)])
        all_sent(ex_send.at[kind, 1], buf.at[pl.ds(0, NX - 1)])

    def crossing(kind, out, s, got, to):
        return rcopy(got, got, ex_send.at[kind, out], ex_recv.at[first_recv[kind] + s], to)

    def gather(kind, buf, own, span):
        targets = [(dx, dev(layer, ahead(dx), z, c)) for dx in offsets()]
        got = cols(buf.at[own], span)
        return [
            crossing(kind, 0, NX * span[2] + dx, got, to)
            for dx, to in targets + [(0, dev(layer, x, z, other))]
        ]

    def gathered(kind, buf, place, span):
        partner = dev(layer, x, z, other)
        for dx in reversed(offsets()):
            got = cols(buf.at[place(behind(dx), c)], span)
            crossing(kind, 0, NX * span[2] + dx, got, partner).wait_recv()
            crossing(kind, 1, NX * span[2], got, partner).start()
        got = buf.at[pl.ds(0, NX), :, pl.ds(span[0], span[1])]
        crossing(kind, 0, NX * span[2], got, partner).wait_recv()

    def by_strip(px, pc):
        return pc * NX + px

    def by_block(px, pc):
        return px * NC + pc

    def z_copy(kind, src, dst, span):
        return rcopy(
            cols(src, span),
            cols(dst.at[z], span),
            z_send.at[kind],
            z_recv.at[kind, span[2]],
            dev(layer, x, ROOT, c),
        )

    def z_arrived(kind, dst, span):
        got = dst.at[pl.ds(0, NZ - 1), :, pl.ds(span[0], span[1])]
        rcopy(got, got, z_send.at[kind], z_recv.at[kind, span[2]], dev(layer, x, z, other)).wait_recv()

    z_bufs = ((z_out_wide, z_in_wide), (z_out, z_in))

    def z_start(z_slot, total, span):
        at = pl.ds(span[0], span[1])
        plane_sum[:, at] = total
        src, dst = z_bufs[z_slot]

        @pl.when(is_rim)
        def _():
            src[:, at] = total.astype(src.dtype)
            z_copy(z_slot, src, dst, span).start()

    def root_total(z_slot, buf, span):
        at = pl.ds(span[0], span[1])
        total = plane_sum[:, at]
        _, dst = z_bufs[z_slot]
        z_arrived(z_slot, dst, span)
        for pz in others:
            total = total + dst[pz, :, at].astype(F32)
        buf[strip, :, at] = total * scale

    def fold(both):
        half_rows = both.shape[0] // 2
        return both[:half_rows] + both[half_rows:]

    def times_inverse(buf):
        value = buf[...].reshape(width, lanes)
        top = value.astype(BF16)
        low = (value - top.astype(F32)).astype(BF16)
        both = dot(a_two[...], jnp.concatenate([top, low], axis=0), (1, 1))
        return fold(both[:, :width] + both[:, width:])

    part_one[...] = dot(grad_t[...], patches[...]).reshape(part_one.shape)
    first = core_copies(0, part_one, in_one)
    first_x = [x_copies(0, out_x_one, in_x_one, span) for span in spans]
    begin(first)
    for span, along in zip(spans, first_x):
        pass_on(first, along, part_one, in_one, out_x_one, span)

    @pl.when(has_prev & (c != 0))
    def _():
        pl.semaphore_wait(barrier, far_greets)
        pl.semaphore_signal(
            ready_sem, inc=1, device_id=dev(layer, x, z, other), device_id_type=MESH
        )

    @pl.when(has_prev & (c == 0))
    def _():
        pl.semaphore_wait(ready_sem, 1)

    @pl.when(sends_near)
    def _():
        shift.start()

    @pl.when(sends_far)
    def _():
        for copy in to_relay:
            copy.start()

    for span in spans:
        z_start(0, plane_total(0, first, part_one, in_one, in_x_one, span), span)

    for q in hops:

        @pl.when(relays & (y == q))
        def _(q=q):
            to_relay[q - 1].wait_recv()
            far_relay[q - 1].start()


    @pl.when(jnp.logical_not(has_next))
    def _():
        xg_next[...] = jnp.zeros_like(xg_next)
        pre[...] = jnp.zeros_like(pre)

    half_blocks = gram_part.shape[0] // 2
    gram_core = core_copies(2, gram_part, gram_in)
    gram_x = x_copies(2, gram_out_x, gram_in_x, narrow)
    gram_gather = gather(5, gram_full, strip, narrow)
    bc_copies = [
        rcopy(
            gram_full.at[strip],
            gram_full.at[strip],
            bc_send.at[0],
            bc_recv.at[0],
            dev(layer, x, pz, c),
        )
        for pz in others
    ]

    def gram_begin():
        arrived()
        shape = (half_blocks, gram_part.shape[1], width)
        gram_part[pl.ds(0, half_blocks)] = dot(grad_t[...], xg_ref[1]).reshape(shape)
        gram_part[pl.ds(half_blocks, half_blocks)] = dot(grad_t[...], xg_next[1]).reshape(shape)
        begin(gram_core)

    def gram_pass():
        pass_on(gram_core, gram_x, gram_part, gram_in, gram_out_x, narrow)

    def gram_end():
        gram_z_out[...] = plane_total(2, gram_core, gram_part, gram_in, gram_in_x, narrow)

    def gram_root():
        total = gram_z_out[...]
        z_arrived(2, gram_z_in, narrow)
        for pz in others:
            total = total + gram_z_in[pz]
        gram_full[strip] = total * scale
        begin(bc_copies)

    def gram_send():
        z_copy(2, gram_z_out, gram_z_in, narrow).start()

    early = jnp.logical_not(late)

    @pl.when(early)
    def _():
        gram_begin()
        gram_pass()

    @pl.when(early & is_rim)
    def _():
        gram_end()

    @pl.when(held_back)
    def _():
        pl.semaphore_wait(go_sem, 1)
        a_remote.start()

    pre_copies = [
        rcopy(
            rows_full,
            pre.at[block],
            pre_send.at[0],
            pre_recv.at[0],
            dev(layer - 1, x, pz, c),
        )
        for pz in far_first
    ]

    def assemble(g):
        taken = a_in.at[pl.ds(g * (NZ // 2), NZ // 2)]
        pltpu.make_async_copy(taken, taken, a_recv.at[g]).wait()
        for q in range(g * (NZ // 2), (g + 1) * (NZ // 2)):
            a_all[pl.ds(q * own_rows, own_rows), :] = a_in[q, :, 0, :]

    @pl.when(is_root)
    def _():
        root_total(0, full_wide, spans[0])
        begin(gather(1, full_wide, strip, spans[0]))
        for d in range(2):
            pl.semaphore_signal(
                go_sem, inc=1, device_id=dev(layer, x, ROOT + 1 + d, c), device_id_type=MESH
            )
        root_total(0, full_wide, spans[1])
        begin(gather(1, full_wide, strip, spans[1]))

        assemble(1)
        for span in spans:
            gathered(1, full_wide, by_strip, span)
        assemble(0)
        rows = a_all[...]
        top = rows.astype(BF16)
        a_two[pl.ds(0, rows.shape[0]), :] = top
        a_two[pl.ds(rows.shape[0], rows.shape[0]), :] = (rows - top.astype(F32)).astype(BF16)
        value = dot(times_inverse(full_wide), ginv_ref[...], precision=HIGH)
        base[...] = value
        rows_full[...] = value.astype(BF16)

        @pl.when(sends_near)
        def _():
            for copy in pre_copies:
                copy.start()

        @pl.when(sends_far)
        def _():
            for copy in reversed(pre_copies):
                copy.start()

        @pl.when(early)
        def _():
            gram_end()


    @pl.when(late)
    def _():
        gram_begin()

    unfold(xg_next.at[0], patches_next, images, side, width)

    @pl.when(has_next)
    def _():
        rcopy(
            rows_full, pre.at[block], pre_send.at[0], pre_recv.at[0], dev(layer, x, z, other)
        ).wait_recv()
        begin(gather(3, pre, block, narrow))
        gathered(3, pre, by_block, narrow)

    @pl.when(early & is_rim)
    def _():
        gram_send()

    mapped = dot(patches_next[...], pre[...].reshape(lanes, width)).astype(BF16)
    product = dot(mapped.T, patches[...])
    part[...] = product.reshape(part.shape)
    out_two[...] = product.astype(BF16).reshape(out_two.shape)
    second = core_copies(4, out_two, in_two)
    second_x = [x_copies(4, out_x_two, in_x_two, span) for span in spans]
    begin(second)

    @pl.when(late)
    def _():
        gram_pass()

    for span, along in zip(spans, second_x):
        pass_on(second, along, part, in_two, out_x_two, span)
    for span in spans:
        z_start(1, plane_total(4, second, part, in_two, in_x_two, span), span)
    def gram_back():
        @pl.when(is_root)
        def _():
            gram_root()

        @pl.when(is_rim)
        def _():
            bc_copies[0].wait_recv()

        begin(gram_gather)

    @pl.when(late)
    def _():
        gram_end()

    @pl.when(late & is_rim)
    def _():
        gram_send()

    @pl.when(early)
    def _():
        gram_back()
        gathered(5, gram_full, by_strip, narrow)

    @pl.when(late & is_rim)
    def _():
        gram_back()
        gathered(5, gram_full, by_strip, narrow)

    @pl.when(is_rim | early)
    def _():
        gram_ref[...] = gram_full[...].reshape(gram_ref.shape)

    plane_sent(0, in_one, in_x_one)
    plane_sent(2, gram_in, gram_in_x)
    plane_sent(4, in_two, in_x_two)

    @pl.when(a_other)
    def _():
        a_remote.wait_send()

    @pl.when(sends_near)
    def _():
        shift.wait_send()

    @pl.when(sends_far)
    def _():
        all_sent(relay_send.at[0], xg_next)

    for q in hops:

        @pl.when(relays & (y == q))
        def _(q=q):
            far_relay[q - 1].wait_send()

    @pl.when(has_next)
    def _():
        gather_sent(3, pre)

    @pl.when(is_root & has_prev)
    def _():
        all_sent(pre_send.at[0], pre)

    @pl.when(is_root)
    def _():
        gather_sent(1, full_wide)

    @pl.when(is_rim)
    def _():
        all_sent(z_send.at[0], z_out_wide)
        all_sent(z_send.at[1], z_out)
        all_sent(z_send.at[2], gram_z_out)
        gather_sent(5, gram_full)

    up_copies = [
        rcopy(
            result_out.at[q],
            result_in,
            up_send.at[0],
            up_recv.at[0],
            dev(layer, x, c * per + q // NC, q % NC),
        )
        for q in range(NZ)
    ]
    own_q = (ROOT - c * per) * NC + c

    @pl.when(is_root)
    def _():
        for span in spans:
            root_total(1, full, span)
            begin(gather(6, full, strip, span))

        @pl.when(late)
        def _():
            gram_back()

        for span in spans:
            gathered(6, full, by_strip, span)

        @pl.when(late)
        def _():
            gathered(5, gram_full, by_strip, narrow)


        @pl.when(late)
        def _():
            gram_ref[...] = gram_full[...].reshape(gram_ref.shape)

        cross_gram = gram_full[pl.ds(half_blocks, half_blocks)].reshape(width, width)
        mix = dot(cross_gram, ginv_ref[...], (0, 0), HIGH)
        value = base[...] - dot(times_inverse(full), mix, precision=HIGH)
        result[...] = value
        for q in sorted(range(NZ), key=lambda q: -abs(q // NC - ROOT % per)):
            result_out[q] = result[pl.ds(q * own_rows, own_rows), :]

            @pl.when(own_q != q)
            def _(copy=up_copies[q]):
                copy.start()

        @pl.when(a_self)
        def _():
            upd_ref[...] = result_out[ROOT % per * NC + ROOT // per]

    @pl.when(a_other)
    def _():
        rcopy(
            result_out.at[0], result_in, up_send.at[0], up_recv.at[0], dev(layer, x, z, other)
        ).wait_recv()
        upd_ref[...] = result_in[...]

    @pl.when(is_root)
    def _():
        all_sent(bc_send.at[0], gram_full.at[pl.ds(0, NZ - 1)])
        gather_sent(5, gram_full)
        gather_sent(6, full)

    @pl.when(a_self)
    def _():
        all_sent(up_send.at[0], result_out.at[pl.ds(0, NZ - 1)])

    @pl.when(is_root & a_other)
    def _():
        all_sent(up_send.at[0], result_out)


def per_device(layers, layer_inputs, output_grads, input_inverse, grad_inverse):
    _, images, side, _, width = layer_inputs.shape
    rows = images * side * side
    own_rows = input_inverse.shape[1]
    lanes = TAPS * width
    n = NX * NC
    strip = width // n
    block_rows = lanes // n
    gram_rows = 2 * width // n
    scale = 1.0 / (rows * n * NZ)
    vmem = pltpu.VMEM
    dma = pltpu.SemaphoreType.DMA
    scratch = [
        vmem((2, rows, width), BF16),
        vmem((width, width), F32),
        vmem((rows, lanes), BF16),
        vmem((rows, lanes), BF16),
        vmem((width, rows), BF16),
        vmem((2, rows, width), BF16),
        vmem((2, part_of(rows, 1)[1], width), BF16),
        vmem((n, strip, lanes), F32),
        vmem((n, strip, lanes), F32),
        vmem((NX, strip, lanes), F32),
        vmem((NX, strip, lanes), F32),
        vmem((NX, strip, lanes), F32),
        vmem((n, strip, lanes), BF16),
        vmem((NX, strip, lanes), BF16),
        vmem((NX, strip, lanes), BF16),
        vmem((NX, strip, lanes), BF16),
        vmem((strip, lanes), F32),
        vmem((strip, lanes), BF16),
        vmem((NZ, strip, lanes), BF16),
        vmem((strip, lanes), F32),
        vmem((NZ, strip, lanes), F32),
        vmem((n, strip, lanes), F32),
        vmem((n, strip, lanes), F32),
        vmem((NZ, own_rows, 1, lanes), F32),
        vmem((block_rows, lanes), F32),
        vmem((2 * block_rows, lanes), BF16),
        vmem((n, block_rows, width), BF16),
        vmem((block_rows, width), BF16),
        vmem((block_rows, width), F32),
        vmem((block_rows, width), F32),
        vmem((NZ, own_rows, width), F32),
        vmem((own_rows, width), F32),
        vmem((n, gram_rows, width), F32),
        vmem((NX, gram_rows, width), F32),
        vmem((NX, gram_rows, width), F32),
        vmem((NX, gram_rows, width), F32),
        vmem((gram_rows, width), F32),
        vmem((NZ, gram_rows, width), F32),
        vmem((n, gram_rows, width), F32),
        dma((7, 2)),
        dma((6 * NX + 5 * NX - 3,)),
        dma((3,)),
        dma((3, 2)),
        dma((1,)),
        dma((2,)),
        dma((1,)),
        dma((1,)),
        dma((1,)),
        dma((1,)),
        dma((1,)),
        dma((NY,)),
        dma((1,)),
        dma((1,)),
        dma((1,)),
        dma((1,)),
        dma((1,)),
        dma((1,)),
        dma((3,)),
        pltpu.SemaphoreType.REGULAR,
        pltpu.SemaphoreType.REGULAR,
    ]
    whole = pl.BlockSpec(memory_space=pltpu.VMEM)
    update, grams = pl.pallas_call(
        functools.partial(kernel, layers, images, side, scale),
        out_shape=(
            jax.ShapeDtypeStruct((own_rows, width), F32),
            jax.ShapeDtypeStruct((2, width, width), F32),
        ),
        in_specs=[pl.BlockSpec(memory_space=pltpu.HBM)] * 4,
        out_specs=(whole, whole),
        scratch_shapes=scratch,
        compiler_params=pltpu.CompilerParams(
            collective_id=0, has_side_effects=True, vmem_limit_bytes=48 * 1024 * 1024
        ),
        name="kfac_step",
    )(
        *(
            pltpu.with_memory_space_constraint(value, pltpu.HBM)
            for value in (
                layer_inputs.reshape(rows, width),
                output_grads.reshape(rows, width),
                input_inverse.transpose(1, 0, 2),
                grad_inverse.reshape(width, width),
            )
        )
    )
    return update[None], grams[None]


def solution(mesh):
    assert mesh.shape["pos"] == NX * NZ * NC and mesh.shape["layer"] % NY == 0
    return jax.shard_map(
        functools.partial(per_device, mesh.shape["layer"]),
        mesh=mesh,
        in_specs=(
            P("layer", "pos", None, None, None),
            P("layer", "pos", None, None, None),
            P("layer", "pos", None),
            P("layer", None, None),
        ),
        out_specs=(P("layer", "pos", None), P("layer", None, None, None)),
        check_vma=False,
    )
```

```python
import functools

import jax
import jax.numpy as jnp
from jax import lax
from jax.experimental import pallas as pl
from jax.experimental.pallas import tpu as pltpu
from jax.sharding import PartitionSpec as P

NX, NY, NZ, NC = 4, 4, 8, 2
ROOT = 3
TAPS = 9
MESH = pl.DeviceIdType.MESH
F32 = jnp.float32
BF16 = jnp.bfloat16
HIGH = lax.Precision.HIGHEST


def offsets():
    return sorted(range(1, NX), key=lambda d: -min(d, NX - d))


def rcopy(src, dst, send_sem, recv_sem, to):
    return pltpu.make_async_remote_copy(
        src_ref=src,
        dst_ref=dst,
        send_sem=send_sem,
        recv_sem=recv_sem,
        device_id=to,
        device_id_type=MESH,
    )


def part_of(rows, q):
    size = -(-rows // (NY - 1) // 16) * 16
    start = (q - 1) * size
    return start, min(size, rows - start)


def dot(a, b, contract=(1, 0), precision=None):
    return lax.dot_general(
        a,
        b,
        (((contract[0],), (contract[1],)), ((), ())),
        precision=precision,
        preferred_element_type=F32,
    )


def unfold(src, dst, images, side, width):
    area = side * side
    rows = images * area
    value = src[...].astype(F32)
    col = lax.rem(lax.broadcasted_iota(jnp.int32, (rows, width), 0), side)
    before = jnp.where(col == 0, 0.0, pltpu.roll(value, 1, 0))
    after = jnp.where(col == side - 1, 0.0, pltpu.roll(value, rows - 1, 0))
    edge = jnp.zeros((side, width), BF16)
    for s, piece in enumerate((before, value, after)):
        piece = piece.astype(BF16)
        for image in range(images):
            top = image * area
            one = piece[top : top + area]
            lanes = pl.ds(s * width, width)
            dst[pl.ds(top, side), lanes] = edge
            dst[pl.ds(top + side, area - side), lanes] = one[: area - side]
            lanes = pl.ds((3 + s) * width, width)
            dst[pl.ds(top, area), lanes] = one
            lanes = pl.ds((6 + s) * width, width)
            dst[pl.ds(top, area - side), lanes] = one[side:]
            dst[pl.ds(top + area - side, side), lanes] = edge


def kernel(
    layers,
    images,
    side,
    scale,
    x_hbm,
    g_hbm,
    a_ref,
    ginv_hbm,
    upd_ref,
    gram_ref,
    xg_ref,
    ginv_ref,
    patches,
    patches_next,
    grad_t,
    xg_next,
    relay,
    part,
    part_one,
    in_one,
    out_x_one,
    in_x_one,
    out_two,
    in_two,
    out_x_two,
    in_x_two,
    plane_sum,
    z_out,
    z_in,
    z_out_wide,
    z_in_wide,
    full,
    full_wide,
    a_in,
    a_all,
    a_two,
    pre,
    rows_full,
    base,
    result,
    result_out,
    result_in,
    gram_part,
    gram_in,
    gram_out_x,
    gram_in_x,
    gram_z_out,
    gram_z_in,
    gram_full,
    ex_send,
    ex_recv,
    z_send,
    z_recv,
    a_send,
    a_recv,
    shift_send,
    shift_recv,
    relay_send,
    relay_recv,
    far_send,
    far_recv,
    pre_send,
    pre_recv,
    bc_send,
    bc_recv,
    up_send,
    up_recv,
    load_sem,
    ready_sem,
    go_sem,
):
    layer = lax.axis_index("layer")
    pos = lax.axis_index("pos")
    c = lax.rem(pos, NC)
    z = lax.rem(lax.div(pos, NC), NZ)
    x = lax.div(pos, NC * NZ)
    block = x * NC + c
    strip = c * NX + x
    n = NX * NC
    _, rows, width = xg_ref.shape
    y = lax.rem(layer, NY)
    lanes = TAPS * width
    per = NZ // NC
    own_rows = result_in.shape[0]
    front = TAPS // 3 * width
    spans = ((0, front, 0), (front, lanes - front, 1))
    narrow = (0, width, 0)
    is_root = z == ROOT
    is_rim = z != ROOT
    has_next = layer < layers - 1
    has_prev = layer > 0
    sends_far = has_prev & (y == 0)
    sends_near = has_prev & (y != 0)
    relays = (layer >= NY) & (y != 0)
    late = has_next & (y == NY - 1)

    def dev(lay, px, pz, pc):
        return (lay, (px * NZ + pz) * NC + pc)

    def ahead(dx):
        return lax.rem(x + dx, NX)

    def behind(dx):
        return lax.rem(x + NX - dx, NX)

    other = NC - 1 - c
    far_first = sorted(range(NZ), key=lambda pz: -abs(pz - ROOT))
    others = far_first[:-1]

    loads = [
        pltpu.make_async_copy(src, dst, load_sem.at[i])
        for i, (src, dst) in enumerate(((x_hbm, xg_ref.at[0]), (g_hbm, xg_ref.at[1]), (ginv_hbm, ginv_ref)))
    ]
    for load in loads:
        load.start()

    barrier = pltpu.get_barrier_semaphore()

    def greet(to):
        pl.semaphore_signal(barrier, inc=1, device_id=to, device_id_type=MESH)

    @pl.when(c != 0)
    def _():
        greet(dev(layer, x, z, 0))

    for dx in offsets():
        greet(dev(layer, ahead(dx), z, 0))

    @pl.when(is_rim)
    def _():
        greet(dev(layer, x, ROOT, 0))

    @pl.when(is_root)
    def _():
        for pz in others:
            greet(dev(layer, x, pz, 0))

    @pl.when(has_next)
    def _():
        greet(dev(layer + 1, x, z, 1))

    @pl.when(has_next & is_rim)
    def _():
        greet(dev(layer + 1, x, ROOT, 1))

    @pl.when(relays)
    def _():
        greet(dev(layer - y, x, z, 1))

    @pl.when(late)
    def _():
        for q in range(1, NY):
            greet(dev(layer + 1 + q, x, z, 1))

    for load in loads:
        load.wait()
    unfold(xg_ref.at[0], patches, images, side, width)
    grad_t[...] = xg_ref[1].T

    root = is_root.astype(jnp.int32)
    chips = 1 + root * (NZ - 2)
    near_greets = 1 + NC * (NX - 1 + chips)
    chips = 1 + root * (NZ - 1) + sends_far.astype(jnp.int32) * (NY - 1) + relays.astype(jnp.int32)
    far_greets = NC * chips

    @pl.when(c == 0)
    def _():
        pl.semaphore_wait(barrier, near_greets)
        pl.semaphore_signal(
            ready_sem, inc=1, device_id=dev(layer, x, z, other), device_id_type=MESH
        )

    @pl.when(c != 0)
    def _():
        pl.semaphore_wait(ready_sem, 1)

    shift = rcopy(xg_ref, xg_next, shift_send.at[0], shift_recv.at[0], dev(layer - 1, x, z, c))
    hops = range(1, NY)

    def piece(ref, q):
        start, size = part_of(rows, q)
        return ref.at[:, pl.ds(start, size)]

    def held(q):
        return relay.at[:, pl.ds(0, part_of(rows, q)[1])]

    to_relay = [
        rcopy(
            piece(xg_ref, q), held(q), relay_send.at[0], relay_recv.at[0], dev(layer + q, x, z, c)
        )
        for q in hops
    ]
    far_relay = [
        rcopy(
            held(q), piece(xg_next, q), far_send.at[0], far_recv.at[q - 1], dev(layer - q - 1, x, z, c)
        )
        for q in hops
    ]

    def arrived():
        @pl.when(has_next & jnp.logical_not(late))
        def _():
            shift.wait_recv()

        @pl.when(late)
        def _():
            for copy in far_relay:
                copy.wait_recv()

    half = lax.div(z, per)
    slot = lax.rem(z, per) * NC + c
    a_self = is_root & (half == c)
    a_other = jnp.logical_not(a_self)
    held_back = (z > ROOT) & (z <= ROOT + 2)
    group = lax.div(slot, NZ // 2)
    a_remote = rcopy(a_ref, a_in.at[slot], a_send.at[0], a_recv.at[group], dev(layer, x, ROOT, half))
    a_local = pltpu.make_async_copy(a_ref, a_in.at[slot], a_recv.at[group])

    @pl.when(a_other & jnp.logical_not(held_back))
    def _():
        a_remote.start()

    @pl.when(a_self)
    def _():
        a_local.start()

    sizes = (NX + 2, 2 * NX, NX + 1, NX, NX + 2, NX, 2 * NX)
    first_recv = [sum(sizes[:kind]) for kind in range(len(sizes))]

    def cols(view, span):
        return view.at[:, pl.ds(span[0], span[1])]

    def begin(copies):
        for copy in copies:
            copy.start()

    def core_copies(kind, out, in_core):
        return [
            rcopy(
                out.at[other * NX + ahead(dx)],
                in_core.at[dx],
                ex_send.at[kind, 0],
                ex_recv.at[first_recv[kind] + dx],
                dev(layer, x, z, other),
            )
            for dx in offsets() + [0]
        ]

    def x_copies(kind, out_x, in_x, span):
        return [
            rcopy(
                cols(out_x.at[dx], span),
                cols(in_x.at[dx], span),
                ex_send.at[kind, 1],
                ex_recv.at[first_recv[kind] + NX + span[2]],
                dev(layer, ahead(dx), z, c),
            )
            for dx in offsets()
        ]

    def pass_on(core, along, part, in_core, out_x, span):
        at = pl.ds(span[0], span[1])
        for dx, arrival, copy in zip(offsets(), core, along):
            if span[2] == 0:
                arrival.wait_recv()
            mine = part[c * NX + ahead(dx), :, at]
            out_x[dx, :, at] = (mine + in_core[dx, :, at].astype(F32)).astype(out_x.dtype)
            copy.start()

    def plane_total(kind, core, part, in_core, in_x, span):
        at = pl.ds(span[0], span[1])
        if span[2] == 0:
            core[-1].wait_recv()
        total = part[strip, :, at] + in_core[0, :, at].astype(F32)
        got = in_x.at[pl.ds(1, NX - 1), :, at]
        rcopy(
            got, got, ex_send.at[kind, 1], ex_recv.at[first_recv[kind] + NX + span[2]], dev(layer, x, z, other)
        ).wait_recv()
        for dx in range(1, NX):
            total = total + in_x[dx, :, at].astype(F32)
        return total

    def all_sent(sem, view):
        rcopy(view, view, sem, ex_recv.at[0], dev(layer, x, z, other)).wait_send()

    def plane_sent(kind, in_core, in_x):
        all_sent(ex_send.at[kind, 0], in_core)
        all_sent(ex_send.at[kind, 1], in_x.at[pl.ds(1, NX - 1)])

    def gather_sent(kind, buf):
        all_sent(ex_send.at[kind, 0], buf.at[pl.ds(0, NX)])
        all_sent(ex_send.at[kind, 1], buf.at[pl.ds(0, NX - 1)])

    def crossing(kind, out, s, got, to):
        return rcopy(got, got, ex_send.at[kind, out], ex_recv.at[first_recv[kind] + s], to)

    def gather(kind, buf, own, span):
        targets = [(dx, dev(layer, ahead(dx), z, c)) for dx in offsets()]
        got = cols(buf.at[own], span)
        return [
            crossing(kind, 0, NX * span[2] + dx, got, to)
            for dx, to in targets + [(0, dev(layer, x, z, other))]
        ]

    def gathered(kind, buf, place, span):
        partner = dev(layer, x, z, other)
        for dx in reversed(offsets()):
            got = cols(buf.at[place(behind(dx), c)], span)
            crossing(kind, 0, NX * span[2] + dx, got, partner).wait_recv()
            crossing(kind, 1, NX * span[2], got, partner).start()
        got = buf.at[pl.ds(0, NX), :, pl.ds(span[0], span[1])]
        crossing(kind, 0, NX * span[2], got, partner).wait_recv()

    def by_strip(px, pc):
        return pc * NX + px

    def by_block(px, pc):
        return px * NC + pc

    def z_copy(kind, src, dst, span):
        return rcopy(
            cols(src, span),
            cols(dst.at[z], span),
            z_send.at[kind],
            z_recv.at[kind, span[2]],
            dev(layer, x, ROOT, c),
        )

    def z_arrived(kind, dst, span):
        got = dst.at[pl.ds(0, NZ - 1), :, pl.ds(span[0], span[1])]
        rcopy(got, got, z_send.at[kind], z_recv.at[kind, span[2]], dev(layer, x, z, other)).wait_recv()

    z_bufs = ((z_out_wide, z_in_wide), (z_out, z_in))

    def z_start(z_slot, total, span):
        at = pl.ds(span[0], span[1])
        plane_sum[:, at] = total
        src, dst = z_bufs[z_slot]

        @pl.when(is_rim)
        def _():
            src[:, at] = total.astype(src.dtype)
            z_copy(z_slot, src, dst, span).start()

    def root_total(z_slot, buf, span):
        at = pl.ds(span[0], span[1])
        total = plane_sum[:, at]
        _, dst = z_bufs[z_slot]
        z_arrived(z_slot, dst, span)
        for pz in others:
            total = total + dst[pz, :, at].astype(F32)
        buf[strip, :, at] = total * scale

    def fold(both):
        half_rows = both.shape[0] // 2
        return both[:half_rows] + both[half_rows:]

    def times_inverse(buf):
        value = buf[...].reshape(width, lanes)
        top = value.astype(BF16)
        low = (value - top.astype(F32)).astype(BF16)
        both = dot(a_two[...], jnp.concatenate([top, low], axis=0), (1, 1))
        return fold(both[:, :width] + both[:, width:])

    part_one[...] = dot(grad_t[...], patches[...]).reshape(part_one.shape)
    first = core_copies(0, part_one, in_one)
    first_x = [x_copies(0, out_x_one, in_x_one, span) for span in spans]
    begin(first)
    for span, along in zip(spans, first_x):
        pass_on(first, along, part_one, in_one, out_x_one, span)

    @pl.when(has_prev & (c != 0))
    def _():
        pl.semaphore_wait(barrier, far_greets)
        pl.semaphore_signal(
            ready_sem, inc=1, device_id=dev(layer, x, z, other), device_id_type=MESH
        )

    @pl.when(has_prev & (c == 0))
    def _():
        pl.semaphore_wait(ready_sem, 1)

    @pl.when(sends_near)
    def _():
        shift.start()

    @pl.when(sends_far)
    def _():
        for copy in to_relay:
            copy.start()

    for span in spans:
        z_start(0, plane_total(0, first, part_one, in_one, in_x_one, span), span)

    for q in hops:

        @pl.when(relays & (y == q))
        def _(q=q):
            to_relay[q - 1].wait_recv()
            far_relay[q - 1].start()


    @pl.when(jnp.logical_not(has_next))
    def _():
        xg_next[...] = jnp.zeros_like(xg_next)
        pre[...] = jnp.zeros_like(pre)

    half_blocks = gram_part.shape[0] // 2
    gram_core = core_copies(2, gram_part, gram_in)
    gram_x = x_copies(2, gram_out_x, gram_in_x, narrow)
    gram_gather = gather(5, gram_full, strip, narrow)
    bc_copies = [
        rcopy(
            gram_full.at[strip],
            gram_full.at[strip],
            bc_send.at[0],
            bc_recv.at[0],
            dev(layer, x, pz, c),
        )
        for pz in others
    ]

    def gram_begin():
        arrived()
        shape = (half_blocks, gram_part.shape[1], width)
        gram_part[pl.ds(0, half_blocks)] = dot(grad_t[...], xg_ref[1]).reshape(shape)
        gram_part[pl.ds(half_blocks, half_blocks)] = dot(grad_t[...], xg_next[1]).reshape(shape)
        begin(gram_core)

    def gram_pass():
        pass_on(gram_core, gram_x, gram_part, gram_in, gram_out_x, narrow)

    def gram_end():
        gram_z_out[...] = plane_total(2, gram_core, gram_part, gram_in, gram_in_x, narrow)

    def gram_root():
        total = gram_z_out[...]
        z_arrived(2, gram_z_in, narrow)
        for pz in others:
            total = total + gram_z_in[pz]
        gram_full[strip] = total * scale
        begin(bc_copies)

    def gram_send():
        z_copy(2, gram_z_out, gram_z_in, narrow).start()

    early = jnp.logical_not(late)

    @pl.when(early)
    def _():
        gram_begin()
        gram_pass()

    @pl.when(early & is_rim)
    def _():
        gram_end()

    @pl.when(held_back)
    def _():
        pl.semaphore_wait(go_sem, 1)
        a_remote.start()

    pre_copies = [
        rcopy(
            rows_full,
            pre.at[block],
            pre_send.at[0],
            pre_recv.at[0],
            dev(layer - 1, x, pz, c),
        )
        for pz in far_first
    ]

    def assemble(g):
        taken = a_in.at[pl.ds(g * (NZ // 2), NZ // 2)]
        pltpu.make_async_copy(taken, taken, a_recv.at[g]).wait()
        for q in range(g * (NZ // 2), (g + 1) * (NZ // 2)):
            a_all[pl.ds(q * own_rows, own_rows), :] = a_in[q, :, 0, :]

    @pl.when(is_root)
    def _():
        root_total(0, full_wide, spans[0])
        begin(gather(1, full_wide, strip, spans[0]))
        for d in range(2):
            pl.semaphore_signal(
                go_sem, inc=1, device_id=dev(layer, x, ROOT + 1 + d, c), device_id_type=MESH
            )
        root_total(0, full_wide, spans[1])
        begin(gather(1, full_wide, strip, spans[1]))

        assemble(1)
        for span in spans:
            gathered(1, full_wide, by_strip, span)
        assemble(0)
        rows = a_all[...]
        top = rows.astype(BF16)
        a_two[pl.ds(0, rows.shape[0]), :] = top
        a_two[pl.ds(rows.shape[0], rows.shape[0]), :] = (rows - top.astype(F32)).astype(BF16)
        value = dot(times_inverse(full_wide), ginv_ref[...], precision=HIGH)
        base[...] = value
        rows_full[...] = value.astype(BF16)

        @pl.when(sends_near)
        def _():
            for copy in pre_copies:
                copy.start()

        @pl.when(sends_far)
        def _():
            for copy in reversed(pre_copies):
                copy.start()

        @pl.when(early)
        def _():
            gram_end()


    @pl.when(late)
    def _():
        gram_begin()

    unfold(xg_next.at[0], patches_next, images, side, width)

    @pl.when(has_next)
    def _():
        rcopy(
            rows_full, pre.at[block], pre_send.at[0], pre_recv.at[0], dev(layer, x, z, other)
        ).wait_recv()
        begin(gather(3, pre, block, narrow))
        gathered(3, pre, by_block, narrow)

    @pl.when(early & is_rim)
    def _():
        gram_send()

    mapped = dot(patches_next[...], pre[...].reshape(lanes, width)).astype(BF16)
    product = dot(mapped.T, patches[...])
    part[...] = product.reshape(part.shape)
    out_two[...] = product.astype(BF16).reshape(out_two.shape)
    second = core_copies(4, out_two, in_two)
    second_x = [x_copies(4, out_x_two, in_x_two, span) for span in spans]
    begin(second)

    @pl.when(late)
    def _():
        gram_pass()

    for span, along in zip(spans, second_x):
        pass_on(second, along, part, in_two, out_x_two, span)
    for span in spans:
        z_start(1, plane_total(4, second, part, in_two, in_x_two, span), span)
    def gram_back():
        @pl.when(is_root)
        def _():
            gram_root()

        @pl.when(is_rim)
        def _():
            bc_copies[0].wait_recv()

        begin(gram_gather)

    @pl.when(late)
    def _():
        gram_end()

    @pl.when(late & is_rim)
    def _():
        gram_send()

    @pl.when(early)
    def _():
        gram_back()
        gathered(5, gram_full, by_strip, narrow)

    @pl.when(late & is_rim)
    def _():
        gram_back()
        gathered(5, gram_full, by_strip, narrow)

    @pl.when(is_rim | early)
    def _():
        gram_ref[...] = gram_full[...].reshape(gram_ref.shape)

    plane_sent(0, in_one, in_x_one)
    plane_sent(2, gram_in, gram_in_x)
    plane_sent(4, in_two, in_x_two)

    @pl.when(a_other)
    def _():
        a_remote.wait_send()

    @pl.when(sends_near)
    def _():
        shift.wait_send()

    @pl.when(sends_far)
    def _():
        all_sent(relay_send.at[0], xg_next)

    for q in hops:

        @pl.when(relays & (y == q))
        def _(q=q):
            far_relay[q - 1].wait_send()

    @pl.when(has_next)
    def _():
        gather_sent(3, pre)

    @pl.when(is_root & has_prev)
    def _():
        all_sent(pre_send.at[0], pre)

    @pl.when(is_root)
    def _():
        gather_sent(1, full_wide)

    @pl.when(is_rim)
    def _():
        all_sent(z_send.at[0], z_out_wide)
        all_sent(z_send.at[1], z_out)
        all_sent(z_send.at[2], gram_z_out)
        gather_sent(5, gram_full)

    up_copies = [
        rcopy(
            result_out.at[q],
            result_in,
            up_send.at[0],
            up_recv.at[0],
            dev(layer, x, c * per + q // NC, q % NC),
        )
        for q in range(NZ)
    ]
    own_q = (ROOT - c * per) * NC + c

    @pl.when(is_root)
    def _():
        for span in spans:
            root_total(1, full, span)
            begin(gather(6, full, strip, span))

        @pl.when(late)
        def _():
            gram_back()

        for span in spans:
            gathered(6, full, by_strip, span)

        @pl.when(late)
        def _():
            gathered(5, gram_full, by_strip, narrow)


        @pl.when(late)
        def _():
            gram_ref[...] = gram_full[...].reshape(gram_ref.shape)

        cross_gram = gram_full[pl.ds(half_blocks, half_blocks)].reshape(width, width)
        mix = dot(cross_gram, ginv_ref[...], (0, 0), HIGH)
        value = base[...] - dot(times_inverse(full), mix, precision=HIGH)
        result[...] = value
        for q in sorted(range(NZ), key=lambda q: -abs(q // NC - ROOT % per)):
            result_out[q] = result[pl.ds(q * own_rows, own_rows), :]

            @pl.when(own_q != q)
            def _(copy=up_copies[q]):
                copy.start()

        @pl.when(a_self)
        def _():
            upd_ref[...] = result_out[ROOT % per * NC + ROOT // per]

    @pl.when(a_other)
    def _():
        rcopy(
            result_out.at[0], result_in, up_send.at[0], up_recv.at[0], dev(layer, x, z, other)
        ).wait_recv()
        upd_ref[...] = result_in[...]

    @pl.when(is_root)
    def _():
        all_sent(bc_send.at[0], gram_full.at[pl.ds(0, NZ - 1)])
        gather_sent(5, gram_full)
        gather_sent(6, full)

    @pl.when(a_self)
    def _():
        all_sent(up_send.at[0], result_out.at[pl.ds(0, NZ - 1)])

    @pl.when(is_root & a_other)
    def _():
        all_sent(up_send.at[0], result_out)


def per_device(layers, layer_inputs, output_grads, input_inverse, grad_inverse):
    _, images, side, _, width = layer_inputs.shape
    rows = images * side * side
    own_rows = input_inverse.shape[1]
    lanes = TAPS * width
    n = NX * NC
    strip = width // n
    block_rows = lanes // n
    gram_rows = 2 * width // n
    scale = 1.0 / (rows * n * NZ)
    vmem = pltpu.VMEM
    dma = pltpu.SemaphoreType.DMA
    scratch = [
        vmem((2, rows, width), BF16),
        vmem((width, width), F32),
        vmem((rows, lanes), BF16),
        vmem((rows, lanes), BF16),
        vmem((width, rows), BF16),
        vmem((2, rows, width), BF16),
        vmem((2, part_of(rows, 1)[1], width), BF16),
        vmem((n, strip, lanes), F32),
        vmem((n, strip, lanes), F32),
        vmem((NX, strip, lanes), F32),
        vmem((NX, strip, lanes), F32),
        vmem((NX, strip, lanes), F32),
        vmem((n, strip, lanes), BF16),
        vmem((NX, strip, lanes), BF16),
        vmem((NX, strip, lanes), BF16),
        vmem((NX, strip, lanes), BF16),
        vmem((strip, lanes), F32),
        vmem((strip, lanes), BF16),
        vmem((NZ, strip, lanes), BF16),
        vmem((strip, lanes), F32),
        vmem((NZ, strip, lanes), F32),
        vmem((n, strip, lanes), F32),
        vmem((n, strip, lanes), F32),
        vmem((NZ, own_rows, 1, lanes), F32),
        vmem((block_rows, lanes), F32),
        vmem((2 * block_rows, lanes), BF16),
        vmem((n, block_rows, width), BF16),
        vmem((block_rows, width), BF16),
        vmem((block_rows, width), F32),
        vmem((block_rows, width), F32),
        vmem((NZ, own_rows, width), F32),
        vmem((own_rows, width), F32),
        vmem((n, gram_rows, width), F32),
        vmem((NX, gram_rows, width), F32),
        vmem((NX, gram_rows, width), F32),
        vmem((NX, gram_rows, width), F32),
        vmem((gram_rows, width), F32),
        vmem((NZ, gram_rows, width), F32),
        vmem((n, gram_rows, width), F32),
        dma((7, 2)),
        dma((6 * NX + 5 * NX - 3,)),
        dma((3,)),
        dma((3, 2)),
        dma((1,)),
        dma((2,)),
        dma((1,)),
        dma((1,)),
        dma((1,)),
        dma((1,)),
        dma((1,)),
        dma((NY - 1,)),
        dma((1,)),
        dma((1,)),
        dma((1,)),
        dma((1,)),
        dma((1,)),
        dma((1,)),
        dma((3,)),
        pltpu.SemaphoreType.REGULAR,
        pltpu.SemaphoreType.REGULAR,
    ]
    whole = pl.BlockSpec(memory_space=pltpu.VMEM)
    update, grams = pl.pallas_call(
        functools.partial(kernel, layers, images, side, scale),
        out_shape=(
            jax.ShapeDtypeStruct((own_rows, width), F32),
            jax.ShapeDtypeStruct((2, width, width), F32),
        ),
        in_specs=[pl.BlockSpec(memory_space=pltpu.HBM)] * 4,
        out_specs=(whole, whole),
        scratch_shapes=scratch,
        compiler_params=pltpu.CompilerParams(
            collective_id=0, has_side_effects=True, vmem_limit_bytes=48 * 1024 * 1024
        ),
        name="kfac_step",
    )(
        *(
            pltpu.with_memory_space_constraint(value, pltpu.HBM)
            for value in (
                layer_inputs.reshape(rows, width),
                output_grads.reshape(rows, width),
                input_inverse.transpose(1, 0, 2),
                grad_inverse.reshape(width, width),
            )
        )
    )
    return update[None], grams[None]


def solution(mesh):
    assert mesh.shape["pos"] == NX * NZ * NC and mesh.shape["layer"] % NY == 0
    return jax.shard_map(
        functools.partial(per_device, mesh.shape["layer"]),
        mesh=mesh,
        in_specs=(
            P("layer", "pos", None, None, None),
            P("layer", "pos", None, None, None),
            P("layer", "pos", None),
            P("layer", None, None),
        ),
        out_specs=(P("layer", "pos", None), P("layer", None, None, None)),
        check_vma=False,
    )
```
